32 devices in a mesh: group: 2 (over y), seq: 4 (over z), mp: 4 (over x, core).
Axes of the slice: x: 2, y: 2, z: 4, core: 2. Of those that a mesh axis runs over, the one named last changes fastest.
Arguments:
- embeds: bfloat16 [8192, 8192], P('seq', 'mp'), may hold values from -250 to 250
- image_feats: bfloat16 [512, 7296], P('seq'), may hold values from -6 to 6
- image_pos: int32 [512], P('seq'), may hold values from 0 to 8191, as said below
- proj_w: bfloat16 [7296, 8192], P('seq', 'mp'), may hold values from -0.0625 to 0.0625
- proj_b: bfloat16 [8192], P('mp'), may hold values from -3 to 3
- norm_gain: bfloat16 [8192], P('mp'), may hold values from 0.099609375 to 1.8984375
- kv_w: bfloat16 [8192, 2048], P('mp'), may hold values from -0.0625 to 0.0625
- prompt_lengths: int32 [2], replicated, may hold values from 2048 to 4096
- page_owner: int32 [512, 1], P('seq'), may hold values from 0 to 3; in each aligned block of 128 rows (0 to 127, 128 to 255, ...) at most 64 rows name the same one
- queries: bfloat16 [512, 8192], P('seq', 'mp'), may hold values from -180 to 180
- kv_cache: bfloat16 [512, 128, 2048], P('seq', None, 'mp'), may hold values from -5 to 5
- new_kv: bfloat16 [512, 2048], P('seq', 'mp'), may hold values from -5 to 5
- cache_lengths: int32 [512], P('seq'), may hold values from 2 to 128
Outputs:
- page_slots: bfloat16 [2048, 16, 2048], P(('group', 'seq'), None, 'mp')
- row_states: bfloat16 [1024, 8192], P(('group', 'seq'), 'mp')
The draws below stay inside these ranges and needn't reach their ends.
Inputs may be any that keep to these rules, and one draw needn't show every extreme that they name: `image_pos`: distinct and increasing; entries s * 128 to (s + 1) * 128 - 1 lie among tokens s * 2048 to (s + 1) * 2048 - 1. `page_owner`: among the 128 pages of one seq index no owner is named more than 64 times.
All inputs are finite; a program needn't handle non-finite values.
Results may differ from the reference program's by a relative error of at most 0.005.
Values may be sent and summed in bfloat16 or wider, within the bound.
A program may use at most 128 MiB of HBM per device.

```python
import math
import jax
import jax.numpy as jnp
import numpy as np
from jax import lax

D = 8192
QH = 64
KVH = 8
HEAD = 128
C_VIS = 7296
PAGE = 16
PROMPT_LEN = 4096
ROWS_DEV = 2048
BATCH_DEV = 128
CACHE = 128
TOKENS = 8192
IMGS = 512
PROMPTS = 2
PAGES_DEV = 128
PAGES = 512
CAP = 64
N_SEQ = 4


def decode_pair(key):
    cache_key = jax.random.fold_in(key, 11)
    query_key = jax.random.fold_in(key, 12)
    stored = jnp.clip(jax.random.normal(cache_key, (IMGS, CACHE, KVH, 2, HEAD), jnp.float32), -5.0, 5.0)
    asked = jnp.clip(jax.random.normal(query_key, (IMGS, KVH, QH // KVH, HEAD), jnp.float32), -5.0, 5.0)
    return (stored.reshape(IMGS, CACHE, KVH * 2 * HEAD), asked.reshape(IMGS, QH * HEAD))


def draw_kv_cache(key, part):
    return decode_pair(key)[0].astype(jnp.bfloat16)


def draw_queries(key, part):
    return decode_pair(key)[1].astype(jnp.bfloat16)


def draw_embeds(key, part):
    row_u = jax.random.uniform(jax.random.fold_in(key, 22), (TOKENS, 1), jnp.float32)
    col_u = jax.random.uniform(jax.random.fold_in(key, 23), (1, D), jnp.float32)
    trend = jnp.arange(D, dtype=jnp.float32)[None, :] / D
    base = jnp.clip(jax.random.normal(jax.random.fold_in(key, 21), (TOKENS, D), jnp.float32), -6.0, 6.0)
    col_scale = 10.0 ** (0.5 * trend + 0.5 * col_u)
    row_scale = 10.0 ** (row_u - 0.5)
    return (base * row_scale * col_scale).astype(jnp.bfloat16)


def draw_image_pos(key, part):

    def one_shard(shard):
        order = jax.random.permutation(jax.random.fold_in(key, 31 + shard), ROWS_DEV)
        picked = jnp.sort(order[:BATCH_DEV])
        return picked.astype(jnp.int32) + shard * ROWS_DEV
    shards = jnp.arange(IMGS // BATCH_DEV, dtype=jnp.int32)
    return jax.vmap(one_shard)(shards).reshape(IMGS).astype(jnp.int32)


def set_ends(array, key, least, largest):
    spot = [jax.random.randint(jax.random.fold_in(key, axis), (), 0, length) for axis, length in enumerate(array.shape)]
    widest = array.shape.index(max(array.shape))
    neighbour = spot[:widest] + [(spot[widest] + 1) % array.shape[widest]] + spot[widest + 1:]
    return array.at[tuple(spot)].set(least).at[tuple(neighbour)].set(largest)


def level_of(stream_key, dims, split, low, largest):
    loudness = 1.0
    for dim, blocks in split:
        draws = jax.random.uniform(jax.random.fold_in(jax.random.fold_in(stream_key, 6), dim), (blocks,), jnp.float32, low / len(split), largest / len(split))
        loudness = loudness * jnp.repeat(jnp.exp(draws), dims[dim] // blocks).reshape((-1,) + (1,) * (len(dims) - 1 - dim))
    return loudness


def assign_block(own_key, own, number, rows, number_of, top, bound, skew):
    sequence = jax.random.permutation(own_key, number_of)
    crowded, usual = load_shares(number_of, rows * top, bound, skew, True), load_shares(number_of, rows * top, bound, skew, False)
    places = jnp.arange(number_of)

    def named(tallies, rotation):
        used = int((tallies > 0).sum())
        fixed = max(1, used // 4)
        shifted = fixed + (places - fixed + rotation * (used - fixed)) % max(1, number_of - fixed)
        return jnp.zeros((number_of,), jnp.int32).at[sequence[jnp.where(places < fixed, places, shifted)]].set(jnp.asarray(tallies, jnp.int32))

    tallies = jnp.where(number % 4 == 0, named(crowded, number // 4), named(usual, number - number // 4 - 1))
    mixed = jax.random.permutation(jax.random.fold_in(own, 3), number_of)
    giver, sink = mixed[0:number_of // 2 * 2:2], mixed[1:number_of // 2 * 2:2]
    slack = jnp.minimum(tallies[giver] - 1, bound - tallies[sink]) // 2
    slack = jnp.where((giver == sequence[0]) | (sink == sequence[0]) | (tallies[sink] == 0), 0, jnp.maximum(slack, 0))
    shifted = jax.random.randint(jax.random.fold_in(own, 4), (number_of // 2,), 0, 1 << 20) % (slack + 1)
    tallies = tallies.at[giver].add(-shifted).at[sink].add(shifted)
    labels = jnp.searchsorted(jnp.cumsum(tallies), jnp.arange(rows * top), side="right").astype(jnp.int32)
    table = labels.reshape(top, rows).T
    table = table[jax.random.permutation(jax.random.fold_in(own, 1), rows)]
    rotation = jax.random.randint(jax.random.fold_in(own, 2), (rows, 1), 0, top)
    return jnp.take_along_axis(table, (jnp.arange(top)[None, :] + rotation) % top, axis=1)


def load_shares(count, total, bound, skew, full):
    loads = [(1 << 20) // math.isqrt(rank ** skew) + 1 for rank in range(1, count + 1)]
    largest = bound if full else min(bound, max(-(-total // count), total * loads[0] // sum(loads)))
    least = 1 if total - largest >= count - 1 else 0
    counts, rest = [largest] + [least] * (count - 1), total - largest - least * (count - 1)
    while rest > 0:
        candidates = [i for i in range(1, count) if counts[i] < largest] or [i for i in range(1, count) if counts[i] < bound]
        whole, remaining = sum([loads[i] for i in candidates]), rest
        for i in candidates:
            extra = min(bound - counts[i], max(1, remaining * loads[i] // whole), rest)
            counts[i] = counts[i] + extra
            rest = rest - extra
    return np.array(counts)


def scatter_about(rng, extent, scale, bound, pieces=(), kind=jnp.bfloat16):
    values = scale * jax.random.normal(rng, extent, jnp.float32)
    if pieces:
        values = values * level_of(rng, extent, pieces, -0.22, 0.18)
    return jnp.clip(values, -bound, bound).astype(kind)


def setup_inputs(seed: int = 0) -> dict:
    splits = jax.random.split(jax.random.key(seed), 14)
    embeds = draw_embeds(jax.random.fold_in(splits[13], 71), 0)
    image_feats = scatter_about(splits[1], (IMGS, C_VIS), 1.0, 6.0, ((0, 4),))
    image_pos = draw_image_pos(jax.random.fold_in(splits[13], 71), 0)
    proj_w = scatter_about(splits[3], (C_VIS, D), C_VIS ** -0.5, 0.0625, ((0, 4), (1, 4)))
    proj_b = scatter_about(splits[4], (D,), 0.5, 3.0, ((0, 4),))
    norm_gain = jnp.clip(1.0 + 0.18 * jax.random.normal(splits[5], (D,), jnp.float32), 0.099609375, 1.8984375).astype(jnp.bfloat16)
    kv_w = scatter_about(splits[6], (D, KVH * 2 * HEAD), D ** -0.5, 0.0625, ((0, 4),))
    prompt_lengths = jax.random.randint(splits[7], (PROMPTS,), PROMPT_LEN // 2, PROMPT_LEN + 1).astype(jnp.int32)
    page_owner_keys = jax.random.split(jax.random.fold_in(splits[8], 1), PAGES // PAGES_DEV)
    page_owner_turns = jax.random.permutation(jax.random.fold_in(splits[8], 3), PAGES // PAGES_DEV)
    page_owner = jax.vmap(lambda own, number: assign_block(jax.random.fold_in(splits[8], 2), own, number, PAGES_DEV, N_SEQ, 1, CAP, 2))(page_owner_keys, page_owner_turns).reshape((PAGES, 1))
    queries = draw_queries(jax.random.fold_in(splits[13], 71), 0)
    kv_cache = draw_kv_cache(jax.random.fold_in(splits[13], 71), 0)
    new_kv = scatter_about(splits[11], (IMGS, KVH * 2 * HEAD), 1.0, 5.0, ((0, 4), (1, 4)))
    cache_lengths = set_ends(jax.random.randint(splits[12], (IMGS,), 2, CACHE + 1), jax.random.fold_in(splits[12], 1), 2, CACHE).astype(jnp.int32)
    return dict(embeds=embeds, image_feats=image_feats, image_pos=image_pos, proj_w=proj_w, proj_b=proj_b, norm_gain=norm_gain, kv_w=kv_w, prompt_lengths=prompt_lengths, page_owner=page_owner, queries=queries, kv_cache=kv_cache, new_kv=new_kv, cache_lengths=cache_lengths)


def reference(embeds, image_feats, image_pos, proj_w, proj_b, norm_gain, kv_w, prompt_lengths, page_owner, queries, kv_cache, new_kv, cache_lengths):
    projected = jnp.dot(image_feats, proj_w, preferred_element_type=jnp.float32) + proj_b.astype(jnp.float32)
    image_hidden = jax.nn.gelu(projected, approximate=False).astype(jnp.bfloat16)
    hidden = embeds.at[image_pos].set(image_hidden)
    hidden_f32 = hidden.astype(jnp.float32)
    squares = lax.optimization_barrier(jnp.sum(hidden_f32 * hidden_f32, axis=1))
    row_scale = lax.rsqrt(squares / D + 1e-05)
    scaled = (hidden_f32 * norm_gain.astype(jnp.float32)).astype(jnp.bfloat16)
    kv_full = jnp.dot(scaled, kv_w, preferred_element_type=jnp.float32) * row_scale[:, None]
    positions = jnp.arange(TOKENS, dtype=jnp.int32)
    prompt_limit = prompt_lengths[positions // PROMPT_LEN]
    is_live = positions % PROMPT_LEN < prompt_limit
    kv_rows = jnp.where(is_live[:, None], kv_full, 0.0).astype(jnp.bfloat16)
    kv_pages = kv_rows.reshape(N_SEQ, PAGES_DEV, PAGE, KVH * 2 * HEAD)
    owners = page_owner[:, 0].reshape(N_SEQ, PAGES_DEV)
    one_hot = (owners[:, :, None] == jnp.arange(N_SEQ, dtype=jnp.int32)[None, None, :]).astype(jnp.int32)
    page_rank = lax.optimization_barrier(jnp.sum((jnp.cumsum(one_hot, axis=1) - one_hot) * one_hot, axis=2))
    slot_index = owners * CAP + page_rank
    selector = (slot_index[:, None, :] == jnp.arange(N_SEQ * CAP, dtype=jnp.int32)[None, :, None]).astype(jnp.float32)
    by_owner = jnp.einsum('sdp,spte->sdte', selector, kv_pages.astype(jnp.float32), precision=lax.Precision.HIGHEST).astype(jnp.bfloat16)
    sent_view = by_owner.reshape(N_SEQ * N_SEQ * CAP, PAGE, KVH * 2 * HEAD)
    received_view = by_owner.reshape(N_SEQ, N_SEQ, CAP, PAGE, KVH * 2 * HEAD).transpose(1, 0, 2, 3, 4).reshape(N_SEQ * N_SEQ * CAP, PAGE, KVH * 2 * HEAD)
    page_slots = jnp.concatenate([sent_view, received_view], axis=0)
    row_count = queries.shape[0]
    grouped = queries.astype(jnp.float32).reshape(row_count, KVH, QH // KVH, HEAD)
    cache_f32 = kv_cache.astype(jnp.float32).reshape(row_count, CACHE, KVH, 2 * HEAD)
    fresh_kv = new_kv.astype(jnp.float32).reshape(row_count, KVH, 2 * HEAD)
    scores = jnp.einsum('rgqh,rjgh->rgqj', grouped, cache_f32[..., :HEAD], precision=lax.Precision.HIGHEST) * HEAD ** (-0.5)
    in_cache = jnp.arange(CACHE, dtype=jnp.int32)[None, :] < cache_lengths[:, None]
    scores = jnp.where(in_cache[:, None, None, :], scores, -1e+30)
    own_score = jnp.einsum('rgqh,rgh->rgq', grouped, fresh_kv[..., :HEAD], precision=lax.Precision.HIGHEST) * HEAD ** (-0.5)
    row_max = jnp.maximum(lax.optimization_barrier(jnp.max(scores, axis=3)), own_score)
    weights = jnp.exp(scores - row_max[..., None])
    own_weight = jnp.exp(own_score - row_max)
    denominator = lax.optimization_barrier(jnp.sum(weights, axis=3)) + own_weight
    probability = lax.optimization_barrier((weights / denominator[..., None]).astype(jnp.bfloat16)).astype(jnp.float32)
    own_prob = lax.optimization_barrier((own_weight / denominator).astype(jnp.bfloat16)).astype(jnp.float32)
    attended = jnp.einsum('rgqj,rjgh->rgqh', probability, cache_f32[..., HEAD:], precision=lax.Precision.HIGHEST)
    attended = attended + own_prob[..., None] * fresh_kv[:, :, None, HEAD:]
    attended = attended.astype(jnp.bfloat16).reshape(row_count, QH * HEAD)
    row_states = jnp.concatenate([image_hidden, attended], axis=0)
    return (page_slots, row_states)
```

```python
import functools

import jax
import jax.numpy as jnp
from jax import lax
from jax.experimental import pallas as pl
from jax.experimental.pallas import tpu as pltpu
from jax.sharding import PartitionSpec as P

HEAD = 128
LANES = 128
TILE = 512
CORES = 2
MESH = pl.DeviceIdType.MESH
F32 = jnp.float32
BF16 = jnp.bfloat16


def gated(condition, action, empty_value, *operands):
    return lax.cond(condition, action, lambda *unused: empty_value, *operands)


def attend_head(queries, keys, values, fresh_key, fresh_value, in_cache):
    scores = jnp.einsum(
        "rqh,rjh->rqj", queries, keys, preferred_element_type=jnp.float32
    ) * HEAD ** (-0.5)
    scores = jnp.where(in_cache[:, None, :], scores, -1e30)
    own_score = jnp.einsum(
        "rqh,rh->rq", queries, fresh_key, preferred_element_type=jnp.float32
    ) * HEAD ** (-0.5)
    row_max = jnp.maximum(jnp.max(scores, axis=2), own_score)
    weights = jnp.exp(scores - row_max[..., None])
    own_weight = jnp.exp(own_score - row_max)
    denominator = jnp.sum(weights, axis=2) + own_weight
    probability = (weights / denominator[..., None]).astype(jnp.bfloat16)
    own_prob = lax.optimization_barrier((own_weight / denominator).astype(jnp.bfloat16)).astype(
        jnp.float32
    )
    attended = jnp.einsum("rqj,rjh->rqh", probability, values, preferred_element_type=jnp.float32)
    attended = attended + own_prob[..., None] * fresh_value[:, None, :].astype(jnp.float32)
    return attended.astype(jnp.bfloat16)


def attend(queries, kv_cache, new_kv, cache_lengths):
    row_count = queries.shape[0]
    heads_kv = kv_cache.shape[2] // (2 * HEAD)
    share = queries.shape[1] // heads_kv
    in_cache = jnp.arange(kv_cache.shape[1], dtype=jnp.int32)[None, :] < cache_lengths[:, None]
    heads = []
    for head in range(heads_kv):
        key, value, end = 2 * HEAD * head, 2 * HEAD * head + HEAD, 2 * HEAD * (head + 1)
        attended = attend_head(
            queries[:, head * share : (head + 1) * share].reshape(row_count, share // HEAD, HEAD),
            kv_cache[:, :, key:value],
            kv_cache[:, :, value:end],
            new_kv[:, key:value],
            new_kv[:, value:end],
            in_cache,
        )
        heads.append(attended.reshape(row_count, share))
    return jnp.concatenate(heads, axis=1)


def live_rows(positions, prompt_lengths, prompt_len):
    prompt_ids = positions // prompt_len
    match = prompt_ids[..., None] == jnp.arange(prompt_lengths.shape[0], dtype=jnp.int32)
    limit = jnp.sum(jnp.where(match, prompt_lengths, 0), axis=-1)
    return positions % prompt_len < limit


def ds(index, size):
    return pl.ds(pl.multiple_of(index * size, size), size)


def spread_rows(row):
    return jnp.transpose(jnp.broadcast_to(row, (LANES, LANES)))


def prefill_kernel(
    groups,
    seqs,
    mps,
    page,
    width,
    embeds,
    feats,
    proj_w,
    bias,
    gain,
    kv_w,
    sel,
    mask,
    dest,
    slots_out,
    hid_out,
    img_out,
    dest_out,
    e_buf,
    w_buf,
    pw_buf,
    f_buf,
    acc1,
    s1,
    r1,
    acc2,
    s2,
    r2,
    sq_own,
    sq_recv,
    scale,
    outf,
    by_owner,
    arrived,
    p_own,
    p_send,
    p_recv,
    hid,
    i_scaled,
    i_acc,
    is1,
    ir1,
    is2,
    ir2,
    isq_own,
    isq_recv,
    ikv,
    load_sem,
    w_sem,
    e_sem,
    pw_sem,
    fl_sem,
    send1,
    recv1,
    send2,
    recv2,
    send_sq,
    recv_sq,
    send_f,
    recv_f,
    send_fc,
    recv_fc,
    send_r,
    recv_r,
    send_h,
    recv_h,
    send_i1,
    recv_i1,
    send_i2,
    recv_i2,
    send_iq,
    recv_iq,
    send_z,
    recv_z,
    send_y,
    recv_y,
    loc_sem,
    send_iz,
    recv_iz,
    send_iy,
    recv_iy,
    send_if,
    recv_if,
    send_d,
    recv_d,
    misc_sem,
):
    g = lax.axis_index("group")
    s = lax.axis_index("seq")
    m = lax.axis_index("mp")
    chips = mps // CORES
    chip = m // CORES
    core = m % CORES
    partner = chip * CORES + (1 - core)
    peer = 1 - g
    chunks, feat_local, _ = w_buf.shape
    tokens = e_buf.shape[0]
    tiles = tokens // TILE
    steps = chunks * tiles
    rows_img = hid.shape[0]
    half_rows = rows_img // groups
    core_rows = half_rows // CORES
    cols = chunks * LANES
    block_cols = cols * groups
    slots = sel.shape[0]
    pages = sel.shape[1]
    block = slots * page // seqs
    own_cols = chips * LANES

    def remote(src, dst, send, recv, **where):
        return pltpu.make_async_remote_copy(
            src_ref=src,
            dst_ref=dst,
            send_sem=send,
            recv_sem=recv,
            device_id=where,
            device_id_type=MESH,
        )

    def seq_at(k):
        return lax.rem(s + k, seqs)

    def seq_from(k):
        return lax.rem(s + seqs - k, seqs)

    def mp_at(k):
        return lax.rem(m + k, mps)

    def chip_at(k):
        return lax.rem(chip + k, chips) * CORES + core

    def e_copy(i):
        return pltpu.make_async_copy(embeds.at[ds(i, TILE), :], e_buf.at[ds(i, TILE), :], e_sem.at[i])

    def w_copy(c, q, k):
        target = lax.rem(chip + k, chips) * CORES + (core if q == 0 else 1 - core)
        start = target * block_cols + g * cols + c * LANES
        return pltpu.make_async_copy(
            kv_w.at[:, pl.ds(pl.multiple_of(start, LANES), LANES)],
            w_buf.at[c, :, (q * chips + k) * LANES : (q * chips + k + 1) * LANES],
            w_sem.at[c, q * chips + k],
        )

    e_copy(0).start()
    for q in range(CORES):
        for k in range(chips):
            w_copy(0, q, k).start()
    for i in range(1, tiles):
        e_copy(i).start()
    for c in range(1, chunks):
        for q in range(CORES):
            for k in range(chips):
                w_copy(c, q, k).start()
    pw_copy = pltpu.make_async_copy(proj_w, pw_buf, pw_sem)
    pw_copy.start()
    own_feats = pltpu.make_async_copy(feats.at[s], f_buf.at[s], fl_sem)
    own_feats.start()

    barrier = pltpu.get_barrier_semaphore()
    for k in range(1, seqs):
        pl.semaphore_signal(barrier, inc=1, device_id={"seq": seq_at(k)}, device_id_type=MESH)
    for k in range(1, mps):
        pl.semaphore_signal(barrier, inc=1, device_id={"mp": mp_at(k)}, device_id_type=MESH)
    pl.semaphore_signal(barrier, inc=1, device_id={"group": peer}, device_id_type=MESH)
    pl.semaphore_wait(barrier, seqs - 1 + mps - 1 + 1)

    def f_send(k):
        rows = ds(core, core_rows)
        return remote(
            feats.at[seq_at(k), rows, :],
            f_buf.at[s, rows, :],
            send_f.at[k - 1],
            recv_f.at[k - 1],
            seq=seq_at(k),
        )

    def f_share(k):
        rows = ds(core, core_rows)
        src = seq_from(k)
        return remote(
            f_buf.at[src, rows, :],
            f_buf.at[src, rows, :],
            send_fc.at[k - 1],
            recv_fc.at[k - 1],
            mp=partner,
        )

    def d_send(k):
        return remote(dest, dest_out.at[s], send_d.at[k - 1], recv_d.at[k - 1], seq=seq_at(k))

    for k in range(1, seqs):
        f_send(k).start()
    for k in range(1, seqs):
        d_send(k).start()
    d_local = pltpu.make_async_copy(dest, dest_out.at[s], misc_sem.at[0])
    d_local.start()

    def first(n):
        return remote(s1.at[n], r1.at[n], send1.at[n], recv1.at[n], mp=partner)

    def second(n, k):
        return remote(
            s2.at[n, k - 1], r2.at[n, k - 1], send2.at[n, k - 1], recv2.at[n, k - 1], mp=chip_at(k)
        )

    def sq_send(k):
        return remote(sq_own, sq_recv.at[k - 1], send_sq.at[k - 1], recv_sq.at[k - 1], mp=mp_at(k))

    def p_copy(k):
        return remote(
            p_send.at[seq_at(k)], p_recv.at[k - 1], send_r.at[k - 1], recv_r.at[k - 1], seq=seq_at(k)
        )

    def scale_tile(i):
        e_copy(i).wait()

        def body(b, carry):
            rows = ds(i * (TILE // LANES) + b, LANES)
            total = jnp.zeros((LANES, LANES), F32)
            for j in range(feat_local // LANES):
                at = slice(j * LANES, (j + 1) * LANES)
                value = e_buf[rows, at].astype(F32)
                total = total + value * value
                e_buf[rows, at] = (value * gain[:, at].astype(F32)).astype(BF16)
            sq_own[pl.ds(i * (TILE // LANES) + b, 1), :] = jnp.sum(
                jnp.transpose(total), axis=0, keepdims=True
            )
            return carry

        lax.fori_loop(0, TILE // LANES, body, 0)

    col_tile = min(512, feat_local)

    def project():
        for k in range(1, seqs):
            f_share(k).wait()
        own_feats.wait()
        pw_copy.wait()
        spread = f_buf[...].reshape(seqs * half_rows, f_buf.shape[2])

        def body(t, carry):
            at = ds(t, col_tile)
            out = jnp.dot(spread, pw_buf[:, at], preferred_element_type=F32)
            out = out.reshape(seqs, half_rows, col_tile)
            p_send[:, :, at] = out.astype(BF16)
            p_own[:, :, at] = out
            for k in range(1, seqs):
                remote(
                    p_send.at[seq_at(k), :, at],
                    p_recv.at[k - 1, :, at],
                    send_r.at[k - 1],
                    recv_r.at[k - 1],
                    seq=seq_at(k),
                ).start()
            return carry

        lax.fori_loop(0, feat_local // col_tile, body, 0)

    share_step = min(tiles + 1, steps)
    proj_step = min(tiles + 3, steps)

    def step(n, carry):
        @pl.when(n < steps)
        def _():
            c, i = n // tiles, lax.rem(n, tiles)

            @pl.when(n == 0)
            def _():
                for q in range(CORES):
                    for k in range(chips):
                        w_copy(0, q, k).wait()

            for cc in range(1, chunks):

                @pl.when(n == cc * tiles)
                def _():
                    for q in range(CORES):
                        for k in range(chips):
                            w_copy(cc, q, k).wait()

            @pl.when(c == 0)
            def _():
                scale_tile(i)

            part = jnp.dot(e_buf[ds(i, TILE), :], w_buf[c], preferred_element_type=F32)
            acc1[lax.rem(n, 2)] = part[:, :own_cols]
            s1[n] = part[:, own_cols:].astype(BF16)
            first(n).start()

            @pl.when(n == tiles - 1)
            def _():
                for k in range(1, mps):
                    sq_send(k).start()

        @pl.when(n == share_step)
        def _():
            for k in range(1, seqs):
                f_send(k).wait_recv()
                f_share(k).start()

        @pl.when(n > 0)
        def _():
            p = n - 1
            c, i = p // tiles, lax.rem(p, tiles)
            first(p).wait()
            total = acc1[lax.rem(p, 2)] + r1[p].astype(F32)
            acc2[c, ds(i, TILE), :] = total[:, :LANES]
            for k in range(1, chips):
                s2[p, k - 1] = total[:, k * LANES : (k + 1) * LANES].astype(BF16)
                second(p, k).start()

        @pl.when(n == proj_step)
        def _():
            project()

        return carry

    lax.fori_loop(0, steps + 1, step, 0)

    for k in range(1, mps):
        sq_send(k).wait()
    squares = sq_own[...]
    for k in range(1, mps):
        squares = squares + sq_recv[k - 1]
    scale[...] = mask[...] * lax.rsqrt(squares / width + 1e-05)

    def z_send(c, k):
        return remote(
            by_owner.at[c, ds(seq_at(k), block), :],
            arrived.at[c, ds(s, block), :],
            send_z.at[c, k - 1],
            recv_z.at[c, k - 1],
            seq=seq_at(k),
        )

    def out_at(rows, half, c):
        at = pl.ds(pl.multiple_of(half * cols + c * LANES, LANES), LANES)
        return slots_out.at[rows, at]

    def y_send(src, rows, c):
        return remote(src, out_at(rows, g, c), send_y.at[c], recv_y.at[c], group=peer)

    def local(src, rows, c):
        return pltpu.make_async_copy(src, out_at(rows, g, c), loc_sem.at[c])

    everything = pl.ds(0, slots * page)

    def finish(c):
        for i in range(tiles):
            for k in range(1, chips):
                second(c * tiles + i, k).wait()

        def body(b, carry):
            rows = ds(b, LANES)
            n = c * tiles + b // (TILE // LANES)
            within = ds(lax.rem(b, TILE // LANES), LANES)
            value = acc2[c, rows, :]
            for k in range(1, chips):
                value = value + r2[n, k - 1, within, :].astype(F32)
            acc2[c, rows, :] = value * spread_rows(scale[pl.ds(b, 1), :])
            return carry

        lax.fori_loop(0, tokens // LANES, body, 0)
        chosen = sel[...]
        for t in range(page):
            rows = acc2[c, pl.ds(t, pages, stride=page), :].astype(BF16)
            outf[pl.ds(t, slots, stride=page), :] = jnp.dot(
                chosen, rows, preferred_element_type=F32
            )
        by_owner[c] = outf[...].astype(BF16)
        for k in range(1, seqs):
            z_send(c, k).start()
        mine = ds(s, block)

        @pl.when(g == 0)
        def _():
            y_send(by_owner.at[c, mine, :], mine, c).start()
            local(by_owner.at[c], everything, c).start()

        @pl.when(g != 0)
        def _():
            y_send(by_owner.at[c], everything, c).start()
            local(by_owner.at[c, mine, :], mine, c).start()

    def forward(c, k):
        z_send(c, k).wait_recv()
        rows = ds(seq_from(k), block)

        @pl.when(g == 0)
        def _():
            y_send(arrived.at[c, rows, :], rows, c).start()

        @pl.when(g != 0)
        def _():
            local(arrived.at[c, rows, :], rows, c).start()

    finish(0)

    for k in range(1, seqs):
        p_copy(k).wait()
    own_rows = ds(g, half_rows)

    def gelu_body(t, carry):
        at = ds(t, col_tile)
        total = p_own[s, :, at] + bias[:, at].astype(F32)
        for k in range(1, seqs):
            total = total + p_recv[k - 1, :, at].astype(F32)
        hid[own_rows, at] = (
            0.5 * total * (1.0 + lax.erf(total * 0.5**0.5))
        ).astype(BF16)
        return carry

    lax.fori_loop(0, feat_local // col_tile, gelu_body, 0)
    h_send = remote(hid.at[own_rows, :], hid.at[own_rows, :], send_h, recv_h, group=peer)
    h_send.start()

    for c in range(1, chunks):
        finish(c)
    for k in range(1, seqs):
        forward(0, k)

    h_send.wait()
    hid_copy = pltpu.make_async_copy(hid, hid_out, misc_sem.at[1])
    hid_copy.start()
    total = jnp.zeros((rows_img, LANES), F32)
    for j in range(feat_local // LANES):
        at = slice(j * LANES, (j + 1) * LANES)
        value = hid[:, at].astype(F32)
        total = total + value * value
        i_scaled[:, at] = (value * gain[:, at].astype(F32)).astype(BF16)
    isq_own[...] = jnp.broadcast_to(
        jnp.sum(jnp.transpose(total), axis=0, keepdims=True), isq_own.shape
    )

    def iq_send(k):
        return remote(isq_own, isq_recv.at[k - 1], send_iq.at[k - 1], recv_iq.at[k - 1], mp=mp_at(k))

    for k in range(1, mps):
        iq_send(k).start()
    for c in range(chunks):
        part = jnp.dot(i_scaled[...], w_buf[c], preferred_element_type=F32)
        i_acc[c] = part[:, :own_cols]
        is1[c] = part[:, own_cols:].astype(BF16)
    i_first = remote(is1, ir1, send_i1, recv_i1, mp=partner)
    i_first.start()

    def i_second(k):
        return remote(
            is2.at[k - 1], ir2.at[k - 1], send_i2.at[k - 1], recv_i2.at[k - 1], mp=chip_at(k)
        )

    i_first.wait()
    for c in range(chunks):
        total = i_acc[c] + ir1[c].astype(F32)
        i_acc[c] = total
        for k in range(1, chips):
            is2[k - 1, c] = total[:, k * LANES : (k + 1) * LANES].astype(BF16)
    for k in range(1, chips):
        i_second(k).start()
    for k in range(1, mps):
        iq_send(k).wait()
    squares = isq_own[...]
    for k in range(1, mps):
        squares = squares + isq_recv[k - 1]
    i_scale = spread_rows(lax.rsqrt(squares / width + 1e-05)[:1])
    for k in range(1, chips):
        i_second(k).wait()
    for c in range(chunks):
        value = i_acc[c, :, :LANES]
        for k in range(1, chips):
            value = value + ir2[k - 1, c].astype(F32)
        ikv[:, c * LANES : (c + 1) * LANES] = (value * i_scale).astype(BF16)

    def img_at(index, half):
        return img_out.at[index, :, pl.ds(pl.multiple_of(half * cols, cols), cols)]

    def iz_send(k):
        return remote(ikv, img_at(s, g), send_iz.at[k - 1], recv_iz.at[k - 1], seq=seq_at(k))

    iy_send = remote(ikv, img_at(s, g), send_iy, recv_iy, group=peer)
    for k in range(1, seqs):
        iz_send(k).start()
    iy_send.start()
    i_local = pltpu.make_async_copy(ikv, img_at(s, g), misc_sem.at[2])
    i_local.start()

    def if_send(k):
        src = seq_from(k)
        return remote(
            img_at(src, 0), img_at(src, 0), send_if.at[k - 1], recv_if.at[k - 1], group=peer
        )

    for c in range(1, chunks):
        for k in range(1, seqs):
            forward(c, k)
    for k in range(1, seqs):
        iz_send(k).wait_recv()

        @pl.when(g == 0)
        def _():
            if_send(k).start()

    for c in range(chunks):
        for k in range(1, seqs):
            z_send(c, k).wait_send()
        y_send(by_owner.at[c], everything, c).wait()
        local(by_owner.at[c], everything, c).wait()
    for k in range(1, seqs):
        f_send(k).wait_send()
        d_send(k).wait()
        iz_send(k).wait_send()

        @pl.when(g == 0)
        def _():
            if_send(k).wait_send()

        @pl.when(g != 0)
        def _():
            if_send(k).wait_recv()

    iy_send.wait()
    i_local.wait()
    d_local.wait()
    hid_copy.wait()


def prefill(mesh_sizes, page, width, embeds, feats, proj_w, bias, gain, kv_w, sel, mask, dest):
    groups, seqs, mps = mesh_sizes
    chips = mps // CORES
    tokens, feat_local = embeds.shape
    tiles = tokens // TILE
    _, half_rows, channels = feats.shape
    rows_img = half_rows * groups
    block_cols = kv_w.shape[1] // mps
    cols = block_cols // groups
    chunks = cols // LANES
    steps = chunks * tiles
    slots = sel.shape[0]
    dma = pltpu.SemaphoreType.DMA
    vmem = pl.BlockSpec(memory_space=pltpu.VMEM)
    anywhere = pl.BlockSpec(memory_space=pl.ANY)
    dense = tokens // LANES
    return pl.pallas_call(
        functools.partial(prefill_kernel, groups, seqs, mps, page, width),
        out_shape=(
            jax.ShapeDtypeStruct((slots * page, block_cols), BF16),
            jax.ShapeDtypeStruct((rows_img, feat_local), BF16),
            jax.ShapeDtypeStruct((seqs, rows_img, block_cols), BF16),
            jax.ShapeDtypeStruct((seqs, 8, rows_img), F32),
        ),
        in_specs=[anywhere] * 3 + [vmem, vmem, anywhere, vmem, vmem, anywhere],
        out_specs=(anywhere,) * 4,
        scratch_shapes=[
            pltpu.VMEM((tokens, feat_local), BF16),
            pltpu.VMEM((chunks, feat_local, mps * LANES), BF16),
            pltpu.VMEM((channels, feat_local), BF16),
            pltpu.VMEM((seqs, half_rows, channels), BF16),
            pltpu.VMEM((2, TILE, chips * LANES), F32),
            pltpu.VMEM((steps, TILE, chips * LANES), BF16),
            pltpu.VMEM((steps, TILE, chips * LANES), BF16),
            pltpu.VMEM((chunks, tokens, LANES), F32),
            pltpu.VMEM((steps, chips - 1, TILE, LANES), BF16),
            pltpu.VMEM((steps, chips - 1, TILE, LANES), BF16),
            pltpu.VMEM((dense, LANES), F32),
            pltpu.VMEM((mps - 1, dense, LANES), F32),
            pltpu.VMEM((dense, LANES), F32),
            pltpu.VMEM((slots * page, LANES), F32),
            pltpu.VMEM((chunks, slots * page, LANES), BF16),
            pltpu.VMEM((chunks, slots * page, LANES), BF16),
            pltpu.VMEM((seqs, half_rows, feat_local), F32),
            pltpu.VMEM((seqs, half_rows, feat_local), BF16),
            pltpu.VMEM((seqs - 1, half_rows, feat_local), BF16),
            pltpu.VMEM((rows_img, feat_local), BF16),
            pltpu.VMEM((rows_img, feat_local), BF16),
            pltpu.VMEM((chunks, rows_img, chips * LANES), F32),
            pltpu.VMEM((chunks, rows_img, chips * LANES), BF16),
            pltpu.VMEM((chunks, rows_img, chips * LANES), BF16),
            pltpu.VMEM((chips - 1, chunks, rows_img, LANES), BF16),
            pltpu.VMEM((chips - 1, chunks, rows_img, LANES), BF16),
            pltpu.VMEM((8, LANES), F32),
            pltpu.VMEM((mps - 1, 8, LANES), F32),
            pltpu.VMEM((rows_img, cols), BF16),
            dma((1,)),
            dma((chunks, mps)),
            dma((tiles,)),
            dma,
            dma,
            dma((steps,)),
            dma((steps,)),
            dma((steps, chips - 1)),
            dma((steps, chips - 1)),
            dma((mps - 1,)),
            dma((mps - 1,)),
            dma((seqs - 1,)),
            dma((seqs - 1,)),
            dma((seqs - 1,)),
            dma((seqs - 1,)),
            dma((seqs - 1,)),
            dma((seqs - 1,)),
            dma,
            dma,
            dma,
            dma,
            dma((chips - 1,)),
            dma((chips - 1,)),
            dma((mps - 1,)),
            dma((mps - 1,)),
            dma((chunks, seqs - 1)),
            dma((chunks, seqs - 1)),
            dma((chunks,)),
            dma((chunks,)),
            dma((chunks,)),
            dma((seqs - 1,)),
            dma((seqs - 1,)),
            dma,
            dma,
            dma((seqs - 1,)),
            dma((seqs - 1,)),
            dma((seqs - 1,)),
            dma((seqs - 1,)),
            dma((3,)),
        ],
        compiler_params=pltpu.CompilerParams(
            collective_id=0, has_side_effects=True, vmem_limit_bytes=62 * 1024 * 1024
        ),
        name="prefill_pages",
    )(embeds, feats, proj_w, bias, gain, kv_w, sel, mask, dest)


def patch_kernel(index_ref, offset_ref, text, img, dest, out):
    rows = text.shape[0]
    first = offset_ref[pl.program_id(0)]
    spots = (dest[0, :1, :] - first.astype(F32)).astype(jnp.int32)
    hit = lax.broadcasted_iota(jnp.int32, (rows, dest.shape[2]), 0) == spots
    placed = jnp.dot(
        jnp.where(hit, 1.0, 0.0).astype(BF16), img[0], preferred_element_type=F32
    )
    out[...] = (text[...].astype(F32) + placed).astype(BF16)


def patch(index, offset, text, img, dest):
    seqs, rows_img, block_cols = img.shape
    block = text.shape[0] // seqs
    return pl.pallas_call(
        patch_kernel,
        out_shape=jax.ShapeDtypeStruct(text.shape, text.dtype),
        grid_spec=pltpu.PrefetchScalarGridSpec(
            num_scalar_prefetch=2,
            grid=(seqs,),
            in_specs=[
                pl.BlockSpec((block, block_cols), lambda b, index, offset: (b, 0)),
                pl.BlockSpec((1, rows_img, block_cols), lambda b, index, offset: (index[b], 0, 0)),
                pl.BlockSpec((1, 8, rows_img), lambda b, index, offset: (index[b], 0, 0)),
            ],
            out_specs=pl.BlockSpec((block, block_cols), lambda b, index, offset: (b, 0)),
        ),
        name="place_images",
    )(index, offset, text, img, dest)


def per_device(
    mesh_sizes,
    embeds,
    image_feats,
    image_pos,
    proj_w,
    proj_b,
    norm_gain,
    kv_w,
    prompt_lengths,
    page_owner,
    queries,
    kv_cache,
    new_kv,
    cache_lengths,
):
    groups, seqs, mps = mesh_sizes
    group_index = lax.axis_index("group")
    prefill_side = group_index == 0
    seq_index = lax.axis_index("seq")
    token_rows, width_local = embeds.shape
    width = width_local * mps
    image_rows, all_channels = image_feats.shape
    prompt_len = token_rows * seqs // prompt_lengths.shape[0]
    channels = proj_w.shape[0]

    half_rows = image_rows // groups
    features = lax.dynamic_slice_in_dim(image_feats, group_index * half_rows, half_rows, axis=0)
    feats = jnp.transpose(features.reshape(half_rows, seqs, channels), (1, 0, 2))

    pages_dev = page_owner.shape[0]
    page = token_rows // pages_dev
    capacity = 2 * pages_dev // seqs
    slots = seqs * capacity
    owners = page_owner[:, 0]
    earlier = jnp.arange(pages_dev)[None, :] < jnp.arange(pages_dev)[:, None]
    same = owners[:, None] == owners[None, :]
    page_rank = jnp.sum((earlier & same).astype(jnp.int32), axis=1)
    slot_index = owners * capacity + page_rank
    sel = (jnp.arange(slots, dtype=jnp.int32)[:, None] == slot_index[None, :]).astype(BF16)

    first = seq_index * token_rows
    positions = first + jnp.arange(token_rows, dtype=jnp.int32)
    is_live = live_rows(positions, prompt_lengths, prompt_len)
    is_image = jnp.any(positions[:, None] == image_pos[None, :], axis=1)
    mask = (is_live & ~is_image).astype(F32).reshape(token_rows // LANES, LANES)

    local_pos = image_pos - first
    on_page = (local_pos // page)[:, None] == jnp.arange(pages_dev, dtype=jnp.int32)[None, :]
    image_slot = jnp.sum(jnp.where(on_page, slot_index[None, :], 0), axis=1)
    image_live = live_rows(image_pos, prompt_lengths, prompt_len)
    dest = jnp.where(image_live, image_slot * page + local_pos % page, -(1 << 20))
    dest = jnp.broadcast_to(dest.astype(F32)[None, :], (8, image_rows))

    text, image_hidden, img, dest_all = prefill(
        mesh_sizes,
        page,
        width,
        embeds,
        feats,
        proj_w,
        proj_b[None, :],
        norm_gain[None, :],
        kv_w,
        sel,
        mask,
        dest,
    )
    order = jnp.arange(seqs, dtype=jnp.int32)
    index = jnp.where(prefill_side, seq_index, order)
    offset = jnp.where(prefill_side, order, seq_index) * (capacity * page)
    page_slots = patch(index, offset, text, img, dest_all)
    page_slots = page_slots.reshape(slots, page, text.shape[1])

    empty_rows = jnp.zeros(queries.shape, BF16)
    attended = gated(
        jnp.logical_not(prefill_side), attend, empty_rows, queries, kv_cache, new_kv, cache_lengths
    )
    row_states = jnp.where(prefill_side, image_hidden, attended)
    return (page_slots, row_states)


def solution(mesh):
    mesh_sizes = (mesh.shape["group"], mesh.shape["seq"], mesh.shape["mp"])
    in_specs = (
        P("seq", "mp"),
        P("seq", None),
        P("seq"),
        P("seq", "mp"),
        P("mp"),
        P("mp"),
        P("mp", None),
        P(),
        P("seq", None),
        P("seq", "mp"),
        P("seq", None, "mp"),
        P("seq", "mp"),
        P("seq"),
    )
    out_specs = (P(("group", "seq"), None, "mp"), P(("group", "seq"), "mp"))
    return jax.shard_map(
        functools.partial(per_device, mesh_sizes),
        mesh=mesh,
        in_specs=in_specs,
        out_specs=out_specs,
        check_vma=False,
    )
```

```python
import functools

import jax
import jax.numpy as jnp
from jax import lax
from jax.experimental import pallas as pl
from jax.experimental.pallas import tpu as pltpu
from jax.sharding import PartitionSpec as P

HEAD = 128
LANES = 128
TILE = 512
CORES = 2
MESH = pl.DeviceIdType.MESH
F32 = jnp.float32
BF16 = jnp.bfloat16


def ds(index, size):
    return pl.ds(pl.multiple_of(index * size, size), size)


def spread_rows(row):
    return jnp.transpose(jnp.broadcast_to(row, (LANES, LANES)))


def prefill_kernel(
    groups,
    seqs,
    mps,
    prompt_len,
    embeds,
    image_feats,
    proj_w,
    kv_w,
    kv_cache,
    image_pos,
    bias,
    gain,
    page_owner,
    queries,
    new_kv,
    cache_lengths,
    prompt_lengths,
    slots_out,
    states_out,
    img_out,
    dest_out,
    sel,
    mask,
    dest,
    f_rows,
    feats,
    e_buf,
    w_buf,
    pw_buf,
    f_buf,
    acc1,
    s1,
    r1,
    acc2,
    s2,
    r2,
    sq_own,
    sq_recv,
    scale,
    outf,
    by_owner,
    arrived,
    kv_send,
    kv_recv,
    by_peer,
    p_own,
    p_send,
    p_recv,
    hid,
    i_scaled,
    i_acc,
    is1,
    ir1,
    is2,
    ir2,
    isq_own,
    isq_recv,
    ikv,
    q_rows,
    fresh,
    lengths,
    cache,
    a_scores,
    a_keys,
    a_values,
    a_limits,
    a_rows,
    attended,
    load_sem,
    cache_sem,
    w_sem,
    e_sem,
    pw_sem,
    fl_sem,
    send1,
    recv1,
    send2,
    recv2,
    send_sq,
    recv_sq,
    send_f,
    recv_f,
    send_fc,
    recv_fc,
    send_r,
    recv_r,
    send_h,
    recv_h,
    send_i1,
    recv_i1,
    send_i2,
    recv_i2,
    send_iq,
    recv_iq,
    send_z,
    recv_z,
    send_y,
    recv_y,
    send_k,
    recv_k,
    loc_sem,
    loc2_sem,
    send_iz,
    recv_iz,
    send_iy,
    recv_iy,
    send_if,
    recv_if,
    send_d,
    recv_d,
    misc_sem,
):
    g = lax.axis_index("group")
    s = lax.axis_index("seq")
    m = lax.axis_index("mp")
    chips = mps // CORES
    chip = m // CORES
    core = m % CORES
    partner = chip * CORES + (1 - core)
    peer = 1 - g
    chunks, feat_local, _ = w_buf.shape
    tokens = e_buf.shape[0]
    tiles = tokens // TILE
    steps = chunks * tiles
    rows_img = hid.shape[0]
    half_rows = rows_img // groups
    core_rows = half_rows // CORES
    cols = chunks * LANES
    block_cols = cols * groups
    slots, pages = sel.shape
    page = tokens // pages
    capacity = slots // seqs
    width = feat_local * mps
    channels = feats.shape[2]
    block = slots * page // seqs
    own_cols = chips * LANES

    def remote(src, dst, send, recv, **where):
        return pltpu.make_async_remote_copy(
            src_ref=src,
            dst_ref=dst,
            send_sem=send,
            recv_sem=recv,
            device_id=where,
            device_id_type=MESH,
        )

    def seq_at(k):
        return lax.rem(s + k, seqs)

    def seq_from(k):
        return lax.rem(s + seqs - k, seqs)

    def mp_at(k):
        return lax.rem(m + k, mps)

    def chip_at(k):
        return lax.rem(chip + k, chips) * CORES + core

    def e_copy(i):
        return pltpu.make_async_copy(embeds.at[ds(i, TILE), :], e_buf.at[ds(i, TILE), :], e_sem.at[i])

    def w_copy(c, q, k):
        target = lax.rem(chip + k, chips) * CORES + (core if q == 0 else 1 - core)
        start = target * block_cols + g * cols + c * LANES
        return pltpu.make_async_copy(
            kv_w.at[:, pl.ds(pl.multiple_of(start, LANES), LANES)],
            w_buf.at[c, :, (q * chips + k) * LANES : (q * chips + k + 1) * LANES],
            w_sem.at[c, q * chips + k],
        )

    f_load = pltpu.make_async_copy(image_feats.at[ds(g, half_rows), :], f_rows, load_sem.at[0])
    f_load.start()
    barrier = pltpu.get_barrier_semaphore()
    for k in range(1, seqs):
        pl.semaphore_signal(barrier, inc=1, device_id={"seq": seq_at(k)}, device_id_type=MESH)
    for k in range(1, mps):
        pl.semaphore_signal(barrier, inc=1, device_id={"mp": mp_at(k)}, device_id_type=MESH)
    pl.semaphore_signal(barrier, inc=1, device_id={"group": peer}, device_id_type=MESH)
    e_copy(0).start()
    for q in range(CORES):
        for k in range(chips):
            w_copy(0, q, k).start()
    for i in range(1, tiles):
        e_copy(i).start()
    for c in range(1, chunks):
        for q in range(CORES):
            for k in range(chips):
                w_copy(c, q, k).start()
    pw_copy = pltpu.make_async_copy(proj_w, pw_buf, pw_sem)
    pw_copy.start()

    f_load.wait()
    for b in range(seqs):
        feats[b] = f_rows[:, b * channels : (b + 1) * channels]
    own_feats = pltpu.make_async_copy(feats.at[s], f_buf.at[s], fl_sem)
    own_feats.start()

    pl.semaphore_wait(barrier, seqs - 1 + mps - 1 + 1)

    def f_send(k):
        rows = ds(core, core_rows)
        return remote(
            feats.at[seq_at(k), rows, :],
            f_buf.at[s, rows, :],
            send_f.at[k - 1],
            recv_f.at[k - 1],
            seq=seq_at(k),
        )

    def f_share(k):
        rows = ds(core, core_rows)
        src = seq_from(k)
        return remote(
            f_buf.at[src, rows, :],
            f_buf.at[src, rows, :],
            send_fc.at[k - 1],
            recv_fc.at[k - 1],
            mp=partner,
        )

    def d_send(k):
        return remote(dest, dest_out.at[s], send_d.at[k - 1], recv_d.at[k - 1], seq=seq_at(k))

    for k in range(1, seqs):
        f_send(k).start()

    prompt = (s * tokens) // prompt_len
    limit = prompt_lengths[prompt]
    base = s * tokens - prompt * prompt_len
    spots = image_pos[...] - s * tokens
    down = lax.broadcasted_iota(jnp.int32, (pages, LANES), 0)
    across = lax.broadcasted_iota(jnp.int32, (pages, LANES), 1)
    owner_down = jnp.broadcast_to(page_owner[...].astype(F32), (pages, LANES))
    owner_across = jnp.transpose(owner_down)
    rank = jnp.sum(
        jnp.where((owner_down == owner_across) & (down < across), 1.0, 0.0), axis=0, keepdims=True
    )
    slot = owner_across[:1] * capacity + rank
    slot_rows = lax.broadcasted_iota(jnp.int32, (slots, LANES), 0).astype(F32)
    sel[...] = jnp.where(slot_rows == slot, 1.0, 0.0).astype(BF16)
    page_bits = page.bit_length() - 1
    on_page = down == lax.shift_right_logical(spots, page_bits)
    image_slot = jnp.sum(jnp.where(on_page, spread_rows(slot), 0.0), axis=0, keepdims=True)
    image_row = image_slot * page + (spots & (page - 1)).astype(F32)
    dest[...] = jnp.broadcast_to(
        jnp.where(spots + base < limit, image_row, -1048576.0), dest.shape
    )
    dense = mask.shape[0]
    tall = lax.broadcasted_iota(jnp.int32, (dense, LANES), 0)
    image_block = jnp.where(tall == lax.shift_right_logical(spots, 7), 1.0, 0.0)
    image_lane = jnp.where(down == (spots & (LANES - 1)), 1.0, 0.0)
    images = lax.dot_general(
        image_block.astype(BF16),
        image_lane.astype(BF16),
        (((1,), (1,)), ((), ())),
        preferred_element_type=F32,
    )
    token = tall * LANES + lax.broadcasted_iota(jnp.int32, (dense, LANES), 1)
    mask[...] = jnp.where((token + base < limit) & (images < 0.5), 1.0, 0.0)
    for k in range(1, seqs):
        d_send(k).start()
    d_local = pltpu.make_async_copy(dest, dest_out.at[s], misc_sem.at[0])
    d_local.start()

    def first(n):
        return remote(s1.at[n], r1.at[n], send1.at[n], recv1.at[n], mp=partner)

    def second(n, k):
        return remote(
            s2.at[n, k - 1], r2.at[n, k - 1], send2.at[n, k - 1], recv2.at[n, k - 1], mp=chip_at(k)
        )

    def sq_send(k):
        return remote(sq_own, sq_recv.at[k - 1], send_sq.at[k - 1], recv_sq.at[k - 1], mp=mp_at(k))

    def p_copy(k):
        return remote(
            p_send.at[seq_at(k)], p_recv.at[k - 1], send_r.at[k - 1], recv_r.at[k - 1], seq=seq_at(k)
        )

    def scale_tile(i):
        e_copy(i).wait()

        def body(b, carry):
            rows = ds(i * (TILE // LANES) + b, LANES)
            total = jnp.zeros((LANES, LANES), F32)
            for j in range(feat_local // LANES):
                at = slice(j * LANES, (j + 1) * LANES)
                value = e_buf[rows, at].astype(F32)
                total = total + value * value
                e_buf[rows, at] = (value * gain[:, at].astype(F32)).astype(BF16)
            sq_own[pl.ds(i * (TILE // LANES) + b, 1), :] = jnp.sum(
                jnp.transpose(total), axis=0, keepdims=True
            )
            return carry

        lax.fori_loop(0, TILE // LANES, body, 0)

    col_tile = min(512, feat_local)

    def project():
        for k in range(1, seqs):
            f_share(k).wait()
        own_feats.wait()
        pw_copy.wait()
        spread = f_buf[...].reshape(seqs * half_rows, f_buf.shape[2])

        def body(t, carry):
            at = ds(t, col_tile)
            out = jnp.dot(spread, pw_buf[:, at], preferred_element_type=F32)
            out = out.reshape(seqs, half_rows, col_tile)
            p_send[:, :, at] = out.astype(BF16)
            p_own[:, :, at] = out
            for k in range(1, seqs):
                remote(
                    p_send.at[seq_at(k), :, at],
                    p_recv.at[k - 1, :, at],
                    send_r.at[k - 1],
                    recv_r.at[k - 1],
                    seq=seq_at(k),
                ).start()
            return carry

        lax.fori_loop(0, feat_local // col_tile, body, 0)

    share_step = min(tiles + 1, steps)
    proj_step = min(tiles + 3, steps)

    def step(n, carry):
        @pl.when(n < steps)
        def _():
            c, i = n // tiles, lax.rem(n, tiles)

            @pl.when(n == 0)
            def _():
                for q in range(CORES):
                    for k in range(chips):
                        w_copy(0, q, k).wait()

            for cc in range(1, chunks):

                @pl.when(n == cc * tiles)
                def _():
                    for q in range(CORES):
                        for k in range(chips):
                            w_copy(cc, q, k).wait()

            @pl.when(c == 0)
            def _():
                scale_tile(i)

            part = jnp.dot(e_buf[ds(i, TILE), :], w_buf[c], preferred_element_type=F32)
            acc1[lax.rem(n, 2)] = part[:, :own_cols]
            s1[n] = part[:, own_cols:].astype(BF16)
            first(n).start()

            @pl.when(n == tiles - 1)
            def _():
                for k in range(1, mps):
                    sq_send(k).start()

        @pl.when(n == share_step)
        def _():
            for k in range(1, seqs):
                f_send(k).wait_recv()
                f_share(k).start()

        @pl.when(n > 0)
        def _():
            p = n - 1
            c, i = p // tiles, lax.rem(p, tiles)
            first(p).wait()
            total = acc1[lax.rem(p, 2)] + r1[p].astype(F32)
            acc2[c, ds(i, TILE), :] = total[:, :LANES]
            for k in range(1, chips):
                s2[p, k - 1] = total[:, k * LANES : (k + 1) * LANES].astype(BF16)
                second(p, k).start()

        @pl.when(n == proj_step)
        def _():
            project()

        return carry

    lax.fori_loop(0, steps + 1, step, 0)

    for k in range(1, mps):
        sq_send(k).wait()
    squares = sq_own[...]
    for k in range(1, mps):
        squares = squares + sq_recv[k - 1]
    scale[...] = mask[...] * lax.rsqrt(squares / width + 1e-05)

    def z_send(c, k):
        return remote(
            by_owner.at[c, ds(seq_at(k), block), :],
            arrived.at[c, ds(s, block), :],
            send_z.at[c, k - 1],
            recv_z.at[c, k - 1],
            seq=seq_at(k),
        )

    def out_at(rows, half, c):
        at = pl.ds(pl.multiple_of(half * cols + c * LANES, LANES), LANES)
        return slots_out.at[rows, at]

    def y_send(src, rows, c):
        return remote(src, out_at(rows, g, c), send_y.at[c], recv_y.at[c], group=peer)

    def local(src, rows, c):
        return pltpu.make_async_copy(src, out_at(rows, g, c), loc_sem.at[c])

    everything = pl.ds(0, slots * page)

    def select(c, target):
        chosen = sel[...]
        for t in range(page):
            rows = acc2[c, pl.ds(t, pages, stride=page), :].astype(BF16)
            outf[pl.ds(t, slots, stride=page), :] = jnp.dot(
                chosen, rows, preferred_element_type=F32
            )
        target[c] = outf[...].astype(BF16)

    def k_send(c):
        return remote(kv_send.at[c], kv_recv.at[c], send_k.at[c], recv_k.at[c], group=peer)

    def local2(c):
        return pltpu.make_async_copy(
            by_peer.at[c], out_at(everything, 1 - g, c), loc2_sem.at[c]
        )

    def finish(c):
        for i in range(tiles):
            for k in range(1, chips):
                second(c * tiles + i, k).wait()

        def body(b, carry):
            rows = ds(b, LANES)
            n = c * tiles + b // (TILE // LANES)
            within = ds(lax.rem(b, TILE // LANES), LANES)
            value = acc2[c, rows, :]
            for k in range(1, chips):
                value = value + r2[n, k - 1, within, :].astype(F32)
            value = value * spread_rows(scale[pl.ds(b, 1), :])
            acc2[c, rows, :] = value
            kv_send[c, rows, :] = value.astype(BF16)
            return carry

        lax.fori_loop(0, tokens // LANES, body, 0)
        select(c, by_owner)
        for k in range(1, seqs):
            z_send(c, k).start()
        mine = ds(s, block)

        @pl.when(g == 0)
        def _():
            y_send(by_owner.at[c, mine, :], mine, c).start()
            local(by_owner.at[c], everything, c).start()

        @pl.when(g != 0)
        def _():
            local(by_owner.at[c, mine, :], mine, c).start()

    def take_peer(c):
        k_send(c).wait_recv()
        acc2[c] = kv_recv[c].astype(F32)
        select(c, by_peer)
        local2(c).start()

    def forward(c, k):
        z_send(c, k).wait_recv()
        rows = ds(seq_from(k), block)

        @pl.when(g == 0)
        def _():
            y_send(arrived.at[c, rows, :], rows, c).start()

        @pl.when(g != 0)
        def _():
            local(arrived.at[c, rows, :], rows, c).start()

    finish(0)

    for k in range(1, seqs):
        p_copy(k).wait()
    own_rows = ds(g, half_rows)

    def gelu_body(t, carry):
        at = ds(t, col_tile)
        total = p_own[s, :, at] + bias[:, at].astype(F32)
        for k in range(1, seqs):
            total = total + p_recv[k - 1, :, at].astype(F32)
        hid[own_rows, at] = (
            0.5 * total * (1.0 + lax.erf(total * 0.5**0.5))
        ).astype(BF16)
        return carry

    lax.fori_loop(0, feat_local // col_tile, gelu_body, 0)
    h_send = remote(hid.at[own_rows, :], hid.at[own_rows, :], send_h, recv_h, group=peer)
    h_send.start()


    @pl.when(g != 0)
    def _():
        k_send(0).start()

    for c in range(1, chunks):
        finish(c)
    forward(0, 1)

    h_send.wait()

    @pl.when(g != 0)
    def _():
        for c in range(1, chunks):
            k_send(c).start()

    hid_copy = pltpu.make_async_copy(hid, states_out, misc_sem.at[1])

    @pl.when(g == 0)
    def _():
        hid_copy.start()

    total = jnp.zeros((rows_img, LANES), F32)
    for j in range(feat_local // LANES):
        at = slice(j * LANES, (j + 1) * LANES)
        value = hid[:, at].astype(F32)
        total = total + value * value
        i_scaled[:, at] = (value * gain[:, at].astype(F32)).astype(BF16)
    isq_own[...] = jnp.broadcast_to(
        jnp.sum(jnp.transpose(total), axis=0, keepdims=True), isq_own.shape
    )

    def iq_send(k):
        return remote(isq_own, isq_recv.at[k - 1], send_iq.at[k - 1], recv_iq.at[k - 1], mp=mp_at(k))

    for k in range(1, mps):
        iq_send(k).start()
    for c in range(chunks):
        part = jnp.dot(i_scaled[...], w_buf[c], preferred_element_type=F32)
        i_acc[c] = part[:, :own_cols]
        is1[c] = part[:, own_cols:].astype(BF16)
    i_first = remote(is1, ir1, send_i1, recv_i1, mp=partner)
    i_first.start()

    def i_second(k):
        return remote(
            is2.at[k - 1], ir2.at[k - 1], send_i2.at[k - 1], recv_i2.at[k - 1], mp=chip_at(k)
        )

    i_first.wait()
    for c in range(chunks):
        total = i_acc[c] + ir1[c].astype(F32)
        i_acc[c] = total
        for k in range(1, chips):
            is2[k - 1, c] = total[:, k * LANES : (k + 1) * LANES].astype(BF16)
    for k in range(1, chips):
        i_second(k).start()
    for k in range(1, mps):
        iq_send(k).wait()
    squares = isq_own[...]
    for k in range(1, mps):
        squares = squares + isq_recv[k - 1]
    i_scale = spread_rows(lax.rsqrt(squares / width + 1e-05)[:1])
    for k in range(1, chips):
        i_second(k).wait()
    for c in range(chunks):
        value = i_acc[c, :, :LANES]
        for k in range(1, chips):
            value = value + ir2[k - 1, c].astype(F32)
        ikv[:, c * LANES : (c + 1) * LANES] = (value * i_scale).astype(BF16)

    def img_at(index, half):
        return img_out.at[index, :, pl.ds(pl.multiple_of(half * cols, cols), cols)]

    def iz_send(k):
        return remote(ikv, img_at(s, g), send_iz.at[k - 1], recv_iz.at[k - 1], seq=seq_at(k))

    iy_send = remote(ikv, img_at(s, g), send_iy, recv_iy, group=peer)
    for k in range(1, seqs):
        iz_send(k).start()
    iy_send.start()
    i_local = pltpu.make_async_copy(ikv, img_at(s, g), misc_sem.at[2])
    i_local.start()

    def if_send(k):
        src = seq_from(k)
        return remote(
            img_at(src, 0), img_at(src, 0), send_if.at[k - 1], recv_if.at[k - 1], group=peer
        )

    heads = queries.shape[1] // HEAD
    kv_heads = kv_cache.shape[2] // (2 * HEAD)
    share = heads // kv_heads
    rows_dec = queries.shape[0]
    batch = LANES // heads

    def cache_copy(b):
        return pltpu.make_async_copy(
            kv_cache.at[ds(b, batch)], cache.at[lax.rem(b, 2)], cache_sem.at[lax.rem(b, 2)]
        )

    def attend_batch(b, carry):
        cache_copy(b).wait()

        @pl.when(b + 1 < rows_dec // batch)
        def _():
            cache_copy(b + 1).start()

        at = lax.rem(b, 2)
        for r in range(batch):
            span = slice(r * heads, (r + 1) * heads)
            query = q_rows[pl.ds(pl.multiple_of(b * LANES + r * heads, 8), heads), :].astype(BF16)
            new = fresh[pl.ds(b * batch + r, 1), :]
            a_limits[span, :] = jnp.broadcast_to(
                lengths[pl.ds(b * batch + r, 1), :], (heads, LANES)
            )
            for h in range(kv_heads):
                part = slice(r * heads + h * share, r * heads + (h + 1) * share)
                key = 2 * HEAD * h
                product = lax.dot_general(
                    query,
                    cache[at, r, :, key : key + HEAD],
                    (((1,), (1,)), ((), ())),
                    preferred_element_type=F32,
                )
                a_scores[part, :] = product[h * share : (h + 1) * share]
                a_keys[part, :] = jnp.broadcast_to(new[:, key : key + HEAD], (share, HEAD))
                a_values[part, :] = jnp.broadcast_to(
                    new[:, key + HEAD : key + 2 * HEAD], (share, HEAD)
                )
        lane = lax.broadcasted_iota(jnp.int32, (LANES, LANES), 1).astype(F32)
        scores = jnp.where(lane < a_limits[...], a_scores[...] * HEAD ** (-0.5), -1e30)
        own = jnp.sum(q_rows[ds(b, LANES), :] * a_keys[...], axis=1, keepdims=True) * HEAD ** (-0.5)
        top = jnp.maximum(jnp.max(scores, axis=1, keepdims=True), own)
        weights = jnp.exp(scores - top)
        own_weight = jnp.exp(own - top)
        total = jnp.sum(weights, axis=1, keepdims=True) + own_weight
        a_scores[...] = weights / total
        own_part = (own_weight / total).astype(BF16).astype(F32) * a_values[...]
        a_values[...] = own_part
        for r in range(batch):
            span = slice(r * heads, (r + 1) * heads)
            probs = a_scores[span, :].astype(BF16)
            for h in range(kv_heads):
                part = slice(r * heads + h * share, r * heads + (h + 1) * share)
                value = 2 * HEAD * h + HEAD
                product = jnp.dot(
                    probs, cache[at, r, :, value : value + HEAD], preferred_element_type=F32
                )
                a_rows[pl.ds(pl.multiple_of(b * LANES, LANES) + r * heads + h * share, share), :] = (
                    product[h * share : (h + 1) * share] + a_values[part, :]
                )
        return carry

    att_copy = pltpu.make_async_copy(attended, states_out, misc_sem.at[1])

    @pl.when(g != 0)
    def _():
        cache_copy(0).start()
        for j in range(heads):
            q_rows[pl.ds(j, rows_dec, stride=heads), :] = queries[
                :, j * HEAD : (j + 1) * HEAD
            ].astype(F32)
        fresh[...] = new_kv[...].astype(F32)
        lengths[...] = spread_rows(cache_lengths[...].astype(F32))
        lax.fori_loop(0, rows_dec // batch, attend_batch, 0)
        for j in range(heads):
            attended[:, j * HEAD : (j + 1) * HEAD] = a_rows[
                pl.ds(j, rows_dec, stride=heads), :
            ].astype(BF16)
        att_copy.start()

    for k in range(2, seqs):
        forward(0, k)

    @pl.when(g == 0)
    def _():
        for c in range(chunks):
            take_peer(c)

    for c in range(1, chunks):
        for k in range(1, seqs):
            forward(c, k)
    for k in range(1, seqs):
        iz_send(k).wait_recv()

        @pl.when(g == 0)
        def _():
            if_send(k).start()

    for c in range(chunks):
        for k in range(1, seqs):
            z_send(c, k).wait_send()
        local(by_owner.at[c], everything, c).wait()

        @pl.when(g == 0)
        def _():
            y_send(by_owner.at[c], everything, c).wait_send()
            local2(c).wait()

        @pl.when(g != 0)
        def _():
            y_send(by_owner.at[c], everything, c).wait_recv()
            k_send(c).wait_send()

    for k in range(1, seqs):
        f_send(k).wait_send()
        d_send(k).wait()
        iz_send(k).wait_send()

        @pl.when(g == 0)
        def _():
            if_send(k).wait_send()

        @pl.when(g != 0)
        def _():
            if_send(k).wait_recv()

    iy_send.wait()
    i_local.wait()
    d_local.wait()
    hid_copy.wait()


def prefill(
    mesh_sizes,
    prompt_len,
    embeds,
    image_feats,
    proj_w,
    kv_w,
    kv_cache,
    image_pos,
    bias,
    gain,
    page_owner,
    queries,
    new_kv,
    cache_lengths,
    prompt_lengths,
):
    groups, seqs, mps = mesh_sizes
    chips = mps // CORES
    tokens, feat_local = embeds.shape
    tiles = tokens // TILE
    rows_img, all_channels = image_feats.shape
    half_rows = rows_img // groups
    channels = proj_w.shape[0]
    block_cols = kv_w.shape[1] // mps
    cols = block_cols // groups
    chunks = cols // LANES
    steps = chunks * tiles
    pages = page_owner.shape[0]
    page = tokens // pages
    slots = seqs * (2 * pages // seqs)
    rows_dec = queries.shape[0]
    heads = queries.shape[1] // HEAD
    batch = LANES // heads
    dma = pltpu.SemaphoreType.DMA
    vmem = pl.BlockSpec(memory_space=pltpu.VMEM)
    anywhere = pl.BlockSpec(memory_space=pl.ANY)
    dense = tokens // LANES
    return pl.pallas_call(
        functools.partial(prefill_kernel, groups, seqs, mps, prompt_len),
        out_shape=(
            jax.ShapeDtypeStruct((slots * page, block_cols), BF16),
            jax.ShapeDtypeStruct((rows_img, feat_local), BF16),
            jax.ShapeDtypeStruct((seqs, rows_img, block_cols), BF16),
            jax.ShapeDtypeStruct((seqs, 8, rows_img), F32),
        ),
        in_specs=[anywhere] * 5 + [vmem] * 7 + [pl.BlockSpec(memory_space=pltpu.SMEM)],
        out_specs=(anywhere,) * 4,
        scratch_shapes=[
            pltpu.VMEM((slots, pages), BF16),
            pltpu.VMEM((dense, LANES), F32),
            pltpu.VMEM((8, rows_img), F32),
            pltpu.VMEM((half_rows, all_channels), BF16),
            pltpu.VMEM((seqs, half_rows, channels), BF16),
            pltpu.VMEM((tokens, feat_local), BF16),
            pltpu.VMEM((chunks, feat_local, mps * LANES), BF16),
            pltpu.VMEM((channels, feat_local), BF16),
            pltpu.VMEM((seqs, half_rows, channels), BF16),
            pltpu.VMEM((2, TILE, chips * LANES), F32),
            pltpu.VMEM((steps, TILE, chips * LANES), BF16),
            pltpu.VMEM((steps, TILE, chips * LANES), BF16),
            pltpu.VMEM((chunks, tokens, LANES), F32),
            pltpu.VMEM((steps, chips - 1, TILE, LANES), BF16),
            pltpu.VMEM((steps, chips - 1, TILE, LANES), BF16),
            pltpu.VMEM((dense, LANES), F32),
            pltpu.VMEM((mps - 1, dense, LANES), F32),
            pltpu.VMEM((dense, LANES), F32),
            pltpu.VMEM((slots * page, LANES), F32),
            pltpu.VMEM((chunks, slots * page, LANES), BF16),
            pltpu.VMEM((chunks, slots * page, LANES), BF16),
            pltpu.VMEM((chunks, tokens, LANES), BF16),
            pltpu.VMEM((chunks, tokens, LANES), BF16),
            pltpu.VMEM((chunks, slots * page, LANES), BF16),
            pltpu.VMEM((seqs, half_rows, feat_local), F32),
            pltpu.VMEM((seqs, half_rows, feat_local), BF16),
            pltpu.VMEM((seqs - 1, half_rows, feat_local), BF16),
            pltpu.VMEM((rows_img, feat_local), BF16),
            pltpu.VMEM((rows_img, feat_local), BF16),
            pltpu.VMEM((chunks, rows_img, chips * LANES), F32),
            pltpu.VMEM((chunks, rows_img, chips * LANES), BF16),
            pltpu.VMEM((chunks, rows_img, chips * LANES), BF16),
            pltpu.VMEM((chips - 1, chunks, rows_img, LANES), BF16),
            pltpu.VMEM((chips - 1, chunks, rows_img, LANES), BF16),
            pltpu.VMEM((8, LANES), F32),
            pltpu.VMEM((mps - 1, 8, LANES), F32),
            pltpu.VMEM((rows_img, cols), BF16),
            pltpu.VMEM((rows_dec * heads, HEAD), F32),
            pltpu.VMEM(new_kv.shape, F32),
            pltpu.VMEM((rows_dec, LANES), F32),
            pltpu.VMEM((2, batch) + kv_cache.shape[1:], BF16),
            pltpu.VMEM((LANES, LANES), F32),
            pltpu.VMEM((LANES, LANES), F32),
            pltpu.VMEM((LANES, LANES), F32),
            pltpu.VMEM((LANES, LANES), F32),
            pltpu.VMEM((rows_dec * heads, HEAD), F32),
            pltpu.VMEM(queries.shape, BF16),
            dma((1,)),
            dma((2,)),
            dma((chunks, mps)),
            dma((tiles,)),
            dma,
            dma,
            dma((steps,)),
            dma((steps,)),
            dma((steps, chips - 1)),
            dma((steps, chips - 1)),
            dma((mps - 1,)),
            dma((mps - 1,)),
            dma((seqs - 1,)),
            dma((seqs - 1,)),
            dma((seqs - 1,)),
            dma((seqs - 1,)),
            dma((seqs - 1,)),
            dma((seqs - 1,)),
            dma,
            dma,
            dma,
            dma,
            dma((chips - 1,)),
            dma((chips - 1,)),
            dma((mps - 1,)),
            dma((mps - 1,)),
            dma((chunks, seqs - 1)),
            dma((chunks, seqs - 1)),
            dma((chunks,)),
            dma((chunks,)),
            dma((chunks,)),
            dma((chunks,)),
            dma((chunks,)),
            dma((chunks,)),
            dma((seqs - 1,)),
            dma((seqs - 1,)),
            dma,
            dma,
            dma((seqs - 1,)),
            dma((seqs - 1,)),
            dma((seqs - 1,)),
            dma((seqs - 1,)),
            dma((3,)),
        ],
        compiler_params=pltpu.CompilerParams(
            collective_id=0, has_side_effects=True, vmem_limit_bytes=62 * 1024 * 1024
        ),
        name="prefill_pages",
    )(
        embeds,
        image_feats,
        proj_w,
        kv_w,
        kv_cache,
        image_pos,
        bias,
        gain,
        page_owner,
        queries,
        new_kv,
        cache_lengths,
        prompt_lengths,
    )


def patch_kernel(index_ref, offset_ref, text, img, dest, out):
    rows = text.shape[0]
    first = offset_ref[pl.program_id(0)]
    spots = (dest[0, :1, :] - first.astype(F32)).astype(jnp.int32)
    hit = lax.broadcasted_iota(jnp.int32, (rows, dest.shape[2]), 0) == spots
    placed = jnp.dot(
        jnp.where(hit, 1.0, 0.0).astype(BF16), img[0], preferred_element_type=F32
    )
    out[...] = (text[...].astype(F32) + placed).astype(BF16)


def patch(index, offset, text, img, dest):
    seqs, rows_img, block_cols = img.shape
    block = text.shape[0] // seqs
    return pl.pallas_call(
        patch_kernel,
        out_shape=jax.ShapeDtypeStruct(text.shape, text.dtype),
        grid_spec=pltpu.PrefetchScalarGridSpec(
            num_scalar_prefetch=2,
            grid=(seqs,),
            in_specs=[
                pl.BlockSpec((block, block_cols), lambda b, index, offset: (b, 0)),
                pl.BlockSpec((1, rows_img, block_cols), lambda b, index, offset: (index[b], 0, 0)),
                pl.BlockSpec((1, 8, rows_img), lambda b, index, offset: (index[b], 0, 0)),
            ],
            out_specs=pl.BlockSpec((block, block_cols), lambda b, index, offset: (b, 0)),
        ),
        name="place_images",
    )(index, offset, text, img, dest)


def per_device(
    mesh_sizes,
    embeds,
    image_feats,
    image_pos,
    proj_w,
    proj_b,
    norm_gain,
    kv_w,
    prompt_lengths,
    page_owner,
    queries,
    kv_cache,
    new_kv,
    cache_lengths,
):
    groups, seqs, mps = mesh_sizes
    group_index = lax.axis_index("group")
    prefill_side = group_index == 0
    seq_index = lax.axis_index("seq")
    token_rows, width_local = embeds.shape
    prompt_len = token_rows * seqs // prompt_lengths.shape[0]
    page = token_rows // page_owner.shape[0]
    capacity = 2 * page_owner.shape[0] // seqs
    text, row_states, img, dest_all = prefill(
        mesh_sizes,
        prompt_len,
        embeds,
        image_feats,
        proj_w,
        kv_w,
        kv_cache,
        image_pos[None, :],
        proj_b[None, :],
        norm_gain[None, :],
        page_owner,
        queries,
        new_kv,
        cache_lengths[None, :],
        prompt_lengths,
    )
    order = jnp.arange(seqs, dtype=jnp.int32)
    index = jnp.where(prefill_side, seq_index, order)
    offset = jnp.where(prefill_side, order, seq_index) * (capacity * page)
    page_slots = patch(index, offset, text, img, dest_all)
    page_slots = page_slots.reshape(-1, page, text.shape[1])
    return (page_slots, row_states)


def solution(mesh):
    mesh_sizes = (mesh.shape["group"], mesh.shape["seq"], mesh.shape["mp"])
    in_specs = (
        P("seq", "mp"),
        P("seq", None),
        P("seq"),
        P("seq", "mp"),
        P("mp"),
        P("mp"),
        P("mp", None),
        P(),
        P("seq", None),
        P("seq", "mp"),
        P("seq", None, "mp"),
        P("seq", "mp"),
        P("seq"),
    )
    out_specs = (P(("group", "seq"), None, "mp"), P(("group", "seq"), "mp"))
    return jax.shard_map(
        functools.partial(per_device, mesh_sizes),
        mesh=mesh,
        in_specs=in_specs,
        out_specs=out_specs,
        check_vma=False,
    )
```

```python
import functools

import jax
import jax.numpy as jnp
from jax import lax
from jax.experimental import pallas as pl
from jax.experimental.pallas import tpu as pltpu
from jax.sharding import PartitionSpec as P

HEAD = 128
LANES = 128
TILE = 256
CORES = 2
MESH = pl.DeviceIdType.MESH
F32 = jnp.float32
BF16 = jnp.bfloat16


def ds(index, size):
    return pl.ds(pl.multiple_of(index * size, size), size)


def flip(index, distance):
    result = index
    bit = 1
    while bit <= distance:
        if distance & bit:
            result = result + bit - 2 * bit * lax.rem(index // bit, 2)
        bit *= 2
    return result


def spread_rows(row):
    return jnp.transpose(jnp.broadcast_to(row, (LANES, LANES)))


def prefill_kernel(
    groups,
    seqs,
    mps,
    prompt_len,
    embeds,
    image_feats,
    proj_w,
    kv_w,
    kv_cache,
    image_pos,
    bias,
    gain,
    page_owner,
    queries,
    new_kv,
    cache_lengths,
    prompt_lengths,
    slots_out,
    states_out,
    img_out,
    dest_out,
    gain_rows,
    bias_rows,
    sel,
    mask,
    dest,
    f_rows,
    feats,
    e_buf,
    w_buf,
    pw_buf,
    f_buf,
    acc1,
    s1,
    r1,
    acc2,
    s2,
    r2,
    sq_own,
    sq_recv,
    scale,
    outf,
    by_owner,
    arrived,
    kv_send,
    kv_recv,
    by_peer,
    p_own,
    p_send,
    p_recv,
    hid,
    i_scaled,
    i_acc,
    is1,
    ir1,
    is2,
    ir2,
    isq_own,
    isq_recv,
    ikv,
    q_rows,
    fresh,
    lengths,
    cache,
    a_scores,
    a_keys,
    a_values,
    a_limits,
    a_rows,
    attended,
    load_sem,
    cache_sem,
    w_sem,
    e_sem,
    pw_sem,
    fl_sem,
    send1,
    recv1,
    send2,
    recv2,
    send_sq,
    recv_sq,
    send_f,
    recv_f,
    send_fc,
    recv_fc,
    send_r,
    recv_r,
    send_h,
    recv_h,
    send_i1,
    recv_i1,
    send_i2,
    recv_i2,
    send_iq,
    recv_iq,
    send_z,
    recv_z,
    send_y,
    recv_y,
    send_k,
    recv_k,
    loc_sem,
    loc2_sem,
    send_iz,
    recv_iz,
    send_iy,
    recv_iy,
    send_if,
    recv_if,
    send_d,
    recv_d,
    misc_sem,
):
    g = lax.axis_index("group")
    s = lax.axis_index("seq")
    m = lax.axis_index("mp")
    chips = mps // CORES
    chip = m // CORES
    core = m % CORES
    partner = chip * CORES + (1 - core)
    peer = 1 - g
    blocks, feat_local, _ = w_buf.shape
    chunks = blocks // groups
    tokens = e_buf.shape[0]
    tiles = tokens // TILE
    steps = chunks * tiles
    col_tile = min(512, feat_local)
    col_tiles = feat_local // col_tile
    rows_img = hid.shape[0]
    half_rows = rows_img // groups
    core_rows = half_rows // CORES
    cols = chunks * LANES
    block_cols = cols * groups
    slots, pages = sel.shape
    page = tokens // pages
    capacity = slots // seqs
    width = feat_local * mps
    channels = feats.shape[2]
    block = slots * page // seqs
    own_cols = chips * LANES

    def remote(src, dst, send, recv, **where):
        return pltpu.make_async_remote_copy(
            src_ref=src,
            dst_ref=dst,
            send_sem=send,
            recv_sem=recv,
            device_id=where,
            device_id_type=MESH,
        )

    def seq_at(k):
        return lax.rem(s + k, seqs)

    def mp_at(k):
        return lax.rem(m + k, mps)

    def chip_at(k):
        return lax.rem(chip + k, chips) * CORES + core

    def e_copy(i):
        return pltpu.make_async_copy(embeds.at[ds(i, TILE), :], e_buf.at[ds(i, TILE), :], e_sem.at[i])

    def half_at(b):
        return lax.rem(g + b // chunks, groups)

    def columns(b):
        return half_at(b) * cols + b % chunks * LANES

    def w_copy(c, q, k):
        target = lax.rem(chip + k, chips) * CORES + (core if q == 0 else 1 - core)
        start = target * block_cols + columns(c)
        return pltpu.make_async_copy(
            kv_w.at[:, pl.ds(pl.multiple_of(start, LANES), LANES)],
            w_buf.at[c, :, (q * chips + k) * LANES : (q * chips + k + 1) * LANES],
            w_sem.at[c, q * chips + k],
        )

    f_load = pltpu.make_async_copy(image_feats.at[ds(g, half_rows), :], f_rows, load_sem.at[0])
    f_load.start()
    barrier = pltpu.get_barrier_semaphore()
    for k in range(1, seqs):
        pl.semaphore_signal(barrier, inc=1, device_id={"seq": seq_at(k)}, device_id_type=MESH)
    for k in range(1, mps):
        pl.semaphore_signal(barrier, inc=1, device_id={"mp": mp_at(k)}, device_id_type=MESH)
    pl.semaphore_signal(barrier, inc=1, device_id={"group": peer}, device_id_type=MESH)
    e_copy(0).start()
    for q in range(CORES):
        for k in range(chips):
            w_copy(0, q, k).start()
    for i in range(1, tiles):
        e_copy(i).start()
    cache_first = pltpu.make_async_copy(
        kv_cache.at[pl.ds(0, LANES // (queries.shape[1] // HEAD))], cache.at[0], cache_sem.at[0]
    )
    pw_copy = pltpu.make_async_copy(proj_w, pw_buf, pw_sem)

    def later_loads():
        pw_copy.start()
        for c in range(1, blocks):
            for q in range(CORES):
                for k in range(chips):
                    w_copy(c, q, k).start()

        @pl.when(g != 0)
        def _():
            cache_first.start()


    f_load.wait()
    for b in range(seqs):
        feats[b] = f_rows[:, b * channels : (b + 1) * channels]
    own_feats = pltpu.make_async_copy(feats.at[s], f_buf.at[0], fl_sem)
    own_feats.start()

    pl.semaphore_wait(barrier, seqs - 1 + mps - 1 + 1)

    def f_send(k):
        rows = ds(core, core_rows)
        return remote(
            feats.at[flip(s, k), rows, :],
            f_buf.at[k, rows, :],
            send_f.at[k - 1],
            recv_f.at[k - 1],
            seq=flip(s, k),
        )

    def f_share(k):
        rows = ds(core, core_rows)
        return remote(
            f_buf.at[k, rows, :],
            f_buf.at[k, rows, :],
            send_fc.at[k - 1],
            recv_fc.at[k - 1],
            mp=partner,
        )

    def d_send(k):
        return remote(dest, dest_out.at[s], send_d.at[k - 1], recv_d.at[k - 1], seq=seq_at(k))

    for k in range(1, seqs):
        f_send(k).start()

    gain_rows[...] = gain[...].astype(F32)
    biases = bias[...].astype(F32)
    for j in range(feat_local // LANES):
        t, within = divmod(j, col_tile // LANES)
        bias_rows[t : t + 1, within * LANES : (within + 1) * LANES] = biases[j : j + 1, :]

    prompt = (s * tokens) // prompt_len
    limit = prompt_lengths[prompt]
    base = s * tokens - prompt * prompt_len
    spots = image_pos[...] - s * tokens
    down = lax.broadcasted_iota(jnp.int32, (pages, LANES), 0)
    across = lax.broadcasted_iota(jnp.int32, (pages, LANES), 1)
    owner_across = jnp.broadcast_to(page_owner[...].astype(F32), (pages, LANES))
    owner_down = jnp.transpose(owner_across)
    rank = jnp.sum(
        jnp.where((owner_down == owner_across) & (down < across), 1.0, 0.0), axis=0, keepdims=True
    )
    slot = owner_across[:1] * capacity + rank
    slot_rows = lax.broadcasted_iota(jnp.int32, (slots, LANES), 0).astype(F32)
    sel[...] = jnp.where(slot_rows == slot, 1.0, 0.0).astype(BF16)
    page_bits = page.bit_length() - 1
    on_page = down == lax.shift_right_logical(spots, page_bits)
    image_slot = jnp.sum(jnp.where(on_page, spread_rows(slot), 0.0), axis=0, keepdims=True)
    image_row = image_slot * page + (spots & (page - 1)).astype(F32)
    dest[...] = jnp.broadcast_to(
        jnp.where(spots + base < limit, image_row, -1048576.0), dest.shape
    )
    dense = mask.shape[0]
    tall = lax.broadcasted_iota(jnp.int32, (dense, LANES), 0)
    image_block = jnp.where(tall == lax.shift_right_logical(spots, 7), 1.0, 0.0)
    image_lane = jnp.where(down == (spots & (LANES - 1)), 1.0, 0.0)
    images = lax.dot_general(
        image_block.astype(BF16),
        image_lane.astype(BF16),
        (((1,), (1,)), ((), ())),
        preferred_element_type=F32,
    )
    token = tall * LANES + lax.broadcasted_iota(jnp.int32, (dense, LANES), 1)
    mask[...] = jnp.where((token + base < limit) & (images < 0.5), 1.0, 0.0)
    for k in range(1, seqs):
        d_send(k).start()
    d_local = pltpu.make_async_copy(dest, dest_out.at[s], misc_sem.at[0])
    d_local.start()

    def first(n):
        return remote(s1.at[n], r1.at[n], send1.at[n], recv1.at[n], mp=partner)

    def second(n, k):
        return remote(
            s2.at[n, k - 1], r2.at[n, k - 1], send2.at[n, k - 1], recv2.at[n, k - 1], mp=chip_at(k)
        )

    def sq_send(k):
        return remote(sq_own, sq_recv.at[k - 1], send_sq.at[k - 1], recv_sq.at[k - 1], mp=mp_at(k))

    far_first = range(seqs - 1, 0, -1)

    levels = seqs.bit_length() - 1

    def sent_at(level):
        step_size = 2 << level
        return list(range(1 << level, seqs, step_size))

    def kept_at(level):
        step_size = 2 << level
        return list(range(0, seqs, step_size))

    def base_at(level):
        return seqs - (seqs >> level)

    def p_copy(level, t):
        span = pl.ds(base_at(level), len(sent_at(level)))
        at = ds(t, col_tile)
        return remote(
            p_send.at[span, :, at],
            p_recv.at[span, :, at],
            send_r.at[level, t],
            recv_r.at[level, t],
            seq=flip(s, 1 << level),
        )

    def scale_tile(i):
        e_copy(i).wait()

        def body(b, carry):
            rows = ds(i * (TILE // LANES) + b, LANES)
            total = jnp.zeros((LANES, LANES), F32)
            for j in range(feat_local // LANES):
                at = slice(j * LANES, (j + 1) * LANES)
                value = e_buf[rows, at].astype(F32)
                total = total + value * value
                e_buf[rows, at] = (value * gain_rows[j : j + 1, :]).astype(BF16)
            sq_own[pl.ds(i * (TILE // LANES) + b, 1), :] = jnp.sum(
                jnp.transpose(total), axis=0, keepdims=True
            )
            return carry

        lax.fori_loop(0, TILE // LANES, body, 0)

    def project():
        for k in range(1, seqs):
            f_share(k).wait()
        own_feats.wait()
        pw_copy.wait()
        spread = f_buf[...].reshape(seqs * half_rows, channels)

        def body(t, carry):
            at = ds(t, col_tile)
            out = jnp.dot(spread, pw_buf[:, at], preferred_element_type=F32)
            out = out.reshape(seqs, half_rows, col_tile)
            for slot_at, e in enumerate(sent_at(0)):
                p_send[slot_at, :, at] = out[e].astype(BF16)
            p_copy(0, t).start()
            for slot_at, e in enumerate(kept_at(0)):
                p_own[slot_at, :, at] = out[e]
            return carry

        lax.fori_loop(0, col_tiles, body, 0)

    def reduce_level(level):
        def body(t, carry):
            at = ds(t, col_tile)
            p_copy(level, t).wait()
            for index in range(len(kept_at(level))):
                total = p_own[index, :, at] + p_recv[base_at(level) + index, :, at].astype(F32)
                if index % 2 == 0:
                    p_own[index // 2, :, at] = total
                else:
                    p_send[base_at(level + 1) + index // 2, :, at] = total.astype(BF16)
            p_copy(level + 1, t).start()
            return carry

        lax.fori_loop(0, col_tiles, body, 0)

    def combine(p):
        c, i = p // tiles, lax.rem(p, tiles)
        first(p).wait()
        total = acc1[lax.rem(p, 2)] + r1[p].astype(F32)
        acc2[c, ds(i, TILE), :] = total[:, :LANES]
        for k in range(1, chips):
            s2[p, k - 1] = total[:, k * LANES : (k + 1) * LANES].astype(BF16)
            second(p, k).start()

    def multiply(n, c, i):
        part = jnp.dot(e_buf[ds(i, TILE), :], w_buf[c], preferred_element_type=F32)
        acc1[lax.rem(n, 2)] = part[:, :own_cols]
        s1[n] = part[:, own_cols:].astype(BF16)
        first(n).start()

    def text_chunk(c):
        for q in range(CORES):
            for k in range(chips):
                w_copy(c, q, k).wait()

        def body(i, carry):
            if c == 0:
                scale_tile(i)

                @pl.when(i == tiles // 2)
                def _():
                    later_loads()

            multiply(c * tiles + i, c, i)

            @pl.when(i > 0)
            def _():
                combine(c * tiles + i - 1)

            return carry

        lax.fori_loop(0, tiles, body, 0)
        if c == 0:
            for k in range(1, mps):
                sq_send(k).start()
        combine(c * tiles + tiles - 1)

    text_chunk(0)
    for k in range(1, seqs):
        f_send(k).wait_recv()
        f_share(k).start()
    project()

    for k in range(1, mps):
        sq_send(k).wait()
    squares = sq_own[...]
    for k in range(1, mps):
        squares = squares + sq_recv[k - 1]
    scale[...] = mask[...] * lax.rsqrt(squares / width + 1e-05)

    def z_send(c, k):
        return remote(
            by_owner.at[c, ds(flip(s, k), block), :],
            arrived.at[c, ds(s, block), :],
            send_z.at[c, k - 1],
            recv_z.at[c, k - 1],
            seq=flip(s, k),
        )

    def out_at(rows, half, c):
        at = pl.ds(pl.multiple_of(half * cols + c * LANES, LANES), LANES)
        return slots_out.at[rows, at]

    def y_send(src, rows, c):
        return remote(src, out_at(rows, g, c), send_y.at[c], recv_y.at[c], group=peer)

    def local(src, rows, c):
        return pltpu.make_async_copy(src, out_at(rows, g, c), loc_sem.at[c])

    everything = pl.ds(0, slots * page)

    def select(c, target):
        chosen = sel[...]
        for t in range(page):
            rows = acc2[c, pl.ds(t, pages, stride=page), :].astype(BF16)
            outf[pl.ds(t, slots, stride=page), :] = jnp.dot(
                chosen, rows, preferred_element_type=F32
            )
        target[c] = outf[...].astype(BF16)

    def k_send(c):
        return remote(kv_send.at[c], kv_recv.at[c], send_k.at[c], recv_k.at[c], group=peer)

    def local2(c):
        return pltpu.make_async_copy(
            by_peer.at[c], out_at(everything, 1 - g, c), loc2_sem.at[c]
        )

    def finish(c):
        def body(i, carry):
            n = c * tiles + i
            for k in range(1, chips):
                second(n, k).wait()
            for b in range(TILE // LANES):
                rows = pl.ds(pl.multiple_of(i * TILE + b * LANES, LANES), LANES)
                within = pl.ds(b * LANES, LANES)
                value = acc2[c, rows, :]
                for k in range(1, chips):
                    value = value + r2[n, k - 1, within, :].astype(F32)
                value = value * spread_rows(scale[pl.ds(i * (TILE // LANES) + b, 1), :])
                acc2[c, rows, :] = value
                kv_send[c, rows, :] = value.astype(BF16)
            return carry

        lax.fori_loop(0, tiles, body, 0)
        select(c, by_owner)

    def own_sends(c):
        mine = ds(s, block)

        @pl.when(g == 0)
        def _():
            y_send(by_owner.at[c, mine, :], mine, c).start()
            local(by_owner.at[c], everything, c).start()

        @pl.when(g != 0)
        def _():
            k_send(c).start()
            local(by_owner.at[c, mine, :], mine, c).start()

    def take_peer(c):
        k_send(c).wait_recv()
        acc2[c] = kv_recv[c].astype(F32)
        select(c, by_peer)
        local2(c).start()

    def forward(c, k):
        z_send(c, k).wait_recv()
        rows = ds(flip(s, k), block)

        @pl.when(g == 0)
        def _():
            y_send(arrived.at[c, rows, :], rows, c).start()

        @pl.when(g != 0)
        def _():
            local(arrived.at[c, rows, :], rows, c).start()

    heads = queries.shape[1] // HEAD
    kv_heads = kv_cache.shape[2] // (2 * HEAD)
    share = heads // kv_heads
    rows_dec = queries.shape[0]
    batch = LANES // heads

    def cache_copy(b):
        return pltpu.make_async_copy(
            kv_cache.at[ds(b, batch)], cache.at[lax.rem(b, 2)], cache_sem.at[lax.rem(b, 2)]
        )

    def attend_batch(b, carry):
        cache_copy(b).wait()

        @pl.when(b + 1 < rows_dec // batch)
        def _():
            cache_copy(b + 1).start()

        at = lax.rem(b, 2)
        for r in range(batch):
            span = slice(r * heads, (r + 1) * heads)
            query = q_rows[pl.ds(pl.multiple_of(b * LANES + r * heads, 8), heads), :].astype(BF16)
            new = fresh[pl.ds(b * batch + r, 1), :]
            a_limits[span, :] = jnp.broadcast_to(
                lengths[pl.ds(b * batch + r, 1), :], (heads, LANES)
            )
            for h in range(kv_heads):
                part = slice(r * heads + h * share, r * heads + (h + 1) * share)
                key = 2 * HEAD * h
                product = lax.dot_general(
                    query,
                    cache[at, r, :, key : key + HEAD],
                    (((1,), (1,)), ((), ())),
                    preferred_element_type=F32,
                )
                a_scores[part, :] = product[h * share : (h + 1) * share]
                a_keys[part, :] = jnp.broadcast_to(new[:, key : key + HEAD], (share, HEAD))
                a_values[part, :] = jnp.broadcast_to(
                    new[:, key + HEAD : key + 2 * HEAD], (share, HEAD)
                )
        lane = lax.broadcasted_iota(jnp.int32, (LANES, LANES), 1).astype(F32)
        scores = jnp.where(lane < a_limits[...], a_scores[...] * HEAD ** (-0.5), -1e30)
        own = jnp.sum(q_rows[ds(b, LANES), :] * a_keys[...], axis=1, keepdims=True) * HEAD ** (-0.5)
        top = jnp.maximum(jnp.max(scores, axis=1, keepdims=True), own)
        weights = jnp.exp(scores - top)
        own_weight = jnp.exp(own - top)
        total = jnp.sum(weights, axis=1, keepdims=True) + own_weight
        a_scores[...] = weights / total
        own_part = (own_weight / total).astype(BF16).astype(F32) * a_values[...]
        a_values[...] = own_part
        for r in range(batch):
            span = slice(r * heads, (r + 1) * heads)
            probs = a_scores[span, :].astype(BF16)
            for h in range(kv_heads):
                part = slice(r * heads + h * share, r * heads + (h + 1) * share)
                value = 2 * HEAD * h + HEAD
                product = jnp.dot(
                    probs, cache[at, r, :, value : value + HEAD], preferred_element_type=F32
                )
                a_rows[pl.ds(pl.multiple_of(b * LANES, LANES) + r * heads + h * share, share), :] = (
                    product[h * share : (h + 1) * share] + a_values[part, :]
                )
        return carry

    att_copy = pltpu.make_async_copy(attended, states_out, misc_sem.at[1])

    batches = rows_dec // batch

    def attend_start():
        for j in range(heads):
            q_rows[pl.ds(j, rows_dec, stride=heads), :] = queries[
                :, j * HEAD : (j + 1) * HEAD
            ].astype(F32)
        fresh[...] = new_kv[...].astype(F32)
        lengths[...] = spread_rows(cache_lengths[...].astype(F32))

    def attend(low, high):
        @pl.when(g != 0)
        def _():
            if low == 0:
                attend_start()
            lax.fori_loop(low, high, attend_batch, 0)
            if high == batches:
                for j in range(heads):
                    attended[:, j * HEAD : (j + 1) * HEAD] = a_rows[
                        pl.ds(j, rows_dec, stride=heads), :
                    ].astype(BF16)
                att_copy.start()

    finish(0)
    z_send(0, 1).start()
    for k in far_first:
        if k not in (1, seqs // 2):
            z_send(0, k).start()
    own_sends(0)
    for c in range(1, chunks):
        text_chunk(c)
    for level in range(levels - 1):
        reduce_level(level)
    z_send(0, seqs // 2).start()
    forward(0, 1)
    for c in range(1, chunks):
        finish(c)
        z_send(c, 1).start()
        own_sends(c)
    forward(0, seqs - 1)

    own_rows = ds(g, half_rows)

    def gelu_body(t, carry):
        at = ds(t, col_tile)
        p_copy(levels - 1, t).wait()
        total = p_own[0, :, at] + p_recv[base_at(levels - 1), :, at].astype(F32)
        total = total + bias_rows[pl.ds(t, 1), :]
        hid[own_rows, at] = (0.5 * total * (1.0 + lax.erf(total * 0.5**0.5))).astype(BF16)
        return carry

    lax.fori_loop(0, col_tiles, gelu_body, 0)
    h_send = remote(hid.at[own_rows, :], hid.at[own_rows, :], send_h, recv_h, group=peer)

    @pl.when(g != 0)
    def _():
        h_send.start()

    for c in range(1, chunks):
        for k in far_first:
            if k not in (1, seqs // 2):
                z_send(c, k).start()
        forward(c, 1)

    total = jnp.zeros((half_rows, LANES), F32)
    for j in range(feat_local // LANES):
        at = slice(j * LANES, (j + 1) * LANES)
        value = hid[own_rows, at].astype(F32)
        total = total + value * value
        i_scaled[:, at] = (value * gain_rows[j : j + 1, :]).astype(BF16)
    total = jnp.concatenate([total, jnp.zeros((LANES - half_rows, LANES), F32)], axis=0)
    isq_own[...] = jnp.broadcast_to(
        jnp.sum(jnp.transpose(total), axis=0, keepdims=True), isq_own.shape
    )

    def iq_send(k):
        return remote(isq_own, isq_recv.at[k - 1], send_iq.at[k - 1], recv_iq.at[k - 1], mp=mp_at(k))

    for k in range(1, mps):
        iq_send(k).start()
    for c in range(chunks, blocks):
        for q in range(CORES):
            for k in range(chips):
                w_copy(c, q, k).wait()
    for b in range(blocks):
        part = jnp.dot(i_scaled[...], w_buf[b], preferred_element_type=F32)
        i_acc[b] = part[:, :own_cols]
        is1[b] = part[:, own_cols:].astype(BF16)
    i_first = remote(is1, ir1, send_i1, recv_i1, mp=partner)
    i_first.start()

    def i_second(k):
        return remote(
            is2.at[k - 1], ir2.at[k - 1], send_i2.at[k - 1], recv_i2.at[k - 1], mp=chip_at(k)
        )

    i_first.wait()
    for b in range(blocks):
        total = i_acc[b] + ir1[b].astype(F32)
        i_acc[b] = total
        for k in range(1, chips):
            is2[k - 1, b] = total[:, k * LANES : (k + 1) * LANES].astype(BF16)
    for k in range(1, chips):
        i_second(k).start()
    for k in range(1, mps):
        iq_send(k).wait()
    squares = isq_own[...]
    for k in range(1, mps):
        squares = squares + isq_recv[k - 1]
    i_scale = spread_rows(lax.rsqrt(squares / width + 1e-05)[:1])[:half_rows]
    for k in range(1, chips):
        i_second(k).wait()
    for b in range(blocks):
        value = i_acc[b, :, :LANES]
        for k in range(1, chips):
            value = value + ir2[k - 1, b].astype(F32)
        ikv[:, pl.ds(pl.multiple_of(columns(b), LANES), LANES)] = (value * i_scale).astype(BF16)

    def img_at(index, half):
        return img_out.at[index, ds(half, half_rows), :]

    def iz_send(k):
        return remote(ikv, img_at(s, g), send_iz.at[k - 1], recv_iz.at[k - 1], seq=flip(s, k))

    iy_send = remote(ikv, img_at(s, g), send_iy, recv_iy, group=peer)
    for k in far_first:
        iz_send(k).start()
    iy_send.start()
    i_local = pltpu.make_async_copy(ikv, img_at(s, g), misc_sem.at[2])
    i_local.start()
    for c in range(1, chunks):
        z_send(c, seqs // 2).start()
    attend(0, batches)
    for k in far_first:
        if k not in (1, seqs - 1):
            forward(0, k)

    def if_send(k):
        src = flip(s, k)
        return remote(
            img_at(src, 0), img_at(src, 0), send_if.at[k - 1], recv_if.at[k - 1], group=peer
        )


    @pl.when(g == 0)
    def _():
        for c in range(chunks):
            take_peer(c)

    for k in far_first:
        iz_send(k).wait_recv()

        @pl.when(g == 0)
        def _():
            if_send(k).start()

    hid_copy = pltpu.make_async_copy(hid, states_out, misc_sem.at[1])

    @pl.when(g == 0)
    def _():
        h_send.wait_recv()
        hid_copy.start()

    for c in range(1, chunks):
        for k in far_first:
            if k != 1:
                forward(c, k)

    for c in range(chunks):
        for k in range(1, seqs):
            z_send(c, k).wait_send()
        local(by_owner.at[c], everything, c).wait()

        @pl.when(g == 0)
        def _():
            y_send(by_owner.at[c], everything, c).wait_send()
            local2(c).wait()

        @pl.when(g != 0)
        def _():
            y_send(by_owner.at[c], everything, c).wait_recv()
            k_send(c).wait_send()

    for k in range(1, seqs):
        f_send(k).wait_send()
        d_send(k).wait()
        iz_send(k).wait_send()

        @pl.when(g == 0)
        def _():
            if_send(k).wait_send()

        @pl.when(g != 0)
        def _():
            if_send(k).wait_recv()

    @pl.when(g != 0)
    def _():
        h_send.wait_send()

    iy_send.wait()
    i_local.wait()
    d_local.wait()
    hid_copy.wait()


def prefill(
    mesh_sizes,
    prompt_len,
    embeds,
    image_feats,
    proj_w,
    kv_w,
    kv_cache,
    image_pos,
    bias,
    gain,
    page_owner,
    queries,
    new_kv,
    cache_lengths,
    prompt_lengths,
):
    groups, seqs, mps = mesh_sizes
    chips = mps // CORES
    tokens, feat_local = embeds.shape
    tiles = tokens // TILE
    rows_img, all_channels = image_feats.shape
    half_rows = rows_img // groups
    channels = proj_w.shape[0]
    block_cols = kv_w.shape[1] // mps
    cols = block_cols // groups
    chunks = cols // LANES
    blocks = groups * chunks
    steps = chunks * tiles
    col_tile = min(512, feat_local)
    col_tiles = feat_local // col_tile
    levels = seqs.bit_length() - 1
    pages = page_owner.shape[1]
    page = tokens // pages
    slots = seqs * (2 * pages // seqs)
    rows_dec = queries.shape[0]
    heads = queries.shape[1] // HEAD
    batch = LANES // heads
    dma = pltpu.SemaphoreType.DMA
    vmem = pl.BlockSpec(memory_space=pltpu.VMEM)
    anywhere = pl.BlockSpec(memory_space=pl.ANY)
    dense = tokens // LANES
    return pl.pallas_call(
        functools.partial(prefill_kernel, groups, seqs, mps, prompt_len),
        out_shape=(
            jax.ShapeDtypeStruct((slots * page, block_cols), BF16),
            jax.ShapeDtypeStruct((rows_img, feat_local), BF16),
            jax.ShapeDtypeStruct((seqs, rows_img, block_cols), BF16),
            jax.ShapeDtypeStruct((seqs, 8, rows_img), F32),
        ),
        in_specs=[anywhere] * 5 + [vmem] * 7 + [pl.BlockSpec(memory_space=pltpu.SMEM)],
        out_specs=(anywhere,) * 4,
        scratch_shapes=[
            pltpu.VMEM((feat_local // LANES, LANES), F32),
            pltpu.VMEM((col_tiles, col_tile), F32),
            pltpu.VMEM((slots, pages), BF16),
            pltpu.VMEM((dense, LANES), F32),
            pltpu.VMEM((8, rows_img), F32),
            pltpu.VMEM((half_rows, all_channels), BF16),
            pltpu.VMEM((seqs, half_rows, channels), BF16),
            pltpu.VMEM((tokens, feat_local), BF16),
            pltpu.VMEM((blocks, feat_local, mps * LANES), BF16),
            pltpu.VMEM((channels, feat_local), BF16),
            pltpu.VMEM((seqs, half_rows, channels), BF16),
            pltpu.VMEM((2, TILE, chips * LANES), F32),
            pltpu.VMEM((steps, TILE, chips * LANES), BF16),
            pltpu.VMEM((steps, TILE, chips * LANES), BF16),
            pltpu.VMEM((chunks, tokens, LANES), F32),
            pltpu.VMEM((steps, chips - 1, TILE, LANES), BF16),
            pltpu.VMEM((steps, chips - 1, TILE, LANES), BF16),
            pltpu.VMEM((dense, LANES), F32),
            pltpu.VMEM((mps - 1, dense, LANES), F32),
            pltpu.VMEM((dense, LANES), F32),
            pltpu.VMEM((slots * page, LANES), F32),
            pltpu.VMEM((chunks, slots * page, LANES), BF16),
            pltpu.VMEM((chunks, slots * page, LANES), BF16),
            pltpu.VMEM((chunks, tokens, LANES), BF16),
            pltpu.VMEM((chunks, tokens, LANES), BF16),
            pltpu.VMEM((chunks, slots * page, LANES), BF16),
            pltpu.VMEM((seqs // 2, half_rows, feat_local), F32),
            pltpu.VMEM((seqs - 1, half_rows, feat_local), BF16),
            pltpu.VMEM((seqs - 1, half_rows, feat_local), BF16),
            pltpu.VMEM((rows_img, feat_local), BF16),
            pltpu.VMEM((half_rows, feat_local), BF16),
            pltpu.VMEM((blocks, half_rows, chips * LANES), F32),
            pltpu.VMEM((blocks, half_rows, chips * LANES), BF16),
            pltpu.VMEM((blocks, half_rows, chips * LANES), BF16),
            pltpu.VMEM((chips - 1, blocks, half_rows, LANES), BF16),
            pltpu.VMEM((chips - 1, blocks, half_rows, LANES), BF16),
            pltpu.VMEM((8, LANES), F32),
            pltpu.VMEM((mps - 1, 8, LANES), F32),
            pltpu.VMEM((half_rows, block_cols), BF16),
            pltpu.VMEM((rows_dec * heads, HEAD), F32),
            pltpu.VMEM(new_kv.shape, F32),
            pltpu.VMEM((rows_dec, LANES), F32),
            pltpu.VMEM((2, batch) + kv_cache.shape[1:], BF16),
            pltpu.VMEM((LANES, LANES), F32),
            pltpu.VMEM((LANES, LANES), F32),
            pltpu.VMEM((LANES, LANES), F32),
            pltpu.VMEM((LANES, LANES), F32),
            pltpu.VMEM((rows_dec * heads, HEAD), F32),
            pltpu.VMEM(queries.shape, BF16),
            dma((1,)),
            dma((2,)),
            dma((blocks, mps)),
            dma((tiles,)),
            dma,
            dma,
            dma((steps,)),
            dma((steps,)),
            dma((steps, chips - 1)),
            dma((steps, chips - 1)),
            dma((mps - 1,)),
            dma((mps - 1,)),
            dma((seqs - 1,)),
            dma((seqs - 1,)),
            dma((seqs - 1,)),
            dma((seqs - 1,)),
            dma((levels, col_tiles)),
            dma((levels, col_tiles)),
            dma,
            dma,
            dma,
            dma,
            dma((chips - 1,)),
            dma((chips - 1,)),
            dma((mps - 1,)),
            dma((mps - 1,)),
            dma((chunks, seqs - 1)),
            dma((chunks, seqs - 1)),
            dma((chunks,)),
            dma((chunks,)),
            dma((chunks,)),
            dma((chunks,)),
            dma((chunks,)),
            dma((chunks,)),
            dma((seqs - 1,)),
            dma((seqs - 1,)),
            dma,
            dma,
            dma((seqs - 1,)),
            dma((seqs - 1,)),
            dma((seqs - 1,)),
            dma((seqs - 1,)),
            dma((3,)),
        ],
        compiler_params=pltpu.CompilerParams(
            collective_id=0, has_side_effects=True, vmem_limit_bytes=62 * 1024 * 1024
        ),
        name="prefill_pages",
    )(
        embeds,
        image_feats,
        proj_w,
        kv_w,
        kv_cache,
        image_pos,
        bias,
        gain,
        page_owner,
        queries,
        new_kv,
        cache_lengths,
        prompt_lengths,
    )


def place_kernel(index, offset, text, img, dest, states, out, states_out, rows, state_rows, sems):
    parts = index.shape[0]
    block = text.shape[0] // parts

    def load(b):
        span = pl.ds(b * block, block)
        return pltpu.make_async_copy(text.at[span, :], rows.at[span, :], sems.at[0, b])

    def store(b):
        span = pl.ds(b * block, block)
        return pltpu.make_async_copy(rows.at[span, :], out.at[span, :], sems.at[1, b])

    state_load = pltpu.make_async_copy(states, state_rows, sems.at[2, 0])
    state_store = pltpu.make_async_copy(state_rows, states_out, sems.at[2, 1])
    for b in range(parts):
        load(b).start()
    state_load.start()
    for b in range(parts):
        spots = dest[index[b]][:1].astype(jnp.int32) - offset[b]
        hit = lax.broadcasted_iota(jnp.int32, (block, dest.shape[2]), 0) == spots
        placed = jnp.dot(
            jnp.where(hit, 1.0, 0.0).astype(BF16), img[index[b]], preferred_element_type=F32
        )
        load(b).wait()
        span = pl.ds(b * block, block)
        rows[span, :] = rows[span, :] + placed.astype(BF16)
        store(b).start()
        if b == 0:
            state_load.wait()
            state_store.start()
    for b in range(parts):
        store(b).wait()
    state_store.wait()


def place(index, offset, text, img, dest, states):
    parts = index.shape[0]
    smem = pl.BlockSpec(memory_space=pltpu.SMEM)
    vmem = pl.BlockSpec(memory_space=pltpu.VMEM)
    anywhere = pl.BlockSpec(memory_space=pl.ANY)
    return pl.pallas_call(
        place_kernel,
        out_shape=(
            jax.ShapeDtypeStruct(text.shape, text.dtype),
            jax.ShapeDtypeStruct(states.shape, states.dtype),
        ),
        in_specs=[smem, smem, anywhere, vmem, vmem, anywhere],
        out_specs=(anywhere, anywhere),
        scratch_shapes=[
            pltpu.VMEM(text.shape, text.dtype),
            pltpu.VMEM(states.shape, states.dtype),
            pltpu.SemaphoreType.DMA((3, max(parts, 2))),
        ],
        name="place_images",
    )(index, offset, text, img, dest, states)


def per_device(
    mesh_sizes,
    embeds,
    image_feats,
    image_pos,
    proj_w,
    proj_b,
    norm_gain,
    kv_w,
    prompt_lengths,
    page_owner,
    queries,
    kv_cache,
    new_kv,
    cache_lengths,
):
    groups, seqs, mps = mesh_sizes
    group_index = lax.axis_index("group")
    prefill_side = group_index == 0
    seq_index = lax.axis_index("seq")
    token_rows, width_local = embeds.shape
    prompt_len = token_rows * seqs // prompt_lengths.shape[0]
    page = token_rows // page_owner.shape[0]
    capacity = 2 * page_owner.shape[0] // seqs
    text, row_states, img, dest_all = prefill(
        mesh_sizes,
        prompt_len,
        embeds,
        image_feats,
        proj_w,
        kv_w,
        kv_cache,
        image_pos[None, :],
        proj_b.reshape(-1, LANES),
        norm_gain.reshape(-1, LANES),
        page_owner.reshape(1, -1),
        queries,
        new_kv,
        cache_lengths[None, :],
        prompt_lengths,
    )
    parts = max(1, 8 // seqs)
    order = jnp.arange(seqs * parts, dtype=jnp.int32)
    source, part = order // parts, order % parts
    index = jnp.where(prefill_side, seq_index, source)
    offset = jnp.where(prefill_side, source, seq_index) * (capacity * page)
    offset = offset + part * (capacity * page // parts)
    page_slots, row_states = place(index, offset, text, img, dest_all, row_states)
    page_slots = page_slots.reshape(-1, page, text.shape[1])
    return (page_slots, row_states)


def solution(mesh):
    mesh_sizes = (mesh.shape["group"], mesh.shape["seq"], mesh.shape["mp"])
    in_specs = (
        P("seq", "mp"),
        P("seq", None),
        P("seq"),
        P("seq", "mp"),
        P("mp"),
        P("mp"),
        P("mp", None),
        P(),
        P("seq", None),
        P("seq", "mp"),
        P("seq", None, "mp"),
        P("seq", "mp"),
        P("seq"),
    )
    out_specs = (P(("group", "seq"), None, "mp"), P(("group", "seq"), "mp"))
    return jax.shard_map(
        functools.partial(per_device, mesh_sizes),
        mesh=mesh,
        in_specs=in_specs,
        out_specs=out_specs,
        check_vma=False,
    )
```

```python
import functools

import jax
import jax.numpy as jnp
from jax import lax
from jax.experimental import pallas as pl
from jax.experimental.pallas import tpu as pltpu
from jax.sharding import PartitionSpec as P

HEAD = 128
LANES = 128
TILE = 256
CORES = 2
MESH = pl.DeviceIdType.MESH
F32 = jnp.float32
BF16 = jnp.bfloat16


def ds(index, size):
    return pl.ds(pl.multiple_of(index * size, size), size)


def flip(index, distance):
    result = index
    bit = 1
    while bit <= distance:
        if distance & bit:
            result = result + bit - 2 * bit * lax.rem(index // bit, 2)
        bit *= 2
    return result


def spread_rows(row):
    return jnp.transpose(jnp.broadcast_to(row, (LANES, LANES)))


def prefill_kernel(
    groups,
    seqs,
    mps,
    prompt_len,
    embeds,
    image_feats,
    proj_w,
    kv_w,
    kv_cache,
    image_pos,
    bias,
    gain,
    page_owner,
    queries,
    new_kv,
    cache_lengths,
    prompt_lengths,
    slots_out,
    states_out,
    img_out,
    dest_out,
    gain_rows,
    bias_rows,
    sel,
    mask,
    dest,
    f_rows,
    feats,
    e_buf,
    w_buf,
    pw_buf,
    f_buf,
    acc1,
    s1,
    r1,
    acc2,
    s2,
    r2,
    sq_own,
    sq_recv,
    scale,
    outf,
    by_owner,
    arrived,
    kv_send,
    kv_recv,
    by_peer,
    p_own,
    p_send,
    p_recv,
    hid,
    i_scaled,
    i_acc,
    is1,
    ir1,
    is2,
    ir2,
    isq_own,
    isq_recv,
    ikv,
    q_rows,
    fresh,
    lengths,
    cache,
    a_scores,
    a_keys,
    a_values,
    a_limits,
    a_rows,
    attended,
    load_sem,
    cache_sem,
    w_sem,
    e_sem,
    pw_sem,
    fl_sem,
    send1,
    recv1,
    send2,
    recv2,
    send_sq,
    recv_sq,
    send_f,
    recv_f,
    send_fc,
    recv_fc,
    send_r,
    recv_r,
    send_h,
    recv_h,
    send_i1,
    recv_i1,
    send_i2,
    recv_i2,
    send_iq,
    recv_iq,
    send_z,
    recv_z,
    send_y,
    recv_y,
    send_k,
    recv_k,
    loc_sem,
    loc2_sem,
    send_iz,
    recv_iz,
    send_iy,
    recv_iy,
    send_if,
    recv_if,
    send_d,
    recv_d,
    misc_sem,
):
    g = lax.axis_index("group")
    s = lax.axis_index("seq")
    m = lax.axis_index("mp")
    chips = mps // CORES
    chip = m // CORES
    core = m % CORES
    partner = chip * CORES + (1 - core)
    peer = 1 - g
    blocks, feat_local, _ = w_buf.shape
    chunks = blocks // groups
    tokens = e_buf.shape[0]
    tiles = tokens // TILE
    steps = chunks * tiles
    col_tile = min(512, feat_local)
    col_tiles = feat_local // col_tile
    rows_img = hid.shape[0]
    half_rows = rows_img // groups
    core_rows = half_rows // CORES
    cols = chunks * LANES
    block_cols = cols * groups
    slots, pages = sel.shape
    page = tokens // pages
    capacity = slots // seqs
    width = feat_local * mps
    channels = feats.shape[2]
    block = slots * page // seqs
    own_cols = chips * LANES

    def remote(src, dst, send, recv, **where):
        return pltpu.make_async_remote_copy(
            src_ref=src,
            dst_ref=dst,
            send_sem=send,
            recv_sem=recv,
            device_id=where,
            device_id_type=MESH,
        )

    def seq_at(k):
        return lax.rem(s + k, seqs)

    def mp_at(k):
        return lax.rem(m + k, mps)

    def chip_at(k):
        return lax.rem(chip + k, chips) * CORES + core

    def e_copy(i):
        return pltpu.make_async_copy(embeds.at[ds(i, TILE), :], e_buf.at[ds(i, TILE), :], e_sem.at[i])

    def half_at(b):
        return lax.rem(g + b // chunks, groups)

    def columns(b):
        return half_at(b) * cols + b % chunks * LANES

    def w_copy(c, q, k):
        target = lax.rem(chip + k, chips) * CORES + (core if q == 0 else 1 - core)
        start = target * block_cols + columns(c)
        return pltpu.make_async_copy(
            kv_w.at[:, pl.ds(pl.multiple_of(start, LANES), LANES)],
            w_buf.at[c, :, (q * chips + k) * LANES : (q * chips + k + 1) * LANES],
            w_sem.at[c, q * chips + k],
        )

    f_load = pltpu.make_async_copy(image_feats.at[ds(g, half_rows), :], f_rows, load_sem.at[0])
    f_load.start()
    barrier = pltpu.get_barrier_semaphore()
    for k in range(1, seqs):
        pl.semaphore_signal(barrier, inc=1, device_id={"seq": seq_at(k)}, device_id_type=MESH)
    for k in range(1, mps):
        pl.semaphore_signal(barrier, inc=1, device_id={"mp": mp_at(k)}, device_id_type=MESH)
    pl.semaphore_signal(barrier, inc=1, device_id={"group": peer}, device_id_type=MESH)
    e_copy(0).start()
    for q in range(CORES):
        for k in range(chips):
            w_copy(0, q, k).start()
    for i in range(1, tiles):
        e_copy(i).start()
    cache_first = pltpu.make_async_copy(
        kv_cache.at[pl.ds(0, LANES // (queries.shape[1] // HEAD))], cache.at[0], cache_sem.at[0]
    )
    pw_copy = pltpu.make_async_copy(proj_w, pw_buf, pw_sem)

    def later_loads():
        pw_copy.start()
        for c in range(1, blocks):
            for q in range(CORES):
                for k in range(chips):
                    w_copy(c, q, k).start()

        @pl.when(g != 0)
        def _():
            cache_first.start()


    f_load.wait()
    for b in range(seqs):
        feats[b] = f_rows[:, b * channels : (b + 1) * channels]
    own_feats = pltpu.make_async_copy(feats.at[s], f_buf.at[0], fl_sem)
    own_feats.start()

    pl.semaphore_wait(barrier, seqs - 1 + mps - 1 + 1)

    def f_send(k):
        rows = ds(core, core_rows)
        return remote(
            feats.at[flip(s, k), rows, :],
            f_buf.at[k, rows, :],
            send_f.at[k - 1],
            recv_f.at[k - 1],
            seq=flip(s, k),
        )

    def f_share(k):
        rows = ds(core, core_rows)
        return remote(
            f_buf.at[k, rows, :],
            f_buf.at[k, rows, :],
            send_fc.at[k - 1],
            recv_fc.at[k - 1],
            mp=partner,
        )

    def d_send(k):
        return remote(dest, dest_out.at[s], send_d.at[k - 1], recv_d.at[k - 1], seq=seq_at(k))

    for k in range(1, seqs):
        f_send(k).start()

    gain_rows[...] = gain[...].astype(F32)
    biases = bias[...].astype(F32)
    for j in range(feat_local // LANES):
        t, within = divmod(j, col_tile // LANES)
        bias_rows[t : t + 1, within * LANES : (within + 1) * LANES] = biases[j : j + 1, :]

    prompt = (s * tokens) // prompt_len
    limit = prompt_lengths[prompt]
    base = s * tokens - prompt * prompt_len
    spots = image_pos[...] - s * tokens
    down = lax.broadcasted_iota(jnp.int32, (pages, LANES), 0)
    across = lax.broadcasted_iota(jnp.int32, (pages, LANES), 1)
    owner_across = jnp.broadcast_to(page_owner[...].astype(F32), (pages, LANES))
    owner_down = jnp.transpose(owner_across)
    rank = jnp.sum(
        jnp.where((owner_down == owner_across) & (down < across), 1.0, 0.0), axis=0, keepdims=True
    )
    slot = owner_across[:1] * capacity + rank
    slot_rows = lax.broadcasted_iota(jnp.int32, (slots, LANES), 0).astype(F32)
    sel[...] = jnp.where(slot_rows == slot, 1.0, 0.0).astype(BF16)
    page_bits = page.bit_length() - 1
    on_page = down == lax.shift_right_logical(spots, page_bits)
    image_slot = jnp.sum(jnp.where(on_page, spread_rows(slot), 0.0), axis=0, keepdims=True)
    image_row = image_slot * page + (spots & (page - 1)).astype(F32)
    dest[...] = jnp.broadcast_to(
        jnp.where(spots + base < limit, image_row, -1048576.0), dest.shape
    )
    dense = mask.shape[0]
    tall = lax.broadcasted_iota(jnp.int32, (dense, LANES), 0)
    image_block = jnp.where(tall == lax.shift_right_logical(spots, 7), 1.0, 0.0)
    image_lane = jnp.where(down == (spots & (LANES - 1)), 1.0, 0.0)
    images = lax.dot_general(
        image_block.astype(BF16),
        image_lane.astype(BF16),
        (((1,), (1,)), ((), ())),
        preferred_element_type=F32,
    )
    token = tall * LANES + lax.broadcasted_iota(jnp.int32, (dense, LANES), 1)
    mask[...] = jnp.where((token + base < limit) & (images < 0.5), 1.0, 0.0)
    for k in range(1, seqs):
        d_send(k).start()
    d_local = pltpu.make_async_copy(dest, dest_out.at[s], misc_sem.at[0])
    d_local.start()

    def first(n):
        return remote(s1.at[n], r1.at[n], send1.at[n], recv1.at[n], mp=partner)

    def second(n, k):
        return remote(
            s2.at[n, k - 1], r2.at[n, k - 1], send2.at[n, k - 1], recv2.at[n, k - 1], mp=chip_at(k)
        )

    def sq_send(k):
        return remote(sq_own, sq_recv.at[k - 1], send_sq.at[k - 1], recv_sq.at[k - 1], mp=mp_at(k))

    far_first = range(seqs - 1, 0, -1)
    outer = lax.rem(s, 2) == lax.rem(s // 2, 2)

    levels = seqs.bit_length() - 1

    def sent_at(level):
        step_size = 2 << level
        return list(range(1 << level, seqs, step_size))

    def kept_at(level):
        step_size = 2 << level
        return list(range(0, seqs, step_size))

    def base_at(level):
        return seqs - (seqs >> level)

    def p_copy(level, t):
        span = pl.ds(base_at(level), len(sent_at(level)))
        at = ds(t, col_tile)
        return remote(
            p_send.at[span, :, at],
            p_recv.at[span, :, at],
            send_r.at[level, t],
            recv_r.at[level, t],
            seq=flip(s, 1 << level),
        )

    def scale_tile(i):
        e_copy(i).wait()

        def body(b, carry):
            rows = ds(i * (TILE // LANES) + b, LANES)
            total = jnp.zeros((LANES, LANES), F32)
            for j in range(feat_local // LANES):
                at = slice(j * LANES, (j + 1) * LANES)
                value = e_buf[rows, at].astype(F32)
                total = total + value * value
                e_buf[rows, at] = (value * gain_rows[j : j + 1, :]).astype(BF16)
            sq_own[pl.ds(i * (TILE // LANES) + b, 1), :] = jnp.sum(
                jnp.transpose(total), axis=0, keepdims=True
            )
            return carry

        lax.fori_loop(0, TILE // LANES, body, 0)

    def project():
        for k in range(1, seqs):
            f_share(k).wait()
        own_feats.wait()
        pw_copy.wait()
        spread = f_buf[...].reshape(seqs * half_rows, channels)

        def body(t, carry):
            at = ds(t, col_tile)
            out = jnp.dot(spread, pw_buf[:, at], preferred_element_type=F32)
            out = out.reshape(seqs, half_rows, col_tile)
            for slot_at, e in enumerate(sent_at(0)):
                p_send[slot_at, :, at] = out[e].astype(BF16)
            p_copy(0, t).start()
            for slot_at, e in enumerate(kept_at(0)):
                p_own[slot_at, :, at] = out[e]
            return carry

        lax.fori_loop(0, col_tiles, body, 0)

    def reduce_level(level):
        def body(t, carry):
            at = ds(t, col_tile)
            p_copy(level, t).wait()
            for index in range(len(kept_at(level))):
                total = p_own[index, :, at] + p_recv[base_at(level) + index, :, at].astype(F32)
                if index % 2 == 0:
                    p_own[index // 2, :, at] = total
                else:
                    p_send[base_at(level + 1) + index // 2, :, at] = total.astype(BF16)
            p_copy(level + 1, t).start()
            return carry

        lax.fori_loop(0, col_tiles, body, 0)

    def combine(p):
        c, i = p // tiles, lax.rem(p, tiles)
        first(p).wait()
        total = acc1[lax.rem(p, 2)] + r1[p].astype(F32)
        acc2[c, ds(i, TILE), :] = total[:, :LANES]
        for k in range(1, chips):
            s2[p, k - 1] = total[:, k * LANES : (k + 1) * LANES].astype(BF16)
            second(p, k).start()

    def multiply(n, c, i):
        part = jnp.dot(e_buf[ds(i, TILE), :], w_buf[c], preferred_element_type=F32)
        acc1[lax.rem(n, 2)] = part[:, :own_cols]
        s1[n] = part[:, own_cols:].astype(BF16)
        first(n).start()

    def text_chunk(c):
        for q in range(CORES):
            for k in range(chips):
                w_copy(c, q, k).wait()

        def body(i, carry):
            if c == 0:
                scale_tile(i)

                @pl.when(i == tiles // 2)
                def _():
                    later_loads()

            multiply(c * tiles + i, c, i)

            @pl.when(i > 0)
            def _():
                combine(c * tiles + i - 1)

            return carry

        lax.fori_loop(0, tiles, body, 0)
        if c == 0:
            for k in range(1, mps):
                sq_send(k).start()
        combine(c * tiles + tiles - 1)

    text_chunk(0)
    for k in range(1, seqs):
        f_send(k).wait_recv()
        f_share(k).start()
    project()

    for k in range(1, mps):
        sq_send(k).wait()
    squares = sq_own[...]
    for k in range(1, mps):
        squares = squares + sq_recv[k - 1]
    scale[...] = mask[...] * lax.rsqrt(squares / width + 1e-05)

    halves = 2
    piece = block // halves

    def z_piece(c, k, h):
        return remote(
            by_owner.at[c, ds(flip(s, k) * halves + h, piece), :],
            arrived.at[c, ds(s * halves + h, piece), :],
            send_z.at[c, (k - 1) * halves + h],
            recv_z.at[c, (k - 1) * halves + h],
            seq=flip(s, k),
        )

    def z_start(c, k):
        for h in range(halves):
            z_piece(c, k, h).start()

    def out_at(rows, half, c):
        at = pl.ds(pl.multiple_of(half * cols + c * LANES, LANES), LANES)
        return slots_out.at[rows, at]

    def y_send(src, rows, c):
        return remote(src, out_at(rows, g, c), send_y.at[c], recv_y.at[c], group=peer)

    def local(src, rows, c):
        return pltpu.make_async_copy(src, out_at(rows, g, c), loc_sem.at[c])

    everything = pl.ds(0, slots * page)

    def select(c, target):
        chosen = sel[...]
        for t in range(page):
            rows = acc2[c, pl.ds(t, pages, stride=page), :].astype(BF16)
            outf[pl.ds(t, slots, stride=page), :] = jnp.dot(
                chosen, rows, preferred_element_type=F32
            )
        target[c] = outf[...].astype(BF16)

    def k_send(c):
        return remote(kv_send.at[c], kv_recv.at[c], send_k.at[c], recv_k.at[c], group=peer)

    def local2(c):
        return pltpu.make_async_copy(
            by_peer.at[c], out_at(everything, 1 - g, c), loc2_sem.at[c]
        )

    def finish(c):
        def body(i, carry):
            n = c * tiles + i
            for k in range(1, chips):
                second(n, k).wait()
            for b in range(TILE // LANES):
                rows = pl.ds(pl.multiple_of(i * TILE + b * LANES, LANES), LANES)
                within = pl.ds(b * LANES, LANES)
                value = acc2[c, rows, :]
                for k in range(1, chips):
                    value = value + r2[n, k - 1, within, :].astype(F32)
                value = value * spread_rows(scale[pl.ds(i * (TILE // LANES) + b, 1), :])
                acc2[c, rows, :] = value
                kv_send[c, rows, :] = value.astype(BF16)
            return carry

        lax.fori_loop(0, tiles, body, 0)
        select(c, by_owner)

    def own_sends(c):
        mine = ds(s, block)

        @pl.when(g == 0)
        def _():
            y_send(by_owner.at[c, mine, :], mine, c).start()
            local(by_owner.at[c], everything, c).start()

        @pl.when(g != 0)
        def _():
            k_send(c).start()
            local(by_owner.at[c, mine, :], mine, c).start()

    def take_peer(c):
        k_send(c).wait_recv()
        acc2[c] = kv_recv[c].astype(F32)
        select(c, by_peer)
        local2(c).start()

    def forward(c, k):
        for h in range(halves):
            z_piece(c, k, h).wait_recv()
            rows = ds(flip(s, k) * halves + h, piece)

            @pl.when(g == 0)
            def _():
                y_send(arrived.at[c, rows, :], rows, c).start()

            @pl.when(g != 0)
            def _():
                local(arrived.at[c, rows, :], rows, c).start()

    heads = queries.shape[1] // HEAD
    kv_heads = kv_cache.shape[2] // (2 * HEAD)
    share = heads // kv_heads
    rows_dec = queries.shape[0]
    batch = LANES // heads

    def cache_copy(b):
        return pltpu.make_async_copy(
            kv_cache.at[ds(b, batch)], cache.at[lax.rem(b, 2)], cache_sem.at[lax.rem(b, 2)]
        )

    def attend_batch(b, carry):
        cache_copy(b).wait()

        @pl.when(b + 1 < rows_dec // batch)
        def _():
            cache_copy(b + 1).start()

        at = lax.rem(b, 2)
        for r in range(batch):
            span = slice(r * heads, (r + 1) * heads)
            query = q_rows[pl.ds(pl.multiple_of(b * LANES + r * heads, 8), heads), :].astype(BF16)
            new = fresh[pl.ds(b * batch + r, 1), :]
            a_limits[span, :] = jnp.broadcast_to(
                lengths[pl.ds(b * batch + r, 1), :], (heads, LANES)
            )
            for h in range(kv_heads):
                part = slice(r * heads + h * share, r * heads + (h + 1) * share)
                key = 2 * HEAD * h
                product = lax.dot_general(
                    query,
                    cache[at, r, :, key : key + HEAD],
                    (((1,), (1,)), ((), ())),
                    preferred_element_type=F32,
                )
                a_scores[part, :] = product[h * share : (h + 1) * share]
                a_keys[part, :] = jnp.broadcast_to(new[:, key : key + HEAD], (share, HEAD))
                a_values[part, :] = jnp.broadcast_to(
                    new[:, key + HEAD : key + 2 * HEAD], (share, HEAD)
                )
        lane = lax.broadcasted_iota(jnp.int32, (LANES, LANES), 1).astype(F32)
        scores = jnp.where(lane < a_limits[...], a_scores[...] * HEAD ** (-0.5), -1e30)
        own = jnp.sum(q_rows[ds(b, LANES), :] * a_keys[...], axis=1, keepdims=True) * HEAD ** (-0.5)
        top = jnp.maximum(jnp.max(scores, axis=1, keepdims=True), own)
        weights = jnp.exp(scores - top)
        own_weight = jnp.exp(own - top)
        total = jnp.sum(weights, axis=1, keepdims=True) + own_weight
        a_scores[...] = weights / total
        own_part = (own_weight / total).astype(BF16).astype(F32) * a_values[...]
        a_values[...] = own_part
        for r in range(batch):
            span = slice(r * heads, (r + 1) * heads)
            probs = a_scores[span, :].astype(BF16)
            for h in range(kv_heads):
                part = slice(r * heads + h * share, r * heads + (h + 1) * share)
                value = 2 * HEAD * h + HEAD
                product = jnp.dot(
                    probs, cache[at, r, :, value : value + HEAD], preferred_element_type=F32
                )
                a_rows[pl.ds(pl.multiple_of(b * LANES, LANES) + r * heads + h * share, share), :] = (
                    product[h * share : (h + 1) * share] + a_values[part, :]
                )
        return carry

    att_copy = pltpu.make_async_copy(attended, states_out, misc_sem.at[1])

    batches = rows_dec // batch

    def attend_start():
        for j in range(heads):
            q_rows[pl.ds(j, rows_dec, stride=heads), :] = queries[
                :, j * HEAD : (j + 1) * HEAD
            ].astype(F32)
        fresh[...] = new_kv[...].astype(F32)
        lengths[...] = spread_rows(cache_lengths[...].astype(F32))

    def attend(low, high):
        @pl.when(g != 0)
        def _():
            if low == 0:
                attend_start()
            lax.fori_loop(low, high, attend_batch, 0)
            if high == batches:
                for j in range(heads):
                    attended[:, j * HEAD : (j + 1) * HEAD] = a_rows[
                        pl.ds(j, rows_dec, stride=heads), :
                    ].astype(BF16)
                att_copy.start()

    finish(0)
    z_start(0, 1)
    for k in far_first:
        if k not in (1, seqs // 2):
            z_start(0, k)
    own_sends(0)
    for c in range(1, chunks):
        text_chunk(c)
    for level in range(levels - 1):
        reduce_level(level)
    z_start(0, seqs // 2)
    for c in range(1, chunks):
        finish(c)
        z_start(c, 1)
        own_sends(c)
    forward(0, 1)
    forward(0, seqs - 1)

    own_rows = ds(g, half_rows)

    def gelu_body(t, carry):
        at = ds(t, col_tile)
        p_copy(levels - 1, t).wait()
        total = p_own[0, :, at] + p_recv[base_at(levels - 1), :, at].astype(F32)
        total = total + bias_rows[pl.ds(t, 1), :]
        hid[own_rows, at] = (0.5 * total * (1.0 + lax.erf(total * 0.5**0.5))).astype(BF16)
        return carry

    lax.fori_loop(0, col_tiles, gelu_body, 0)
    h_send = remote(hid.at[own_rows, :], hid.at[own_rows, :], send_h, recv_h, group=peer)

    @pl.when(g != 0)
    def _():
        h_send.start()

    for c in range(1, chunks):
        for k in far_first:
            if k not in (1, seqs // 2):
                z_start(c, k)
        forward(c, 1)

    total = jnp.zeros((half_rows, LANES), F32)
    for j in range(feat_local // LANES):
        at = slice(j * LANES, (j + 1) * LANES)
        value = hid[own_rows, at].astype(F32)
        total = total + value * value
        i_scaled[:, at] = (value * gain_rows[j : j + 1, :]).astype(BF16)
    total = jnp.concatenate([total, jnp.zeros((LANES - half_rows, LANES), F32)], axis=0)
    isq_own[...] = jnp.broadcast_to(
        jnp.sum(jnp.transpose(total), axis=0, keepdims=True), isq_own.shape
    )

    def iq_send(k):
        return remote(isq_own, isq_recv.at[k - 1], send_iq.at[k - 1], recv_iq.at[k - 1], mp=mp_at(k))

    for k in range(1, mps):
        iq_send(k).start()
    for c in range(chunks, blocks):
        for q in range(CORES):
            for k in range(chips):
                w_copy(c, q, k).wait()
    for b in range(blocks):
        part = jnp.dot(i_scaled[...], w_buf[b], preferred_element_type=F32)
        i_acc[b] = part[:, :own_cols]
        is1[b] = part[:, own_cols:].astype(BF16)
    i_first = remote(is1, ir1, send_i1, recv_i1, mp=partner)
    i_first.start()

    def i_second(k):
        return remote(
            is2.at[k - 1], ir2.at[k - 1], send_i2.at[k - 1], recv_i2.at[k - 1], mp=chip_at(k)
        )

    i_first.wait()
    for b in range(blocks):
        total = i_acc[b] + ir1[b].astype(F32)
        i_acc[b] = total
        for k in range(1, chips):
            is2[k - 1, b] = total[:, k * LANES : (k + 1) * LANES].astype(BF16)
    for k in range(1, chips):
        i_second(k).start()
    for k in range(1, mps):
        iq_send(k).wait()
    squares = isq_own[...]
    for k in range(1, mps):
        squares = squares + isq_recv[k - 1]
    i_scale = spread_rows(lax.rsqrt(squares / width + 1e-05)[:1])[:half_rows]
    for k in range(1, chips):
        i_second(k).wait()
    for b in range(blocks):
        value = i_acc[b, :, :LANES]
        for k in range(1, chips):
            value = value + ir2[k - 1, b].astype(F32)
        ikv[:, pl.ds(pl.multiple_of(columns(b), LANES), LANES)] = (value * i_scale).astype(BF16)

    def img_at(index, half):
        return img_out.at[index, ds(half, half_rows), :]

    def iz_send(k):
        return remote(ikv, img_at(s, g), send_iz.at[k - 1], recv_iz.at[k - 1], seq=flip(s, k))

    iy_send = remote(ikv, img_at(s, g), send_iy, recv_iy, group=peer)
    for k in far_first:
        iz_send(k).start()
    iy_send.start()
    i_local = pltpu.make_async_copy(ikv, img_at(s, g), misc_sem.at[2])
    i_local.start()
    for c in range(1, chunks):
        z_start(c, seqs // 2)
    attend(0, batches)
    for k in far_first:
        if k not in (1, seqs - 1):
            forward(0, k)

    def if_send(k):
        src = flip(s, k)
        return remote(
            img_at(src, 0), img_at(src, 0), send_if.at[k - 1], recv_if.at[k - 1], group=peer
        )


    @pl.when(g == 0)
    def _():
        for c in range(chunks):
            take_peer(c)

    hid_copy = pltpu.make_async_copy(hid, states_out, misc_sem.at[1])

    @pl.when(g == 0)
    def _():
        h_send.wait_recv()
        hid_copy.start()

    rest = [k for k in far_first if k != 1]
    for c in range(1, chunks):

        @pl.when(outer)
        def _():
            forward(c, rest[0])

        @pl.when(jnp.logical_not(outer))
        def _():
            forward(c, rest[-1])

    for k in far_first:
        iz_send(k).wait_recv()

        @pl.when(g == 0)
        def _():
            if_send(k).start()

    for c in range(1, chunks):

        @pl.when(outer)
        def _():
            for k in rest[1:]:
                forward(c, k)

        @pl.when(jnp.logical_not(outer))
        def _():
            for k in rest[:-1]:
                forward(c, k)


    for c in range(chunks):
        for k in range(1, seqs):
            for h in range(halves):
                z_piece(c, k, h).wait_send()
        local(by_owner.at[c], everything, c).wait()

        @pl.when(g == 0)
        def _():
            y_send(by_owner.at[c], everything, c).wait_send()
            local2(c).wait()

        @pl.when(g != 0)
        def _():
            y_send(by_owner.at[c], everything, c).wait_recv()
            k_send(c).wait_send()

    for k in range(1, seqs):
        f_send(k).wait_send()
        d_send(k).wait()
        iz_send(k).wait_send()

        @pl.when(g == 0)
        def _():
            if_send(k).wait_send()

        @pl.when(g != 0)
        def _():
            if_send(k).wait_recv()

    @pl.when(g != 0)
    def _():
        h_send.wait_send()

    iy_send.wait()
    i_local.wait()
    d_local.wait()
    hid_copy.wait()


def prefill(
    mesh_sizes,
    prompt_len,
    embeds,
    image_feats,
    proj_w,
    kv_w,
    kv_cache,
    image_pos,
    bias,
    gain,
    page_owner,
    queries,
    new_kv,
    cache_lengths,
    prompt_lengths,
):
    groups, seqs, mps = mesh_sizes
    chips = mps // CORES
    tokens, feat_local = embeds.shape
    tiles = tokens // TILE
    rows_img, all_channels = image_feats.shape
    half_rows = rows_img // groups
    channels = proj_w.shape[0]
    block_cols = kv_w.shape[1] // mps
    cols = block_cols // groups
    chunks = cols // LANES
    blocks = groups * chunks
    steps = chunks * tiles
    col_tile = min(512, feat_local)
    col_tiles = feat_local // col_tile
    levels = seqs.bit_length() - 1
    pages = page_owner.shape[1]
    page = tokens // pages
    slots = seqs * (2 * pages // seqs)
    rows_dec = queries.shape[0]
    heads = queries.shape[1] // HEAD
    batch = LANES // heads
    dma = pltpu.SemaphoreType.DMA
    vmem = pl.BlockSpec(memory_space=pltpu.VMEM)
    anywhere = pl.BlockSpec(memory_space=pl.ANY)
    dense = tokens // LANES
    return pl.pallas_call(
        functools.partial(prefill_kernel, groups, seqs, mps, prompt_len),
        out_shape=(
            pltpu.VMEM((slots * page, block_cols), BF16),
            pltpu.VMEM((rows_img, feat_local), BF16),
            pltpu.VMEM((seqs, rows_img, block_cols), BF16),
            pltpu.VMEM((seqs, 8, rows_img), F32),
        ),
        in_specs=[anywhere] * 5 + [vmem] * 7 + [pl.BlockSpec(memory_space=pltpu.SMEM)],
        out_specs=(vmem,) * 4,
        scratch_shapes=[
            pltpu.VMEM((feat_local // LANES, LANES), F32),
            pltpu.VMEM((col_tiles, col_tile), F32),
            pltpu.VMEM((slots, pages), BF16),
            pltpu.VMEM((dense, LANES), F32),
            pltpu.VMEM((8, rows_img), F32),
            pltpu.VMEM((half_rows, all_channels), BF16),
            pltpu.VMEM((seqs, half_rows, channels), BF16),
            pltpu.VMEM((tokens, feat_local), BF16),
            pltpu.VMEM((blocks, feat_local, mps * LANES), BF16),
            pltpu.VMEM((channels, feat_local), BF16),
            pltpu.VMEM((seqs, half_rows, channels), BF16),
            pltpu.VMEM((2, TILE, chips * LANES), F32),
            pltpu.VMEM((steps, TILE, chips * LANES), BF16),
            pltpu.VMEM((steps, TILE, chips * LANES), BF16),
            pltpu.VMEM((chunks, tokens, LANES), F32),
            pltpu.VMEM((steps, chips - 1, TILE, LANES), BF16),
            pltpu.VMEM((steps, chips - 1, TILE, LANES), BF16),
            pltpu.VMEM((dense, LANES), F32),
            pltpu.VMEM((mps - 1, dense, LANES), F32),
            pltpu.VMEM((dense, LANES), F32),
            pltpu.VMEM((slots * page, LANES), F32),
            pltpu.VMEM((chunks, slots * page, LANES), BF16),
            pltpu.VMEM((chunks, slots * page, LANES), BF16),
            pltpu.VMEM((chunks, tokens, LANES), BF16),
            pltpu.VMEM((chunks, tokens, LANES), BF16),
            pltpu.VMEM((chunks, slots * page, LANES), BF16),
            pltpu.VMEM((seqs // 2, half_rows, feat_local), F32),
            pltpu.VMEM((seqs - 1, half_rows, feat_local), BF16),
            pltpu.VMEM((seqs - 1, half_rows, feat_local), BF16),
            pltpu.VMEM((rows_img, feat_local), BF16),
            pltpu.VMEM((half_rows, feat_local), BF16),
            pltpu.VMEM((blocks, half_rows, chips * LANES), F32),
            pltpu.VMEM((blocks, half_rows, chips * LANES), BF16),
            pltpu.VMEM((blocks, half_rows, chips * LANES), BF16),
            pltpu.VMEM((chips - 1, blocks, half_rows, LANES), BF16),
            pltpu.VMEM((chips - 1, blocks, half_rows, LANES), BF16),
            pltpu.VMEM((8, LANES), F32),
            pltpu.VMEM((mps - 1, 8, LANES), F32),
            pltpu.VMEM((half_rows, block_cols), BF16),
            pltpu.VMEM((rows_dec * heads, HEAD), F32),
            pltpu.VMEM(new_kv.shape, F32),
            pltpu.VMEM((rows_dec, LANES), F32),
            pltpu.VMEM((2, batch) + kv_cache.shape[1:], BF16),
            pltpu.VMEM((LANES, LANES), F32),
            pltpu.VMEM((LANES, LANES), F32),
            pltpu.VMEM((LANES, LANES), F32),
            pltpu.VMEM((LANES, LANES), F32),
            pltpu.VMEM((rows_dec * heads, HEAD), F32),
            pltpu.VMEM(queries.shape, BF16),
            dma((1,)),
            dma((2,)),
            dma((blocks, mps)),
            dma((tiles,)),
            dma,
            dma,
            dma((steps,)),
            dma((steps,)),
            dma((steps, chips - 1)),
            dma((steps, chips - 1)),
            dma((mps - 1,)),
            dma((mps - 1,)),
            dma((seqs - 1,)),
            dma((seqs - 1,)),
            dma((seqs - 1,)),
            dma((seqs - 1,)),
            dma((levels, col_tiles)),
            dma((levels, col_tiles)),
            dma,
            dma,
            dma,
            dma,
            dma((chips - 1,)),
            dma((chips - 1,)),
            dma((mps - 1,)),
            dma((mps - 1,)),
            dma((chunks, 2 * (seqs - 1))),
            dma((chunks, 2 * (seqs - 1))),
            dma((chunks,)),
            dma((chunks,)),
            dma((chunks,)),
            dma((chunks,)),
            dma((chunks,)),
            dma((chunks,)),
            dma((seqs - 1,)),
            dma((seqs - 1,)),
            dma,
            dma,
            dma((seqs - 1,)),
            dma((seqs - 1,)),
            dma((seqs - 1,)),
            dma((seqs - 1,)),
            dma((3,)),
        ],
        compiler_params=pltpu.CompilerParams(
            collective_id=0, has_side_effects=True, vmem_limit_bytes=57 * 1024 * 1024
        ),
        name="prefill_pages",
    )(
        embeds,
        image_feats,
        proj_w,
        kv_w,
        kv_cache,
        image_pos,
        bias,
        gain,
        page_owner,
        queries,
        new_kv,
        cache_lengths,
        prompt_lengths,
    )


def place_kernel(index, offset, text, img, dest, states, out, states_out, rows, sems):
    parts = index.shape[0]
    block = text.shape[0] // parts

    def store(b):
        span = pl.ds(b * block, block)
        return pltpu.make_async_copy(rows.at[span, :], out.at[span, :], sems.at[b])

    for b in range(parts):
        spots = dest[index[b]][:1].astype(jnp.int32) - offset[b]
        hit = lax.broadcasted_iota(jnp.int32, (block, dest.shape[2]), 0) == spots
        placed = jnp.dot(
            jnp.where(hit, 1.0, 0.0).astype(BF16), img[index[b]], preferred_element_type=F32
        )
        span = pl.ds(b * block, block)
        rows[span, :] = text[span, :] + placed.astype(BF16)
        store(b).start()
    state_store = pltpu.make_async_copy(states, states_out, sems.at[parts])
    state_store.start()
    for b in range(parts):
        store(b).wait()
    state_store.wait()


def place(index, offset, text, img, dest, states):
    parts = index.shape[0]
    smem = pl.BlockSpec(memory_space=pltpu.SMEM)
    vmem = pl.BlockSpec(memory_space=pltpu.VMEM)
    anywhere = pl.BlockSpec(memory_space=pl.ANY)
    near = [pltpu.with_memory_space_constraint(x, pltpu.VMEM) for x in (text, img, dest, states)]
    return pl.pallas_call(
        place_kernel,
        out_shape=(
            jax.ShapeDtypeStruct(text.shape, text.dtype),
            jax.ShapeDtypeStruct(states.shape, states.dtype),
        ),
        in_specs=[smem, smem, vmem, vmem, vmem, vmem],
        out_specs=(anywhere, anywhere),
        scratch_shapes=[
            pltpu.VMEM(text.shape, text.dtype),
            pltpu.SemaphoreType.DMA((parts + 1,)),
        ],
        compiler_params=pltpu.CompilerParams(vmem_limit_bytes=16 * 1024 * 1024),
        name="place_images",
    )(index, offset, *near)


def per_device(
    mesh_sizes,
    embeds,
    image_feats,
    image_pos,
    proj_w,
    proj_b,
    norm_gain,
    kv_w,
    prompt_lengths,
    page_owner,
    queries,
    kv_cache,
    new_kv,
    cache_lengths,
):
    groups, seqs, mps = mesh_sizes
    group_index = lax.axis_index("group")
    prefill_side = group_index == 0
    seq_index = lax.axis_index("seq")
    token_rows, width_local = embeds.shape
    prompt_len = token_rows * seqs // prompt_lengths.shape[0]
    page = token_rows // page_owner.shape[0]
    capacity = 2 * page_owner.shape[0] // seqs
    text, row_states, img, dest_all = prefill(
        mesh_sizes,
        prompt_len,
        embeds,
        image_feats,
        proj_w,
        kv_w,
        kv_cache,
        image_pos[None, :],
        proj_b.reshape(-1, LANES),
        norm_gain.reshape(-1, LANES),
        page_owner.reshape(1, -1),
        queries,
        new_kv,
        cache_lengths[None, :],
        prompt_lengths,
    )
    parts = max(1, 8 // seqs)
    order = jnp.arange(seqs * parts, dtype=jnp.int32)
    source, part = order // parts, order % parts
    index = jnp.where(prefill_side, seq_index, source)
    offset = jnp.where(prefill_side, source, seq_index) * (capacity * page)
    offset = offset + part * (capacity * page // parts)
    page_slots, row_states = place(index, offset, text, img, dest_all, row_states)
    page_slots = page_slots.reshape(-1, page, text.shape[1])
    return (page_slots, row_states)


def solution(mesh):
    mesh_sizes = (mesh.shape["group"], mesh.shape["seq"], mesh.shape["mp"])
    in_specs = (
        P("seq", "mp"),
        P("seq", None),
        P("seq"),
        P("seq", "mp"),
        P("mp"),
        P("mp"),
        P("mp", None),
        P(),
        P("seq", None),
        P("seq", "mp"),
        P("seq", None, "mp"),
        P("seq", "mp"),
        P("seq"),
    )
    out_specs = (P(("group", "seq"), None, "mp"), P(("group", "seq"), "mp"))
    return jax.shard_map(
        functools.partial(per_device, mesh_sizes),
        mesh=mesh,
        in_specs=in_specs,
        out_specs=out_specs,
        check_vma=False,
    )
```

```python
import functools

import jax
import jax.numpy as jnp
from jax import lax
from jax.experimental import pallas as pl
from jax.experimental.pallas import tpu as pltpu
from jax.sharding import PartitionSpec as P

HEAD = 128
LANES = 128
TILE = 256
CORES = 2
PIECES = 4
MESH = pl.DeviceIdType.MESH
F32 = jnp.float32
BF16 = jnp.bfloat16


def ds(index, size):
    return pl.ds(pl.multiple_of(index * size, size), size)


def flip(index, distance):
    result = index
    bit = 1
    while bit <= distance:
        if distance & bit:
            result = result + bit - 2 * bit * lax.rem(index // bit, 2)
        bit *= 2
    return result


def spread_rows(row):
    return jnp.transpose(jnp.broadcast_to(row, (LANES, LANES)))


def prefill_kernel(
    groups,
    seqs,
    mps,
    prompt_len,
    embeds,
    image_feats,
    proj_w,
    kv_w,
    kv_cache,
    image_pos,
    bias,
    gain,
    page_owner,
    queries,
    new_kv,
    cache_lengths,
    prompt_lengths,
    slots_out,
    states_out,
    img_out,
    dest_out,
    gain_rows,
    bias_rows,
    sel,
    mask,
    dest,
    f_rows,
    feats,
    e_buf,
    w_buf,
    pw_buf,
    f_buf,
    acc1,
    s1,
    r1,
    acc2,
    s2,
    r2,
    sq_own,
    sq_recv,
    scale,
    outf,
    by_owner,
    arrived,
    kv_send,
    kv_recv,
    by_peer,
    p_own,
    p_send,
    p_recv,
    d_send_buf,
    d_recv_buf,
    hid,
    i_scaled,
    i_acc,
    is1,
    ir1,
    is2,
    ir2,
    isq_own,
    isq_recv,
    ikv,
    q_rows,
    fresh,
    lengths,
    cache,
    a_scores,
    a_keys,
    a_values,
    a_limits,
    a_rows,
    attended,
    load_sem,
    cache_sem,
    w_sem,
    e_sem,
    pw_sem,
    fl_sem,
    send1,
    recv1,
    send2,
    recv2,
    send_sq,
    recv_sq,
    send_f,
    recv_f,
    send_fc,
    recv_fc,
    send_r,
    recv_r,
    send_dr,
    recv_dr,
    send_h,
    recv_h,
    send_i1,
    recv_i1,
    send_i2,
    recv_i2,
    send_iq,
    recv_iq,
    send_z,
    recv_z,
    send_y,
    recv_y,
    send_k,
    recv_k,
    loc_sem,
    loc2_sem,
    send_iz,
    recv_iz,
    send_iy,
    recv_iy,
    send_if,
    recv_if,
    send_d,
    recv_d,
    misc_sem,
):
    g = lax.axis_index("group")
    s = lax.axis_index("seq")
    m = lax.axis_index("mp")
    chips = mps // CORES
    chip = m // CORES
    core = m % CORES
    partner = chip * CORES + (1 - core)
    peer = 1 - g
    blocks, feat_local, _ = w_buf.shape
    chunks = blocks // groups
    tokens = e_buf.shape[0]
    tiles = tokens // TILE
    steps = chunks * tiles
    col_tile = min(512, feat_local)
    col_tiles = feat_local // col_tile
    rows_img = hid.shape[0]
    half_rows = rows_img // groups
    core_rows = half_rows // CORES
    cols = chunks * LANES
    block_cols = cols * groups
    slots, pages = sel.shape
    page = tokens // pages
    capacity = slots // seqs
    width = feat_local * mps
    channels = feats.shape[2]
    block = slots * page // seqs
    own_cols = chips * LANES

    def remote(src, dst, send, recv, **where):
        return pltpu.make_async_remote_copy(
            src_ref=src,
            dst_ref=dst,
            send_sem=send,
            recv_sem=recv,
            device_id=where,
            device_id_type=MESH,
        )

    def seq_at(k):
        return lax.rem(s + k, seqs)

    def mp_at(k):
        return lax.rem(m + k, mps)

    def chip_at(k):
        return lax.rem(chip + k, chips) * CORES + core

    def e_copy(i):
        return pltpu.make_async_copy(embeds.at[ds(i, TILE), :], e_buf.at[ds(i, TILE), :], e_sem.at[i])

    def half_at(b):
        return lax.rem(g + b // chunks, groups)

    def columns(b):
        return half_at(b) * cols + b % chunks * LANES

    def w_copy(c, q, k):
        target = lax.rem(chip + k, chips) * CORES + (core if q == 0 else 1 - core)
        start = target * block_cols + columns(c)
        return pltpu.make_async_copy(
            kv_w.at[:, pl.ds(pl.multiple_of(start, LANES), LANES)],
            w_buf.at[c, :, (q * chips + k) * LANES : (q * chips + k + 1) * LANES],
            w_sem.at[c, q * chips + k],
        )

    f_load = pltpu.make_async_copy(image_feats.at[ds(g, half_rows), :], f_rows, load_sem.at[0])
    f_load.start()
    barrier = pltpu.get_barrier_semaphore()
    for k in range(1, seqs):
        pl.semaphore_signal(barrier, inc=1, device_id={"seq": seq_at(k)}, device_id_type=MESH)
    for k in range(1, mps):
        pl.semaphore_signal(barrier, inc=1, device_id={"mp": mp_at(k)}, device_id_type=MESH)
    pl.semaphore_signal(barrier, inc=1, device_id={"group": peer}, device_id_type=MESH)
    e_copy(0).start()
    for q in range(CORES):
        for k in range(chips):
            w_copy(0, q, k).start()
    cache_first = pltpu.make_async_copy(
        kv_cache.at[pl.ds(0, LANES // (queries.shape[1] // HEAD))], cache.at[0], cache_sem.at[0]
    )
    pw_copy = pltpu.make_async_copy(proj_w, pw_buf, pw_sem)

    def later_loads():
        pw_copy.start()
        for c in range(1, blocks):
            for q in range(CORES):
                for k in range(chips):
                    w_copy(c, q, k).start()

        @pl.when(g != 0)
        def _():
            cache_first.start()


    f_load.wait()
    for i in range(1, tiles):
        e_copy(i).start()
    for b in range(seqs):
        feats[b] = f_rows[:, b * channels : (b + 1) * channels]
    own_feats = pltpu.make_async_copy(feats.at[s], f_buf.at[0], fl_sem)
    own_feats.start()

    pl.semaphore_wait(barrier, seqs - 1 + mps - 1 + 1)

    def f_send(k):
        rows = ds(core, core_rows)
        return remote(
            feats.at[flip(s, k), rows, :],
            f_buf.at[k, rows, :],
            send_f.at[k - 1],
            recv_f.at[k - 1],
            seq=flip(s, k),
        )

    def f_share(k):
        rows = ds(core, core_rows)
        return remote(
            f_buf.at[k, rows, :],
            f_buf.at[k, rows, :],
            send_fc.at[k - 1],
            recv_fc.at[k - 1],
            mp=partner,
        )

    def d_send(k):
        return remote(dest, dest_out.at[s], send_d.at[k - 1], recv_d.at[k - 1], seq=seq_at(k))

    for k in range(1, seqs):
        f_send(k).start()

    gain_rows[...] = gain[...].astype(F32)
    biases = bias[...].astype(F32)
    for j in range(feat_local // LANES):
        t, within = divmod(j, col_tile // LANES)
        bias_rows[t : t + 1, within * LANES : (within + 1) * LANES] = biases[j : j + 1, :]

    prompt = (s * tokens) // prompt_len
    limit = prompt_lengths[prompt]
    base = s * tokens - prompt * prompt_len
    spots = image_pos[...] - s * tokens
    down = lax.broadcasted_iota(jnp.int32, (pages, LANES), 0)
    across = lax.broadcasted_iota(jnp.int32, (pages, LANES), 1)
    owner_across = jnp.broadcast_to(page_owner[...].astype(F32), (pages, LANES))
    owner_down = jnp.transpose(owner_across)
    rank = jnp.sum(
        jnp.where((owner_down == owner_across) & (down < across), 1.0, 0.0), axis=0, keepdims=True
    )
    slot = owner_across[:1] * capacity + rank
    slot_rows = lax.broadcasted_iota(jnp.int32, (slots, LANES), 0).astype(F32)
    sel[...] = jnp.where(slot_rows == slot, 1.0, 0.0).astype(BF16)
    page_bits = page.bit_length() - 1
    on_page = down == lax.shift_right_logical(spots, page_bits)
    image_slot = jnp.sum(jnp.where(on_page, spread_rows(slot), 0.0), axis=0, keepdims=True)
    image_row = image_slot * page + (spots & (page - 1)).astype(F32)
    dest[...] = jnp.broadcast_to(
        jnp.where(spots + base < limit, image_row, -1048576.0), dest.shape
    )
    dense = mask.shape[0]
    tall = lax.broadcasted_iota(jnp.int32, (dense, LANES), 0)
    image_block = jnp.where(tall == lax.shift_right_logical(spots, 7), 1.0, 0.0)
    image_lane = jnp.where(down == (spots & (LANES - 1)), 1.0, 0.0)
    images = lax.dot_general(
        image_block.astype(BF16),
        image_lane.astype(BF16),
        (((1,), (1,)), ((), ())),
        preferred_element_type=F32,
    )
    token = tall * LANES + lax.broadcasted_iota(jnp.int32, (dense, LANES), 1)
    mask[...] = jnp.where((token + base < limit) & (images < 0.5), 1.0, 0.0)
    for k in range(1, seqs):
        d_send(k).start()
    d_local = pltpu.make_async_copy(dest, dest_out.at[s], misc_sem.at[0])
    d_local.start()

    def first(n):
        return remote(s1.at[n], r1.at[n], send1.at[n], recv1.at[n], mp=partner)

    def second(n, k):
        return remote(
            s2.at[n, k - 1], r2.at[n, k - 1], send2.at[n, k - 1], recv2.at[n, k - 1], mp=chip_at(k)
        )

    def sq_send(k):
        return remote(sq_own, sq_recv.at[k - 1], send_sq.at[k - 1], recv_sq.at[k - 1], mp=mp_at(k))

    far_first = range(seqs - 1, 0, -1)
    outer = lax.rem(s, 2) == lax.rem(s // 2, 2)

    levels = seqs.bit_length() - 1

    def sent_at(level):
        step_size = 2 << level
        return list(range(1 << level, seqs, step_size))

    def kept_at(level):
        step_size = 2 << level
        return list(range(0, seqs, step_size))

    def base_at(level):
        return seqs - (seqs >> level)

    def p_copy(level, t):
        span = pl.ds(base_at(level), len(sent_at(level)))
        at = ds(t, col_tile)
        return remote(
            p_send.at[span, :, at],
            p_recv.at[span, :, at],
            send_r.at[level, t],
            recv_r.at[level, t],
            seq=flip(s, 1 << level),
        )

    first_tile = slice(0, col_tile)

    def direct(k):
        return remote(
            d_send_buf.at[k - 1],
            d_recv_buf.at[k - 1],
            send_dr.at[k - 1],
            recv_dr.at[k - 1],
            seq=flip(s, k),
        )

    def scale_tile(i):
        e_copy(i).wait()

        def body(b, carry):
            rows = ds(i * (TILE // LANES) + b, LANES)
            total = jnp.zeros((LANES, LANES), F32)
            for j in range(feat_local // LANES):
                at = slice(j * LANES, (j + 1) * LANES)
                value = e_buf[rows, at].astype(F32)
                total = total + value * value
                e_buf[rows, at] = (value * gain_rows[j : j + 1, :]).astype(BF16)
            sq_own[pl.ds(i * (TILE // LANES) + b, 1), :] = jnp.sum(
                jnp.transpose(total), axis=0, keepdims=True
            )
            return carry

        lax.fori_loop(0, TILE // LANES, body, 0)

    def project():
        for k in range(1, seqs):
            f_share(k).wait()
        own_feats.wait()
        pw_copy.wait()
        spread = f_buf[...].reshape(seqs * half_rows, channels)

        def tile(at):
            out = jnp.dot(spread, pw_buf[:, at], preferred_element_type=F32)
            return out.reshape(seqs, half_rows, col_tile)

        out = tile(first_tile)
        for k in far_first:
            d_send_buf[k - 1] = out[k].astype(BF16)
            direct(k).start()
        p_own[0, :, first_tile] = out[0]

        def body(t, carry):
            at = ds(t, col_tile)
            out = tile(at)
            for slot_at, e in enumerate(sent_at(0)):
                p_send[slot_at, :, at] = out[e].astype(BF16)
            p_copy(0, t).start()
            for slot_at, e in enumerate(kept_at(0)):
                p_own[slot_at, :, at] = out[e]
            return carry

        lax.fori_loop(1, col_tiles, body, 0)

    def reduce_level(level):
        def body(t, carry):
            at = ds(t, col_tile)
            p_copy(level, t).wait()
            for index in range(len(kept_at(level))):
                total = p_own[index, :, at] + p_recv[base_at(level) + index, :, at].astype(F32)
                if index % 2 == 0:
                    p_own[index // 2, :, at] = total
                else:
                    p_send[base_at(level + 1) + index // 2, :, at] = total.astype(BF16)
            p_copy(level + 1, t).start()
            return carry

        lax.fori_loop(1, col_tiles, body, 0)

    def combine(p):
        c, i = p // tiles, lax.rem(p, tiles)
        first(p).wait()
        total = acc1[lax.rem(p, 2)] + r1[p].astype(F32)
        acc2[c, ds(i, TILE), :] = total[:, :LANES]
        for k in range(1, chips):
            s2[p, k - 1] = total[:, k * LANES : (k + 1) * LANES].astype(BF16)
            second(p, k).start()

    def multiply(n, c, i):
        part = jnp.dot(e_buf[ds(i, TILE), :], w_buf[c], preferred_element_type=F32)
        acc1[lax.rem(n, 2)] = part[:, :own_cols]
        s1[n] = part[:, own_cols:].astype(BF16)
        first(n).start()

    def text_chunk(c):
        for q in range(CORES):
            for k in range(chips):
                w_copy(c, q, k).wait()

        def body(i, carry):
            if c == 0:
                scale_tile(i)

                @pl.when(i == tiles // 2)
                def _():
                    later_loads()

            multiply(c * tiles + i, c, i)

            @pl.when(i > 0)
            def _():
                combine(c * tiles + i - 1)

            return carry

        lax.fori_loop(0, tiles, body, 0)
        if c == 0:
            for k in range(1, mps):
                sq_send(k).start()
        combine(c * tiles + tiles - 1)

    text_chunk(0)
    for k in range(1, seqs):
        f_send(k).wait_recv()
        f_share(k).start()
    project()

    for k in range(1, mps):
        sq_send(k).wait()
    squares = sq_own[...]
    for k in range(1, mps):
        squares = squares + sq_recv[k - 1]
    scale[...] = mask[...] * lax.rsqrt(squares / width + 1e-05)

    pieces = PIECES
    piece = block // pieces

    def z_piece(c, k, h):
        return remote(
            by_owner.at[c, ds(flip(s, k) * pieces + h, piece), :],
            arrived.at[c, ds(s * pieces + h, piece), :],
            send_z.at[c, (k - 1) * pieces + h],
            recv_z.at[c, (k - 1) * pieces + h],
            seq=flip(s, k),
        )

    def z_start(c, k):
        for h in range(pieces):
            z_piece(c, k, h).start()

    def out_at(rows, half, c):
        at = pl.ds(pl.multiple_of(half * cols + c * LANES, LANES), LANES)
        return slots_out.at[rows, at]

    def y_send(src, rows, c):
        return remote(src, out_at(rows, g, c), send_y.at[c], recv_y.at[c], group=peer)

    def local(src, rows, c):
        return pltpu.make_async_copy(src, out_at(rows, g, c), loc_sem.at[c])

    everything = pl.ds(0, slots * page)

    def select(c, target):
        chosen = sel[...]
        for t in range(page):
            rows = acc2[c, pl.ds(t, pages, stride=page), :].astype(BF16)
            outf[pl.ds(t, slots, stride=page), :] = jnp.dot(
                chosen, rows, preferred_element_type=F32
            )
        target[c] = outf[...].astype(BF16)

    def k_send(c):
        return remote(kv_send.at[c], kv_recv.at[c], send_k.at[c], recv_k.at[c], group=peer)

    def local2(c):
        return pltpu.make_async_copy(
            by_peer.at[c], out_at(everything, 1 - g, c), loc2_sem.at[c]
        )

    def finish(c):
        def body(i, carry):
            n = c * tiles + i
            for k in range(1, chips):
                second(n, k).wait()
            for b in range(TILE // LANES):
                rows = pl.ds(pl.multiple_of(i * TILE + b * LANES, LANES), LANES)
                within = pl.ds(b * LANES, LANES)
                value = acc2[c, rows, :]
                for k in range(1, chips):
                    value = value + r2[n, k - 1, within, :].astype(F32)
                value = value * spread_rows(scale[pl.ds(i * (TILE // LANES) + b, 1), :])
                acc2[c, rows, :] = value
                kv_send[c, rows, :] = value.astype(BF16)
            return carry

        lax.fori_loop(0, tiles, body, 0)
        select(c, by_owner)

    def own_sends(c):
        mine = ds(s, block)

        @pl.when(g == 0)
        def _():
            y_send(by_owner.at[c, mine, :], mine, c).start()
            local(by_owner.at[c], everything, c).start()

        @pl.when(g != 0)
        def _():
            k_send(c).start()
            local(by_owner.at[c, mine, :], mine, c).start()

    def take_peer(c):
        k_send(c).wait_recv()
        acc2[c] = kv_recv[c].astype(F32)
        select(c, by_peer)
        local2(c).start()

    def forward(c, k):
        for h in range(pieces):
            z_piece(c, k, h).wait_recv()
            rows = ds(flip(s, k) * pieces + h, piece)

            @pl.when(g == 0)
            def _():
                y_send(arrived.at[c, rows, :], rows, c).start()

            @pl.when(g != 0)
            def _():
                local(arrived.at[c, rows, :], rows, c).start()

    heads = queries.shape[1] // HEAD
    kv_heads = kv_cache.shape[2] // (2 * HEAD)
    share = heads // kv_heads
    rows_dec = queries.shape[0]
    batch = LANES // heads

    def cache_copy(b):
        return pltpu.make_async_copy(
            kv_cache.at[ds(b, batch)], cache.at[lax.rem(b, 2)], cache_sem.at[lax.rem(b, 2)]
        )

    def attend_batch(b, carry):
        cache_copy(b).wait()

        @pl.when(b + 1 < rows_dec // batch)
        def _():
            cache_copy(b + 1).start()

        at = lax.rem(b, 2)
        for r in range(batch):
            span = slice(r * heads, (r + 1) * heads)
            query = q_rows[pl.ds(pl.multiple_of(b * LANES + r * heads, 8), heads), :].astype(BF16)
            new = fresh[pl.ds(b * batch + r, 1), :]
            a_limits[span, :] = jnp.broadcast_to(
                lengths[pl.ds(b * batch + r, 1), :], (heads, LANES)
            )
            for h in range(kv_heads):
                part = slice(r * heads + h * share, r * heads + (h + 1) * share)
                key = 2 * HEAD * h
                product = lax.dot_general(
                    query,
                    cache[at, r, :, key : key + HEAD],
                    (((1,), (1,)), ((), ())),
                    preferred_element_type=F32,
                )
                a_scores[part, :] = product[h * share : (h + 1) * share]
                a_keys[part, :] = jnp.broadcast_to(new[:, key : key + HEAD], (share, HEAD))
                a_values[part, :] = jnp.broadcast_to(
                    new[:, key + HEAD : key + 2 * HEAD], (share, HEAD)
                )
        lane = lax.broadcasted_iota(jnp.int32, (LANES, LANES), 1).astype(F32)
        scores = jnp.where(lane < a_limits[...], a_scores[...] * HEAD ** (-0.5), -1e30)
        own = jnp.sum(q_rows[ds(b, LANES), :] * a_keys[...], axis=1, keepdims=True) * HEAD ** (-0.5)
        top = jnp.maximum(jnp.max(scores, axis=1, keepdims=True), own)
        weights = jnp.exp(scores - top)
        own_weight = jnp.exp(own - top)
        total = jnp.sum(weights, axis=1, keepdims=True) + own_weight
        a_scores[...] = weights / total
        own_part = (own_weight / total).astype(BF16).astype(F32) * a_values[...]
        a_values[...] = own_part
        for r in range(batch):
            span = slice(r * heads, (r + 1) * heads)
            probs = a_scores[span, :].astype(BF16)
            for h in range(kv_heads):
                part = slice(r * heads + h * share, r * heads + (h + 1) * share)
                value = 2 * HEAD * h + HEAD
                product = jnp.dot(
                    probs, cache[at, r, :, value : value + HEAD], preferred_element_type=F32
                )
                a_rows[pl.ds(pl.multiple_of(b * LANES, LANES) + r * heads + h * share, share), :] = (
                    product[h * share : (h + 1) * share] + a_values[part, :]
                )
        return carry

    att_copy = pltpu.make_async_copy(attended, states_out, misc_sem.at[1])

    batches = rows_dec // batch
    early = batches * 5 // 16

    def attend_start():
        for j in range(heads):
            q_rows[pl.ds(j, rows_dec, stride=heads), :] = queries[
                :, j * HEAD : (j + 1) * HEAD
            ].astype(F32)
        fresh[...] = new_kv[...].astype(F32)
        lengths[...] = spread_rows(cache_lengths[...].astype(F32))

    def attend(low, high):
        @pl.when(g != 0)
        def _():
            if low == 0:
                attend_start()
            lax.fori_loop(low, high, attend_batch, 0)
            if high == batches:
                for j in range(heads):
                    attended[:, j * HEAD : (j + 1) * HEAD] = a_rows[
                        pl.ds(j, rows_dec, stride=heads), :
                    ].astype(BF16)
                att_copy.start()

    finish(0)
    z_start(0, 1)
    for k in far_first:
        if k not in (1, seqs // 2):
            z_start(0, k)
    own_sends(0)
    for c in range(1, chunks):
        text_chunk(c)
    for level in range(levels - 1):
        reduce_level(level)
    z_start(0, seqs // 2)
    for c in range(1, chunks):
        finish(c)
        z_start(c, 1)
        own_sends(c)
    attend(0, early)
    forward(0, 1)
    forward(0, seqs - 1)

    own_rows = ds(g, half_rows)

    def activate(total, t, at):
        total = total + bias_rows[pl.ds(t, 1), :]
        hid[own_rows, at] = (0.5 * total * (1.0 + lax.erf(total * 0.5**0.5))).astype(BF16)

    def gelu_body(t, carry):
        at = ds(t, col_tile)
        p_copy(levels - 1, t).wait()
        activate(p_own[0, :, at] + p_recv[base_at(levels - 1), :, at].astype(F32), t, at)
        return carry

    total = p_own[0, :, first_tile]
    for k in range(1, seqs):
        direct(k).wait()
        total = total + d_recv_buf[k - 1].astype(F32)
    activate(total, 0, first_tile)
    lax.fori_loop(1, col_tiles, gelu_body, 0)
    h_send = remote(hid.at[own_rows, :], hid.at[own_rows, :], send_h, recv_h, group=peer)

    @pl.when(g != 0)
    def _():
        h_send.start()

    for c in range(1, chunks):
        for k in far_first:
            if k not in (1, seqs // 2):
                z_start(c, k)
        forward(c, 1)

    total = jnp.zeros((half_rows, LANES), F32)
    for j in range(feat_local // LANES):
        at = slice(j * LANES, (j + 1) * LANES)
        value = hid[own_rows, at].astype(F32)
        total = total + value * value
        i_scaled[:, at] = (value * gain_rows[j : j + 1, :]).astype(BF16)
    total = jnp.concatenate([total, jnp.zeros((LANES - half_rows, LANES), F32)], axis=0)
    isq_own[...] = jnp.broadcast_to(
        jnp.sum(jnp.transpose(total), axis=0, keepdims=True), isq_own.shape
    )

    def iq_send(k):
        return remote(isq_own, isq_recv.at[k - 1], send_iq.at[k - 1], recv_iq.at[k - 1], mp=mp_at(k))

    for k in range(1, mps):
        iq_send(k).start()
    for c in range(chunks, blocks):
        for q in range(CORES):
            for k in range(chips):
                w_copy(c, q, k).wait()
    for b in range(blocks):
        part = jnp.dot(i_scaled[...], w_buf[b], preferred_element_type=F32)
        i_acc[b] = part[:, :own_cols]
        is1[b] = part[:, own_cols:].astype(BF16)
    i_first = remote(is1, ir1, send_i1, recv_i1, mp=partner)
    i_first.start()

    def i_second(k):
        return remote(
            is2.at[k - 1], ir2.at[k - 1], send_i2.at[k - 1], recv_i2.at[k - 1], mp=chip_at(k)
        )

    i_first.wait()
    for b in range(blocks):
        total = i_acc[b] + ir1[b].astype(F32)
        i_acc[b] = total
        for k in range(1, chips):
            is2[k - 1, b] = total[:, k * LANES : (k + 1) * LANES].astype(BF16)
    for k in range(1, chips):
        i_second(k).start()

    @pl.when(g == 0)
    def _():
        for c in range(chunks):
            take_peer(c)

    for k in range(1, mps):
        iq_send(k).wait()
    squares = isq_own[...]
    for k in range(1, mps):
        squares = squares + isq_recv[k - 1]
    i_scale = spread_rows(lax.rsqrt(squares / width + 1e-05)[:1])[:half_rows]
    for k in range(1, chips):
        i_second(k).wait()
    for b in range(blocks):
        value = i_acc[b, :, :LANES]
        for k in range(1, chips):
            value = value + ir2[k - 1, b].astype(F32)
        ikv[:, pl.ds(pl.multiple_of(columns(b), LANES), LANES)] = (value * i_scale).astype(BF16)

    def img_at(index, half):
        return img_out.at[index, ds(half, half_rows), :]

    def iz_send(k):
        return remote(ikv, img_at(s, g), send_iz.at[k - 1], recv_iz.at[k - 1], seq=flip(s, k))

    iy_send = remote(ikv, img_at(s, g), send_iy, recv_iy, group=peer)
    for k in far_first:
        iz_send(k).start()
    iy_send.start()
    i_local = pltpu.make_async_copy(ikv, img_at(s, g), misc_sem.at[2])
    i_local.start()
    for c in range(1, chunks):
        z_start(c, seqs // 2)
    attend(early, batches)
    for k in far_first:
        if k not in (1, seqs - 1):
            forward(0, k)

    def if_send(k):
        src = flip(s, k)
        return remote(
            img_at(src, 0), img_at(src, 0), send_if.at[k - 1], recv_if.at[k - 1], group=peer
        )


    hid_copy = pltpu.make_async_copy(hid, states_out, misc_sem.at[1])

    @pl.when(g == 0)
    def _():
        h_send.wait_recv()
        hid_copy.start()

    rest = [k for k in far_first if k != 1]

    @pl.when(outer)
    def _():
        for c in range(1, chunks):
            forward(c, rest[0])

    @pl.when(jnp.logical_not(outer))
    def _():
        for c in range(1, chunks):
            for k in reversed(rest):
                forward(c, k)

    for k in far_first:
        iz_send(k).wait_recv()

        @pl.when(g == 0)
        def _():
            if_send(k).start()

    @pl.when(outer)
    def _():
        for c in range(1, chunks):
            for k in rest[1:]:
                forward(c, k)

    for c in range(chunks):
        for k in range(1, seqs):
            for h in range(pieces):
                z_piece(c, k, h).wait_send()
        local(by_owner.at[c], everything, c).wait()

        @pl.when(g == 0)
        def _():
            y_send(by_owner.at[c], everything, c).wait_send()
            local2(c).wait()

        @pl.when(g != 0)
        def _():
            y_send(by_owner.at[c], everything, c).wait_recv()
            k_send(c).wait_send()

    for k in range(1, seqs):
        f_send(k).wait_send()
        d_send(k).wait()
        iz_send(k).wait_send()

        @pl.when(g == 0)
        def _():
            if_send(k).wait_send()

        @pl.when(g != 0)
        def _():
            if_send(k).wait_recv()

    @pl.when(g != 0)
    def _():
        h_send.wait_send()

    iy_send.wait()
    i_local.wait()
    d_local.wait()
    hid_copy.wait()


def prefill(
    mesh_sizes,
    prompt_len,
    embeds,
    image_feats,
    proj_w,
    kv_w,
    kv_cache,
    image_pos,
    bias,
    gain,
    page_owner,
    queries,
    new_kv,
    cache_lengths,
    prompt_lengths,
):
    groups, seqs, mps = mesh_sizes
    chips = mps // CORES
    tokens, feat_local = embeds.shape
    tiles = tokens // TILE
    rows_img, all_channels = image_feats.shape
    half_rows = rows_img // groups
    channels = proj_w.shape[0]
    block_cols = kv_w.shape[1] // mps
    cols = block_cols // groups
    chunks = cols // LANES
    blocks = groups * chunks
    steps = chunks * tiles
    col_tile = min(512, feat_local)
    col_tiles = feat_local // col_tile
    levels = seqs.bit_length() - 1
    pages = page_owner.shape[1]
    page = tokens // pages
    slots = seqs * (2 * pages // seqs)
    rows_dec = queries.shape[0]
    heads = queries.shape[1] // HEAD
    batch = LANES // heads
    dma = pltpu.SemaphoreType.DMA
    vmem = pl.BlockSpec(memory_space=pltpu.VMEM)
    anywhere = pl.BlockSpec(memory_space=pl.ANY)
    dense = tokens // LANES
    return pl.pallas_call(
        functools.partial(prefill_kernel, groups, seqs, mps, prompt_len),
        out_shape=(
            pltpu.VMEM((slots * page, block_cols), BF16),
            pltpu.VMEM((rows_img, feat_local), BF16),
            pltpu.VMEM((seqs, rows_img, block_cols), BF16),
            pltpu.VMEM((seqs, 8, rows_img), F32),
        ),
        in_specs=[anywhere] * 5 + [vmem] * 7 + [pl.BlockSpec(memory_space=pltpu.SMEM)],
        out_specs=(vmem,) * 4,
        scratch_shapes=[
            pltpu.VMEM((feat_local // LANES, LANES), F32),
            pltpu.VMEM((col_tiles, col_tile), F32),
            pltpu.VMEM((slots, pages), BF16),
            pltpu.VMEM((dense, LANES), F32),
            pltpu.VMEM((8, rows_img), F32),
            pltpu.VMEM((half_rows, all_channels), BF16),
            pltpu.VMEM((seqs, half_rows, channels), BF16),
            pltpu.VMEM((tokens, feat_local), BF16),
            pltpu.VMEM((blocks, feat_local, mps * LANES), BF16),
            pltpu.VMEM((channels, feat_local), BF16),
            pltpu.VMEM((seqs, half_rows, channels), BF16),
            pltpu.VMEM((2, TILE, chips * LANES), F32),
            pltpu.VMEM((steps, TILE, chips * LANES), BF16),
            pltpu.VMEM((steps, TILE, chips * LANES), BF16),
            pltpu.VMEM((chunks, tokens, LANES), F32),
            pltpu.VMEM((steps, chips - 1, TILE, LANES), BF16),
            pltpu.VMEM((steps, chips - 1, TILE, LANES), BF16),
            pltpu.VMEM((dense, LANES), F32),
            pltpu.VMEM((mps - 1, dense, LANES), F32),
            pltpu.VMEM((dense, LANES), F32),
            pltpu.VMEM((slots * page, LANES), F32),
            pltpu.VMEM((chunks, slots * page, LANES), BF16),
            pltpu.VMEM((chunks, slots * page, LANES), BF16),
            pltpu.VMEM((chunks, tokens, LANES), BF16),
            pltpu.VMEM((chunks, tokens, LANES), BF16),
            pltpu.VMEM((chunks, slots * page, LANES), BF16),
            pltpu.VMEM((seqs // 2, half_rows, feat_local), F32),
            pltpu.VMEM((seqs - 1, half_rows, feat_local), BF16),
            pltpu.VMEM((seqs - 1, half_rows, feat_local), BF16),
            pltpu.VMEM((seqs - 1, half_rows, col_tile), BF16),
            pltpu.VMEM((seqs - 1, half_rows, col_tile), BF16),
            pltpu.VMEM((rows_img, feat_local), BF16),
            pltpu.VMEM((half_rows, feat_local), BF16),
            pltpu.VMEM((blocks, half_rows, chips * LANES), F32),
            pltpu.VMEM((blocks, half_rows, chips * LANES), BF16),
            pltpu.VMEM((blocks, half_rows, chips * LANES), BF16),
            pltpu.VMEM((chips - 1, blocks, half_rows, LANES), BF16),
            pltpu.VMEM((chips - 1, blocks, half_rows, LANES), BF16),
            pltpu.VMEM((8, LANES), F32),
            pltpu.VMEM((mps - 1, 8, LANES), F32),
            pltpu.VMEM((half_rows, block_cols), BF16),
            pltpu.VMEM((rows_dec * heads, HEAD), F32),
            pltpu.VMEM(new_kv.shape, F32),
            pltpu.VMEM((rows_dec, LANES), F32),
            pltpu.VMEM((2, batch) + kv_cache.shape[1:], BF16),
            pltpu.VMEM((LANES, LANES), F32),
            pltpu.VMEM((LANES, LANES), F32),
            pltpu.VMEM((LANES, LANES), F32),
            pltpu.VMEM((LANES, LANES), F32),
            pltpu.VMEM((rows_dec * heads, HEAD), F32),
            pltpu.VMEM(queries.shape, BF16),
            dma((1,)),
            dma((2,)),
            dma((blocks, mps)),
            dma((tiles,)),
            dma,
            dma,
            dma((steps,)),
            dma((steps,)),
            dma((steps, chips - 1)),
            dma((steps, chips - 1)),
            dma((mps - 1,)),
            dma((mps - 1,)),
            dma((seqs - 1,)),
            dma((seqs - 1,)),
            dma((seqs - 1,)),
            dma((seqs - 1,)),
            dma((levels, col_tiles)),
            dma((levels, col_tiles)),
            dma((seqs - 1,)),
            dma((seqs - 1,)),
            dma,
            dma,
            dma,
            dma,
            dma((chips - 1,)),
            dma((chips - 1,)),
            dma((mps - 1,)),
            dma((mps - 1,)),
            dma((chunks, PIECES * (seqs - 1))),
            dma((chunks, PIECES * (seqs - 1))),
            dma((chunks,)),
            dma((chunks,)),
            dma((chunks,)),
            dma((chunks,)),
            dma((chunks,)),
            dma((chunks,)),
            dma((seqs - 1,)),
            dma((seqs - 1,)),
            dma,
            dma,
            dma((seqs - 1,)),
            dma((seqs - 1,)),
            dma((seqs - 1,)),
            dma((seqs - 1,)),
            dma((3,)),
        ],
        compiler_params=pltpu.CompilerParams(
            collective_id=0, has_side_effects=True, vmem_limit_bytes=57 * 1024 * 1024
        ),
        name="prefill_pages",
    )(
        embeds,
        image_feats,
        proj_w,
        kv_w,
        kv_cache,
        image_pos,
        bias,
        gain,
        page_owner,
        queries,
        new_kv,
        cache_lengths,
        prompt_lengths,
    )


def place_kernel(index, offset, text, img, dest, states, out, states_out, rows, sems):
    parts = index.shape[0]
    block = text.shape[0] // parts

    def store(b):
        span = pl.ds(b * block, block)
        return pltpu.make_async_copy(rows.at[span, :], out.at[span, :], sems.at[b])

    for b in range(parts):
        spots = dest[index[b]][:1].astype(jnp.int32) - offset[b]
        hit = lax.broadcasted_iota(jnp.int32, (block, dest.shape[2]), 0) == spots
        placed = jnp.dot(
            jnp.where(hit, 1.0, 0.0).astype(BF16), img[index[b]], preferred_element_type=F32
        )
        span = pl.ds(b * block, block)
        rows[span, :] = text[span, :] + placed.astype(BF16)
        store(b).start()
    state_store = pltpu.make_async_copy(states, states_out, sems.at[parts])
    state_store.start()
    for b in range(parts):
        store(b).wait()
    state_store.wait()


def place(index, offset, text, img, dest, states):
    parts = index.shape[0]
    smem = pl.BlockSpec(memory_space=pltpu.SMEM)
    vmem = pl.BlockSpec(memory_space=pltpu.VMEM)
    anywhere = pl.BlockSpec(memory_space=pl.ANY)
    near = [pltpu.with_memory_space_constraint(x, pltpu.VMEM) for x in (text, img, dest, states)]
    return pl.pallas_call(
        place_kernel,
        out_shape=(
            jax.ShapeDtypeStruct(text.shape, text.dtype),
            jax.ShapeDtypeStruct(states.shape, states.dtype),
        ),
        in_specs=[smem, smem, vmem, vmem, vmem, vmem],
        out_specs=(anywhere, anywhere),
        scratch_shapes=[
            pltpu.VMEM(text.shape, text.dtype),
            pltpu.SemaphoreType.DMA((parts + 1,)),
        ],
        compiler_params=pltpu.CompilerParams(vmem_limit_bytes=16 * 1024 * 1024),
        name="place_images",
    )(index, offset, *near)


def per_device(
    mesh_sizes,
    embeds,
    image_feats,
    image_pos,
    proj_w,
    proj_b,
    norm_gain,
    kv_w,
    prompt_lengths,
    page_owner,
    queries,
    kv_cache,
    new_kv,
    cache_lengths,
):
    groups, seqs, mps = mesh_sizes
    group_index = lax.axis_index("group")
    prefill_side = group_index == 0
    seq_index = lax.axis_index("seq")
    token_rows, width_local = embeds.shape
    prompt_len = token_rows * seqs // prompt_lengths.shape[0]
    page = token_rows // page_owner.shape[0]
    capacity = 2 * page_owner.shape[0] // seqs
    text, row_states, img, dest_all = prefill(
        mesh_sizes,
        prompt_len,
        embeds,
        image_feats,
        proj_w,
        kv_w,
        kv_cache,
        image_pos[None, :],
        proj_b.reshape(-1, LANES),
        norm_gain.reshape(-1, LANES),
        page_owner.reshape(1, -1),
        queries,
        new_kv,
        cache_lengths[None, :],
        prompt_lengths,
    )
    parts = max(1, 8 // seqs)
    order = jnp.arange(seqs * parts, dtype=jnp.int32)
    source, part = order // parts, order % parts
    index = jnp.where(prefill_side, seq_index, source)
    offset = jnp.where(prefill_side, source, seq_index) * (capacity * page)
    offset = offset + part * (capacity * page // parts)
    page_slots, row_states = place(index, offset, text, img, dest_all, row_states)
    page_slots = page_slots.reshape(-1, page, text.shape[1])
    return (page_slots, row_states)


def solution(mesh):
    mesh_sizes = (mesh.shape["group"], mesh.shape["seq"], mesh.shape["mp"])
    in_specs = (
        P("seq", "mp"),
        P("seq", None),
        P("seq"),
        P("seq", "mp"),
        P("mp"),
        P("mp"),
        P("mp", None),
        P(),
        P("seq", None),
        P("seq", "mp"),
        P("seq", None, "mp"),
        P("seq", "mp"),
        P("seq"),
    )
    out_specs = (P(("group", "seq"), None, "mp"), P(("group", "seq"), "mp"))
    return jax.shard_map(
        functools.partial(per_device, mesh_sizes),
        mesh=mesh,
        in_specs=in_specs,
        out_specs=out_specs,
        check_vma=False,
    )
```

```python
import functools

import jax
import jax.numpy as jnp
from jax import lax
from jax.experimental import pallas as pl
from jax.experimental.pallas import tpu as pltpu
from jax.sharding import PartitionSpec as P

HEAD = 128
LANES = 128
TILE = 256
CORES = 2
PIECES = 4
MESH = pl.DeviceIdType.MESH
F32 = jnp.float32
BF16 = jnp.bfloat16


def ds(index, size):
    return pl.ds(pl.multiple_of(index * size, size), size)


def flip(index, distance):
    result = index
    bit = 1
    while bit <= distance:
        if distance & bit:
            result = result + bit - 2 * bit * lax.rem(index // bit, 2)
        bit *= 2
    return result


def spread_rows(row):
    return jnp.transpose(jnp.broadcast_to(row, (LANES, LANES)))


def prefill_kernel(
    groups,
    seqs,
    mps,
    prompt_len,
    embeds,
    image_feats,
    proj_w,
    kv_w,
    kv_cache,
    image_pos,
    bias,
    gain,
    page_owner,
    queries,
    new_kv,
    cache_lengths,
    prompt_lengths,
    slots_out,
    states_out,
    img_out,
    dest_out,
    gain_rows,
    bias_rows,
    sel,
    mask,
    dest,
    f_rows,
    feats,
    e_buf,
    w_buf,
    pw_buf,
    f_buf,
    acc1,
    s1,
    r1,
    acc2,
    s2,
    r2,
    sq_own,
    sq_recv,
    scale,
    outf,
    by_owner,
    arrived,
    kv_send,
    kv_recv,
    by_peer,
    p_own,
    p_send,
    p_recv,
    d_send_buf,
    d_recv_buf,
    hid,
    i_scaled,
    i_acc,
    is1,
    ir1,
    is2,
    ir2,
    isq_own,
    isq_recv,
    ikv,
    q_rows,
    fresh,
    lengths,
    cache,
    a_scores,
    a_keys,
    a_values,
    a_limits,
    a_rows,
    attended,
    load_sem,
    cache_sem,
    w_sem,
    e_sem,
    pw_sem,
    fl_sem,
    send1,
    recv1,
    send2,
    recv2,
    send_sq,
    recv_sq,
    send_f,
    recv_f,
    send_fc,
    recv_fc,
    send_r,
    recv_r,
    send_dr,
    recv_dr,
    send_h,
    recv_h,
    send_i1,
    recv_i1,
    send_i2,
    recv_i2,
    send_iq,
    recv_iq,
    send_z,
    recv_z,
    send_y,
    recv_y,
    send_k,
    recv_k,
    loc_sem,
    loc2_sem,
    send_iz,
    recv_iz,
    send_iy,
    recv_iy,
    send_if,
    recv_if,
    send_d,
    recv_d,
    misc_sem,
):
    g = lax.axis_index("group")
    s = lax.axis_index("seq")
    m = lax.axis_index("mp")
    chips = mps // CORES
    chip = m // CORES
    core = m % CORES
    partner = chip * CORES + (1 - core)
    peer = 1 - g
    blocks, feat_local, _ = w_buf.shape
    chunks = blocks // groups
    tokens = e_buf.shape[0]
    tiles = tokens // TILE
    steps = chunks * tiles
    col_tile = min(512, feat_local)
    col_tiles = feat_local // col_tile
    rows_img = hid.shape[0]
    half_rows = rows_img // groups
    core_rows = half_rows // CORES
    cols = chunks * LANES
    block_cols = cols * groups
    slots, pages = sel.shape
    page = tokens // pages
    capacity = slots // seqs
    width = feat_local * mps
    channels = feats.shape[2]
    block = slots * page // seqs
    own_cols = chips * LANES

    def remote(src, dst, send, recv, **where):
        return pltpu.make_async_remote_copy(
            src_ref=src,
            dst_ref=dst,
            send_sem=send,
            recv_sem=recv,
            device_id=where,
            device_id_type=MESH,
        )

    def seq_at(k):
        return lax.rem(s + k, seqs)

    def mp_at(k):
        return lax.rem(m + k, mps)

    def chip_at(k):
        return lax.rem(chip + k, chips) * CORES + core

    def e_copy(i):
        return pltpu.make_async_copy(embeds.at[ds(i, TILE), :], e_buf.at[ds(i, TILE), :], e_sem.at[i])

    def half_at(b):
        return lax.rem(g + b // chunks, groups)

    def columns(b):
        return half_at(b) * cols + b % chunks * LANES

    def w_copy(c, q, k):
        target = lax.rem(chip + k, chips) * CORES + (core if q == 0 else 1 - core)
        start = target * block_cols + columns(c)
        return pltpu.make_async_copy(
            kv_w.at[:, pl.ds(pl.multiple_of(start, LANES), LANES)],
            w_buf.at[c, :, (q * chips + k) * LANES : (q * chips + k + 1) * LANES],
            w_sem.at[c, q * chips + k],
        )

    f_load = pltpu.make_async_copy(image_feats.at[ds(g, half_rows), :], f_rows, load_sem.at[0])
    f_load.start()
    barrier = pltpu.get_barrier_semaphore()
    for k in range(1, seqs):
        pl.semaphore_signal(barrier, inc=1, device_id={"seq": seq_at(k)}, device_id_type=MESH)
    for k in range(1, mps):
        pl.semaphore_signal(barrier, inc=1, device_id={"mp": mp_at(k)}, device_id_type=MESH)
    pl.semaphore_signal(barrier, inc=1, device_id={"group": peer}, device_id_type=MESH)
    e_copy(0).start()
    for q in range(CORES):
        for k in range(chips):
            w_copy(0, q, k).start()
    cache_first = pltpu.make_async_copy(
        kv_cache.at[pl.ds(0, LANES // (queries.shape[1] // HEAD))], cache.at[0], cache_sem.at[0]
    )
    pw_copy = pltpu.make_async_copy(proj_w, pw_buf, pw_sem)

    def later_loads():
        pw_copy.start()
        for c in range(1, blocks):
            for q in range(CORES):
                for k in range(chips):
                    w_copy(c, q, k).start()

        @pl.when(g != 0)
        def _():
            cache_first.start()


    f_load.wait()
    for i in range(1, tiles):
        e_copy(i).start()
    for b in range(seqs):
        feats[b] = f_rows[:, b * channels : (b + 1) * channels]
    own_feats = pltpu.make_async_copy(feats.at[s], f_buf.at[0], fl_sem)
    own_feats.start()

    pl.semaphore_wait(barrier, seqs - 1 + mps - 1 + 1)

    def f_send(k):
        rows = ds(core, core_rows)
        return remote(
            feats.at[flip(s, k), rows, :],
            f_buf.at[k, rows, :],
            send_f.at[k - 1],
            recv_f.at[k - 1],
            seq=flip(s, k),
        )

    def f_share(k):
        rows = ds(core, core_rows)
        return remote(
            f_buf.at[k, rows, :],
            f_buf.at[k, rows, :],
            send_fc.at[k - 1],
            recv_fc.at[k - 1],
            mp=partner,
        )

    def d_send(k):
        return remote(dest, dest_out.at[s], send_d.at[k - 1], recv_d.at[k - 1], seq=seq_at(k))

    for k in range(1, seqs):
        f_send(k).start()

    gain_rows[...] = gain[...].astype(F32)
    biases = bias[...].astype(F32)
    for j in range(feat_local // LANES):
        t, within = divmod(j, col_tile // LANES)
        bias_rows[t : t + 1, within * LANES : (within + 1) * LANES] = biases[j : j + 1, :]

    prompt = (s * tokens) // prompt_len
    limit = prompt_lengths[prompt]
    base = s * tokens - prompt * prompt_len
    spots = image_pos[...] - s * tokens
    down = lax.broadcasted_iota(jnp.int32, (pages, LANES), 0)
    across = lax.broadcasted_iota(jnp.int32, (pages, LANES), 1)
    owner_across = jnp.broadcast_to(page_owner[...].astype(F32), (pages, LANES))
    owner_down = jnp.transpose(owner_across)
    rank = jnp.sum(
        jnp.where((owner_down == owner_across) & (down < across), 1.0, 0.0), axis=0, keepdims=True
    )
    slot = owner_across[:1] * capacity + rank
    slot_rows = lax.broadcasted_iota(jnp.int32, (slots, LANES), 0).astype(F32)
    sel[...] = jnp.where(slot_rows == slot, 1.0, 0.0).astype(BF16)
    page_bits = page.bit_length() - 1
    on_page = down == lax.shift_right_logical(spots, page_bits)
    image_slot = jnp.sum(jnp.where(on_page, spread_rows(slot), 0.0), axis=0, keepdims=True)
    image_row = image_slot * page + (spots & (page - 1)).astype(F32)
    dest[...] = jnp.broadcast_to(
        jnp.where(spots + base < limit, image_row, -1048576.0), dest.shape
    )
    dense = mask.shape[0]
    tall = lax.broadcasted_iota(jnp.int32, (dense, LANES), 0)
    image_block = jnp.where(tall == lax.shift_right_logical(spots, 7), 1.0, 0.0)
    image_lane = jnp.where(down == (spots & (LANES - 1)), 1.0, 0.0)
    images = lax.dot_general(
        image_block.astype(BF16),
        image_lane.astype(BF16),
        (((1,), (1,)), ((), ())),
        preferred_element_type=F32,
    )
    token = tall * LANES + lax.broadcasted_iota(jnp.int32, (dense, LANES), 1)
    mask[...] = jnp.where((token + base < limit) & (images < 0.5), 1.0, 0.0)
    for k in range(1, seqs):
        d_send(k).start()
    d_local = pltpu.make_async_copy(dest, dest_out.at[s], misc_sem.at[0])
    d_local.start()

    def first(n):
        return remote(s1.at[n], r1.at[n], send1.at[n], recv1.at[n], mp=partner)

    def second(n, k):
        return remote(
            s2.at[n, k - 1], r2.at[n, k - 1], send2.at[n, k - 1], recv2.at[n, k - 1], mp=chip_at(k)
        )

    def sq_send(k):
        return remote(sq_own, sq_recv.at[k - 1], send_sq.at[k - 1], recv_sq.at[k - 1], mp=mp_at(k))

    far_first = range(seqs - 1, 0, -1)
    outer = lax.rem(s, 2) == lax.rem(s // 2, 2)

    levels = seqs.bit_length() - 1

    def sent_at(level):
        step_size = 2 << level
        return list(range(1 << level, seqs, step_size))

    def kept_at(level):
        step_size = 2 << level
        return list(range(0, seqs, step_size))

    def base_at(level):
        return seqs - (seqs >> level)

    def p_copy(level, t):
        span = pl.ds(base_at(level), len(sent_at(level)))
        at = ds(t, col_tile)
        return remote(
            p_send.at[span, :, at],
            p_recv.at[span, :, at],
            send_r.at[level, t],
            recv_r.at[level, t],
            seq=flip(s, 1 << level),
        )

    first_tile = slice(0, col_tile)

    def direct(k):
        return remote(
            d_send_buf.at[k - 1],
            d_recv_buf.at[k - 1],
            send_dr.at[k - 1],
            recv_dr.at[k - 1],
            seq=flip(s, k),
        )

    def scale_tile(i):
        e_copy(i).wait()

        def body(b, carry):
            rows = ds(i * (TILE // LANES) + b, LANES)
            total = jnp.zeros((LANES, LANES), F32)
            for j in range(feat_local // LANES):
                at = slice(j * LANES, (j + 1) * LANES)
                value = e_buf[rows, at].astype(F32)
                total = total + value * value
                e_buf[rows, at] = e_buf[rows, at] * gain_rows[j : j + 1, :].astype(BF16)
            sq_own[pl.ds(i * (TILE // LANES) + b, 1), :] = jnp.sum(
                jnp.transpose(total), axis=0, keepdims=True
            )
            return carry

        lax.fori_loop(0, TILE // LANES, body, 0)

    def project():
        for k in range(1, seqs):
            f_share(k).wait()
        own_feats.wait()
        pw_copy.wait()
        spread = f_buf[...].reshape(seqs * half_rows, channels)

        def tile(at):
            out = jnp.dot(spread, pw_buf[:, at], preferred_element_type=F32)
            return out.reshape(seqs, half_rows, col_tile)

        out = tile(first_tile)
        for k in far_first:
            d_send_buf[k - 1] = out[k].astype(BF16)
            direct(k).start()
        p_own[0, :, first_tile] = out[0]

        def body(t, carry):
            at = ds(t, col_tile)
            out = tile(at)
            for slot_at, e in enumerate(sent_at(0)):
                p_send[slot_at, :, at] = out[e].astype(BF16)
            p_copy(0, t).start()
            for slot_at, e in enumerate(kept_at(0)):
                p_own[slot_at, :, at] = out[e]
            return carry

        lax.fori_loop(1, col_tiles, body, 0)

    def reduce_level(level):
        def body(t, carry):
            at = ds(t, col_tile)
            p_copy(level, t).wait()
            for index in range(len(kept_at(level))):
                total = p_own[index, :, at] + p_recv[base_at(level) + index, :, at].astype(F32)
                if index % 2 == 0:
                    p_own[index // 2, :, at] = total
                else:
                    p_send[base_at(level + 1) + index // 2, :, at] = total.astype(BF16)
            p_copy(level + 1, t).start()
            return carry

        lax.fori_loop(1, col_tiles, body, 0)

    def combine(p):
        c, i = p // tiles, lax.rem(p, tiles)
        first(p).wait()
        total = acc1[lax.rem(p, 2)] + r1[p].astype(F32)
        acc2[c, ds(i, TILE), :] = total[:, :LANES]
        for k in range(1, chips):
            s2[p, k - 1] = total[:, k * LANES : (k + 1) * LANES].astype(BF16)
            second(p, k).start()

    def multiply(n, c, i):
        part = jnp.dot(e_buf[ds(i, TILE), :], w_buf[c], preferred_element_type=F32)
        acc1[lax.rem(n, 2)] = part[:, :own_cols]
        s1[n] = part[:, own_cols:].astype(BF16)
        first(n).start()

    def text_chunk(c):
        for q in range(CORES):
            for k in range(chips):
                w_copy(c, q, k).wait()

        def body(i, carry):
            if c == 0:
                scale_tile(i)

                @pl.when(i == tiles // 2)
                def _():
                    later_loads()

            multiply(c * tiles + i, c, i)

            @pl.when(i > 0)
            def _():
                combine(c * tiles + i - 1)

            return carry

        lax.fori_loop(0, tiles, body, 0)
        if c == 0:
            for k in range(1, mps):
                sq_send(k).start()
        combine(c * tiles + tiles - 1)

    text_chunk(0)
    for k in range(1, seqs):
        f_send(k).wait_recv()
        f_share(k).start()
    project()

    for k in range(1, mps):
        sq_send(k).wait()
    squares = sq_own[...]
    for k in range(1, mps):
        squares = squares + sq_recv[k - 1]
    scale[...] = mask[...] * lax.rsqrt(squares / width + 1e-05)

    pieces = PIECES
    piece = block // pieces

    def z_piece(c, k, h):
        return remote(
            by_owner.at[c, ds(flip(s, k) * pieces + h, piece), :],
            arrived.at[c, ds(s * pieces + h, piece), :],
            send_z.at[c, (k - 1) * pieces + h],
            recv_z.at[c, (k - 1) * pieces + h],
            seq=flip(s, k),
        )

    def z_start(c, k):
        for h in range(pieces):
            z_piece(c, k, h).start()

    def out_at(rows, half, c):
        at = pl.ds(pl.multiple_of(half * cols + c * LANES, LANES), LANES)
        return slots_out.at[rows, at]

    def y_send(src, rows, c):
        return remote(src, out_at(rows, g, c), send_y.at[c], recv_y.at[c], group=peer)

    def local(src, rows, c):
        return pltpu.make_async_copy(src, out_at(rows, g, c), loc_sem.at[c])

    everything = pl.ds(0, slots * page)

    def select(c, target):
        chosen = sel[...]
        for t in range(page):
            rows = acc2[c, pl.ds(t, pages, stride=page), :].astype(BF16)
            outf[pl.ds(t, slots, stride=page), :] = jnp.dot(
                chosen, rows, preferred_element_type=F32
            )
        target[c] = outf[...].astype(BF16)

    def k_send(c):
        return remote(kv_send.at[c], kv_recv.at[c], send_k.at[c], recv_k.at[c], group=peer)

    def local2(c):
        return pltpu.make_async_copy(
            by_peer.at[c], out_at(everything, 1 - g, c), loc2_sem.at[c]
        )

    def finish(c):
        def body(i, carry):
            n = c * tiles + i
            for k in range(1, chips):
                second(n, k).wait()
            for b in range(TILE // LANES):
                rows = pl.ds(pl.multiple_of(i * TILE + b * LANES, LANES), LANES)
                within = pl.ds(b * LANES, LANES)
                value = acc2[c, rows, :]
                for k in range(1, chips):
                    value = value + r2[n, k - 1, within, :].astype(F32)
                value = value * spread_rows(scale[pl.ds(i * (TILE // LANES) + b, 1), :])
                acc2[c, rows, :] = value
                kv_send[c, rows, :] = value.astype(BF16)
            return carry

        lax.fori_loop(0, tiles, body, 0)
        select(c, by_owner)

    def own_sends(c):
        mine = ds(s, block)

        @pl.when(g == 0)
        def _():
            y_send(by_owner.at[c, mine, :], mine, c).start()
            local(by_owner.at[c], everything, c).start()

        @pl.when(g != 0)
        def _():
            k_send(c).start()
            local(by_owner.at[c, mine, :], mine, c).start()

    def take_peer(c):
        k_send(c).wait_recv()
        acc2[c] = kv_recv[c].astype(F32)
        select(c, by_peer)
        local2(c).start()

    def forward(c, k):
        for h in range(pieces):
            z_piece(c, k, h).wait_recv()
            rows = ds(flip(s, k) * pieces + h, piece)

            @pl.when(g == 0)
            def _():
                y_send(arrived.at[c, rows, :], rows, c).start()

            @pl.when(g != 0)
            def _():
                local(arrived.at[c, rows, :], rows, c).start()

    heads = queries.shape[1] // HEAD
    kv_heads = kv_cache.shape[2] // (2 * HEAD)
    share = heads // kv_heads
    rows_dec = queries.shape[0]
    batch = LANES // heads

    def cache_copy(b):
        return pltpu.make_async_copy(
            kv_cache.at[ds(b, batch)], cache.at[lax.rem(b, 2)], cache_sem.at[lax.rem(b, 2)]
        )

    def attend_batch(b, carry):
        cache_copy(b).wait()

        @pl.when(b + 1 < rows_dec // batch)
        def _():
            cache_copy(b + 1).start()

        at = lax.rem(b, 2)
        for r in range(batch):
            span = slice(r * heads, (r + 1) * heads)
            query = q_rows[pl.ds(pl.multiple_of(b * LANES + r * heads, 8), heads), :].astype(BF16)
            new = fresh[pl.ds(b * batch + r, 1), :]
            a_limits[span, :] = jnp.broadcast_to(
                lengths[pl.ds(b * batch + r, 1), :], (heads, LANES)
            )
            for h in range(kv_heads):
                part = slice(r * heads + h * share, r * heads + (h + 1) * share)
                key = 2 * HEAD * h
                product = lax.dot_general(
                    query,
                    cache[at, r, :, key : key + HEAD],
                    (((1,), (1,)), ((), ())),
                    preferred_element_type=F32,
                )
                a_scores[part, :] = product[h * share : (h + 1) * share]
                a_keys[part, :] = jnp.broadcast_to(new[:, key : key + HEAD], (share, HEAD))
                a_values[part, :] = jnp.broadcast_to(
                    new[:, key + HEAD : key + 2 * HEAD], (share, HEAD)
                )
        lane = lax.broadcasted_iota(jnp.int32, (LANES, LANES), 1).astype(F32)
        scores = jnp.where(lane < a_limits[...], a_scores[...] * HEAD ** (-0.5), -1e30)
        own = jnp.sum(q_rows[ds(b, LANES), :] * a_keys[...], axis=1, keepdims=True) * HEAD ** (-0.5)
        top = jnp.maximum(jnp.max(scores, axis=1, keepdims=True), own)
        weights = jnp.exp(scores - top)
        own_weight = jnp.exp(own - top)
        total = jnp.sum(weights, axis=1, keepdims=True) + own_weight
        a_scores[...] = weights / total
        own_part = (own_weight / total).astype(BF16).astype(F32) * a_values[...]
        a_values[...] = own_part
        for r in range(batch):
            span = slice(r * heads, (r + 1) * heads)
            probs = a_scores[span, :].astype(BF16)
            for h in range(kv_heads):
                part = slice(r * heads + h * share, r * heads + (h + 1) * share)
                value = 2 * HEAD * h + HEAD
                product = jnp.dot(
                    probs, cache[at, r, :, value : value + HEAD], preferred_element_type=F32
                )
                a_rows[pl.ds(pl.multiple_of(b * LANES, LANES) + r * heads + h * share, share), :] = (
                    product[h * share : (h + 1) * share] + a_values[part, :]
                )
        return carry

    att_copy = pltpu.make_async_copy(attended, states_out, misc_sem.at[1])

    batches = rows_dec // batch
    early = batches * 5 // 16

    def attend_start():
        for j in range(heads):
            q_rows[pl.ds(j, rows_dec, stride=heads), :] = queries[
                :, j * HEAD : (j + 1) * HEAD
            ].astype(F32)
        fresh[...] = new_kv[...].astype(F32)
        lengths[...] = spread_rows(cache_lengths[...].astype(F32))

    def attend(low, high):
        @pl.when(g != 0)
        def _():
            if low == 0:
                attend_start()
            lax.fori_loop(low, high, attend_batch, 0)
            if high == batches:
                for j in range(heads):
                    attended[:, j * HEAD : (j + 1) * HEAD] = a_rows[
                        pl.ds(j, rows_dec, stride=heads), :
                    ].astype(BF16)
                att_copy.start()

    finish(0)
    z_start(0, 1)
    for k in far_first:
        if k not in (1, seqs // 2):
            z_start(0, k)
    own_sends(0)
    for c in range(1, chunks):
        text_chunk(c)
    for level in range(levels - 1):
        reduce_level(level)
    z_start(0, seqs // 2)
    for c in range(1, chunks):
        finish(c)
        z_start(c, 1)
        own_sends(c)
    attend(0, early)
    forward(0, 1)
    forward(0, seqs - 1)

    own_rows = ds(g, half_rows)

    def activate(total, t, at):
        total = total + bias_rows[pl.ds(t, 1), :]
        hid[own_rows, at] = (0.5 * total * (1.0 + lax.erf(total * 0.5**0.5))).astype(BF16)

    def gelu_body(t, carry):
        at = ds(t, col_tile)
        p_copy(levels - 1, t).wait()
        activate(p_own[0, :, at] + p_recv[base_at(levels - 1), :, at].astype(F32), t, at)
        return carry

    total = p_own[0, :, first_tile]
    for k in range(1, seqs):
        direct(k).wait()
        total = total + d_recv_buf[k - 1].astype(F32)
    activate(total, 0, first_tile)
    lax.fori_loop(1, col_tiles, gelu_body, 0)
    h_send = remote(hid.at[own_rows, :], hid.at[own_rows, :], send_h, recv_h, group=peer)

    @pl.when(g != 0)
    def _():
        h_send.start()

    for c in range(1, chunks):
        for k in far_first:
            if k not in (1, seqs // 2):
                z_start(c, k)
        forward(c, 1)

    total = jnp.zeros((half_rows, LANES), F32)
    for j in range(feat_local // LANES):
        at = slice(j * LANES, (j + 1) * LANES)
        value = hid[own_rows, at].astype(F32)
        total = total + value * value
        i_scaled[:, at] = (value * gain_rows[j : j + 1, :]).astype(BF16)
    total = jnp.concatenate([total, jnp.zeros((LANES - half_rows, LANES), F32)], axis=0)
    isq_own[...] = jnp.broadcast_to(
        jnp.sum(jnp.transpose(total), axis=0, keepdims=True), isq_own.shape
    )

    def iq_send(k):
        return remote(isq_own, isq_recv.at[k - 1], send_iq.at[k - 1], recv_iq.at[k - 1], mp=mp_at(k))

    for k in range(1, mps):
        iq_send(k).start()
    for c in range(chunks, blocks):
        for q in range(CORES):
            for k in range(chips):
                w_copy(c, q, k).wait()
    for b in range(blocks):
        part = jnp.dot(i_scaled[...], w_buf[b], preferred_element_type=F32)
        i_acc[b] = part[:, :own_cols]
        is1[b] = part[:, own_cols:].astype(BF16)
    i_first = remote(is1, ir1, send_i1, recv_i1, mp=partner)
    i_first.start()

    def i_second(k):
        return remote(
            is2.at[k - 1], ir2.at[k - 1], send_i2.at[k - 1], recv_i2.at[k - 1], mp=chip_at(k)
        )

    i_first.wait()
    for b in range(blocks):
        total = i_acc[b] + ir1[b].astype(F32)
        i_acc[b] = total
        for k in range(1, chips):
            is2[k - 1, b] = total[:, k * LANES : (k + 1) * LANES].astype(BF16)
    for k in range(1, chips):
        i_second(k).start()

    @pl.when(g == 0)
    def _():
        for c in range(chunks):
            take_peer(c)

    for k in range(1, mps):
        iq_send(k).wait()
    squares = isq_own[...]
    for k in range(1, mps):
        squares = squares + isq_recv[k - 1]
    i_scale = spread_rows(lax.rsqrt(squares / width + 1e-05)[:1])[:half_rows]
    for k in range(1, chips):
        i_second(k).wait()
    for b in range(blocks):
        value = i_acc[b, :, :LANES]
        for k in range(1, chips):
            value = value + ir2[k - 1, b].astype(F32)
        ikv[:, pl.ds(pl.multiple_of(columns(b), LANES), LANES)] = (value * i_scale).astype(BF16)

    def img_at(index, half):
        return img_out.at[index, ds(half, half_rows), :]

    def iz_send(k):
        return remote(ikv, img_at(s, g), send_iz.at[k - 1], recv_iz.at[k - 1], seq=flip(s, k))

    iy_send = remote(ikv, img_at(s, g), send_iy, recv_iy, group=peer)
    for k in far_first:
        iz_send(k).start()
    iy_send.start()
    i_local = pltpu.make_async_copy(ikv, img_at(s, g), misc_sem.at[2])
    i_local.start()
    for c in range(1, chunks):
        z_start(c, seqs // 2)
    attend(early, batches)
    for k in far_first:
        if k not in (1, seqs - 1):
            forward(0, k)

    def if_send(k):
        src = flip(s, k)
        return remote(
            img_at(src, 0), img_at(src, 0), send_if.at[k - 1], recv_if.at[k - 1], group=peer
        )


    hid_copy = pltpu.make_async_copy(hid, states_out, misc_sem.at[1])

    @pl.when(g == 0)
    def _():
        h_send.wait_recv()
        hid_copy.start()

    rest = [k for k in far_first if k != 1]

    @pl.when(outer)
    def _():
        for c in range(1, chunks):
            forward(c, rest[0])

    @pl.when(jnp.logical_not(outer))
    def _():
        for c in range(1, chunks):
            for k in reversed(rest):
                forward(c, k)

    for k in far_first:
        iz_send(k).wait_recv()

        @pl.when(g == 0)
        def _():
            if_send(k).start()

    @pl.when(outer)
    def _():
        for c in range(1, chunks):
            for k in rest[1:]:
                forward(c, k)

    for c in range(chunks):
        for k in range(1, seqs):
            for h in range(pieces):
                z_piece(c, k, h).wait_send()
        local(by_owner.at[c], everything, c).wait()

        @pl.when(g == 0)
        def _():
            y_send(by_owner.at[c], everything, c).wait_send()
            local2(c).wait()

        @pl.when(g != 0)
        def _():
            y_send(by_owner.at[c], everything, c).wait_recv()
            k_send(c).wait_send()

    for k in range(1, seqs):
        f_send(k).wait_send()
        d_send(k).wait()
        iz_send(k).wait_send()

        @pl.when(g == 0)
        def _():
            if_send(k).wait_send()

        @pl.when(g != 0)
        def _():
            if_send(k).wait_recv()

    @pl.when(g != 0)
    def _():
        h_send.wait_send()

    iy_send.wait()
    i_local.wait()
    d_local.wait()
    hid_copy.wait()


def prefill(
    mesh_sizes,
    prompt_len,
    embeds,
    image_feats,
    proj_w,
    kv_w,
    kv_cache,
    image_pos,
    bias,
    gain,
    page_owner,
    queries,
    new_kv,
    cache_lengths,
    prompt_lengths,
):
    groups, seqs, mps = mesh_sizes
    chips = mps // CORES
    tokens, feat_local = embeds.shape
    tiles = tokens // TILE
    rows_img, all_channels = image_feats.shape
    half_rows = rows_img // groups
    channels = proj_w.shape[0]
    block_cols = kv_w.shape[1] // mps
    cols = block_cols // groups
    chunks = cols // LANES
    blocks = groups * chunks
    steps = chunks * tiles
    col_tile = min(512, feat_local)
    col_tiles = feat_local // col_tile
    levels = seqs.bit_length() - 1
    pages = page_owner.shape[1]
    page = tokens // pages
    slots = seqs * (2 * pages // seqs)
    rows_dec = queries.shape[0]
    heads = queries.shape[1] // HEAD
    batch = LANES // heads
    dma = pltpu.SemaphoreType.DMA
    vmem = pl.BlockSpec(memory_space=pltpu.VMEM)
    anywhere = pl.BlockSpec(memory_space=pl.ANY)
    dense = tokens // LANES
    return pl.pallas_call(
        functools.partial(prefill_kernel, groups, seqs, mps, prompt_len),
        out_shape=(
            pltpu.VMEM((slots * page, block_cols), BF16),
            pltpu.VMEM((rows_img, feat_local), BF16),
            pltpu.VMEM((seqs, rows_img, block_cols), BF16),
            pltpu.VMEM((seqs, 8, rows_img), F32),
        ),
        in_specs=[anywhere] * 5 + [vmem] * 7 + [pl.BlockSpec(memory_space=pltpu.SMEM)],
        out_specs=(vmem,) * 4,
        scratch_shapes=[
            pltpu.VMEM((feat_local // LANES, LANES), F32),
            pltpu.VMEM((col_tiles, col_tile), F32),
            pltpu.VMEM((slots, pages), BF16),
            pltpu.VMEM((dense, LANES), F32),
            pltpu.VMEM((8, rows_img), F32),
            pltpu.VMEM((half_rows, all_channels), BF16),
            pltpu.VMEM((seqs, half_rows, channels), BF16),
            pltpu.VMEM((tokens, feat_local), BF16),
            pltpu.VMEM((blocks, feat_local, mps * LANES), BF16),
            pltpu.VMEM((channels, feat_local), BF16),
            pltpu.VMEM((seqs, half_rows, channels), BF16),
            pltpu.VMEM((2, TILE, chips * LANES), F32),
            pltpu.VMEM((steps, TILE, chips * LANES), BF16),
            pltpu.VMEM((steps, TILE, chips * LANES), BF16),
            pltpu.VMEM((chunks, tokens, LANES), F32),
            pltpu.VMEM((steps, chips - 1, TILE, LANES), BF16),
            pltpu.VMEM((steps, chips - 1, TILE, LANES), BF16),
            pltpu.VMEM((dense, LANES), F32),
            pltpu.VMEM((mps - 1, dense, LANES), F32),
            pltpu.VMEM((dense, LANES), F32),
            pltpu.VMEM((slots * page, LANES), F32),
            pltpu.VMEM((chunks, slots * page, LANES), BF16),
            pltpu.VMEM((chunks, slots * page, LANES), BF16),
            pltpu.VMEM((chunks, tokens, LANES), BF16),
            pltpu.VMEM((chunks, tokens, LANES), BF16),
            pltpu.VMEM((chunks, slots * page, LANES), BF16),
            pltpu.VMEM((seqs // 2, half_rows, feat_local), F32),
            pltpu.VMEM((seqs - 1, half_rows, feat_local), BF16),
            pltpu.VMEM((seqs - 1, half_rows, feat_local), BF16),
            pltpu.VMEM((seqs - 1, half_rows, col_tile), BF16),
            pltpu.VMEM((seqs - 1, half_rows, col_tile), BF16),
            pltpu.VMEM((rows_img, feat_local), BF16),
            pltpu.VMEM((half_rows, feat_local), BF16),
            pltpu.VMEM((blocks, half_rows, chips * LANES), F32),
            pltpu.VMEM((blocks, half_rows, chips * LANES), BF16),
            pltpu.VMEM((blocks, half_rows, chips * LANES), BF16),
            pltpu.VMEM((chips - 1, blocks, half_rows, LANES), BF16),
            pltpu.VMEM((chips - 1, blocks, half_rows, LANES), BF16),
            pltpu.VMEM((8, LANES), F32),
            pltpu.VMEM((mps - 1, 8, LANES), F32),
            pltpu.VMEM((half_rows, block_cols), BF16),
            pltpu.VMEM((rows_dec * heads, HEAD), F32),
            pltpu.VMEM(new_kv.shape, F32),
            pltpu.VMEM((rows_dec, LANES), F32),
            pltpu.VMEM((2, batch) + kv_cache.shape[1:], BF16),
            pltpu.VMEM((LANES, LANES), F32),
            pltpu.VMEM((LANES, LANES), F32),
            pltpu.VMEM((LANES, LANES), F32),
            pltpu.VMEM((LANES, LANES), F32),
            pltpu.VMEM((rows_dec * heads, HEAD), F32),
            pltpu.VMEM(queries.shape, BF16),
            dma((1,)),
            dma((2,)),
            dma((blocks, mps)),
            dma((tiles,)),
            dma,
            dma,
            dma((steps,)),
            dma((steps,)),
            dma((steps, chips - 1)),
            dma((steps, chips - 1)),
            dma((mps - 1,)),
            dma((mps - 1,)),
            dma((seqs - 1,)),
            dma((seqs - 1,)),
            dma((seqs - 1,)),
            dma((seqs - 1,)),
            dma((levels, col_tiles)),
            dma((levels, col_tiles)),
            dma((seqs - 1,)),
            dma((seqs - 1,)),
            dma,
            dma,
            dma,
            dma,
            dma((chips - 1,)),
            dma((chips - 1,)),
            dma((mps - 1,)),
            dma((mps - 1,)),
            dma((chunks, PIECES * (seqs - 1))),
            dma((chunks, PIECES * (seqs - 1))),
            dma((chunks,)),
            dma((chunks,)),
            dma((chunks,)),
            dma((chunks,)),
            dma((chunks,)),
            dma((chunks,)),
            dma((seqs - 1,)),
            dma((seqs - 1,)),
            dma,
            dma,
            dma((seqs - 1,)),
            dma((seqs - 1,)),
            dma((seqs - 1,)),
            dma((seqs - 1,)),
            dma((3,)),
        ],
        compiler_params=pltpu.CompilerParams(
            collective_id=0, has_side_effects=True, vmem_limit_bytes=57 * 1024 * 1024
        ),
        name="prefill_pages",
    )(
        embeds,
        image_feats,
        proj_w,
        kv_w,
        kv_cache,
        image_pos,
        bias,
        gain,
        page_owner,
        queries,
        new_kv,
        cache_lengths,
        prompt_lengths,
    )


def place_kernel(index, offset, text, img, dest, states, out, states_out, rows, sems):
    parts = index.shape[0]
    block = text.shape[0] // parts

    def store(b):
        span = pl.ds(b * block, block)
        return pltpu.make_async_copy(rows.at[span, :], out.at[span, :], sems.at[b])

    for b in range(parts):
        spots = dest[index[b]][:1].astype(jnp.int32) - offset[b]
        hit = lax.broadcasted_iota(jnp.int32, (block, dest.shape[2]), 0) == spots
        placed = jnp.dot(
            jnp.where(hit, 1.0, 0.0).astype(BF16), img[index[b]], preferred_element_type=F32
        )
        span = pl.ds(b * block, block)
        rows[span, :] = text[span, :] + placed.astype(BF16)
        store(b).start()
    state_store = pltpu.make_async_copy(states, states_out, sems.at[parts])
    state_store.start()
    for b in range(parts):
        store(b).wait()
    state_store.wait()


def place(index, offset, text, img, dest, states):
    parts = index.shape[0]
    smem = pl.BlockSpec(memory_space=pltpu.SMEM)
    vmem = pl.BlockSpec(memory_space=pltpu.VMEM)
    anywhere = pl.BlockSpec(memory_space=pl.ANY)
    near = [pltpu.with_memory_space_constraint(x, pltpu.VMEM) for x in (text, img, dest, states)]
    return pl.pallas_call(
        place_kernel,
        out_shape=(
            jax.ShapeDtypeStruct(text.shape, text.dtype),
            jax.ShapeDtypeStruct(states.shape, states.dtype),
        ),
        in_specs=[smem, smem, vmem, vmem, vmem, vmem],
        out_specs=(anywhere, anywhere),
        scratch_shapes=[
            pltpu.VMEM(text.shape, text.dtype),
            pltpu.SemaphoreType.DMA((parts + 1,)),
        ],
        compiler_params=pltpu.CompilerParams(vmem_limit_bytes=16 * 1024 * 1024),
        name="place_images",
    )(index, offset, *near)


def per_device(
    mesh_sizes,
    embeds,
    image_feats,
    image_pos,
    proj_w,
    proj_b,
    norm_gain,
    kv_w,
    prompt_lengths,
    page_owner,
    queries,
    kv_cache,
    new_kv,
    cache_lengths,
):
    groups, seqs, mps = mesh_sizes
    group_index = lax.axis_index("group")
    prefill_side = group_index == 0
    seq_index = lax.axis_index("seq")
    token_rows, width_local = embeds.shape
    prompt_len = token_rows * seqs // prompt_lengths.shape[0]
    page = token_rows // page_owner.shape[0]
    capacity = 2 * page_owner.shape[0] // seqs
    text, row_states, img, dest_all = prefill(
        mesh_sizes,
        prompt_len,
        embeds,
        image_feats,
        proj_w,
        kv_w,
        kv_cache,
        image_pos[None, :],
        proj_b.reshape(-1, LANES),
        norm_gain.reshape(-1, LANES),
        page_owner.reshape(1, -1),
        queries,
        new_kv,
        cache_lengths[None, :],
        prompt_lengths,
    )
    parts = max(1, 8 // seqs)
    order = jnp.arange(seqs * parts, dtype=jnp.int32)
    source, part = order // parts, order % parts
    index = jnp.where(prefill_side, seq_index, source)
    offset = jnp.where(prefill_side, source, seq_index) * (capacity * page)
    offset = offset + part * (capacity * page // parts)
    page_slots, row_states = place(index, offset, text, img, dest_all, row_states)
    page_slots = page_slots.reshape(-1, page, text.shape[1])
    return (page_slots, row_states)


def solution(mesh):
    mesh_sizes = (mesh.shape["group"], mesh.shape["seq"], mesh.shape["mp"])
    in_specs = (
        P("seq", "mp"),
        P("seq", None),
        P("seq"),
        P("seq", "mp"),
        P("mp"),
        P("mp"),
        P("mp", None),
        P(),
        P("seq", None),
        P("seq", "mp"),
        P("seq", None, "mp"),
        P("seq", "mp"),
        P("seq"),
    )
    out_specs = (P(("group", "seq"), None, "mp"), P(("group", "seq"), "mp"))
    return jax.shard_map(
        functools.partial(per_device, mesh_sizes),
        mesh=mesh,
        in_specs=in_specs,
        out_specs=out_specs,
        check_vma=False,
    )
```
